32 devices in a mesh: dp: 8 (over y, x, core), head: 4 (over z).
Axes of the slice: x: 2, y: 2, z: 4, core: 2. Of those that a mesh axis runs over, the one named last changes fastest.
Arguments:
- activations: bfloat16 [4, 6144, 1024], P(None, ('dp', 'head')), may hold values from -6 to 6
- conditioning: bfloat16 [4, 1536, 1024], P(None, ('dp', 'head')), may hold values from -3 to 3
- cotangent: bfloat16 [4, 6144, 1024], P(None, ('dp', 'head')), may hold values from -6 to 6
- block_targets: int32 [4, 48], replicated, may hold values from -1 to 46, as said below
- up_gain: float32 [4, 1024], replicated, may hold values from -6 to 6
- norm1_gain: float32 [1024], replicated, may hold values from 0.1 to 1.9
- norm1_shift: float32 [1024], replicated, may hold values from -1.75 to 1.75
- w_qkv: bfloat16 [3, 1024, 1024], P(None, None, 'head'), may hold values from -0.1875 to 0.1875
- b_qv: float32 [2, 1024], P(None, 'head'), may hold values from -3 to 3
- w_out: bfloat16 [1024, 1024], P('head'), may hold values from -1.5 to 1.5
- b_out: float32 [1024], replicated, may hold values from -3 to 3
- norm2_gain: float32 [1024], replicated, may hold values from 0.1 to 1.9
- norm2_shift: float32 [1024], replicated, may hold values from -1.75 to 1.75
- w_fc1: bfloat16 [1024, 4096], P(None, 'head'), may hold values from -0.1875 to 0.1875
- b_fc1: float32 [4096], P('head'), may hold values from -3 to 3
- w_fc2: bfloat16 [4096, 1024], P('head'), may hold values from -0.09375 to 0.09375
- b_fc2: float32 [1024], replicated, may hold values from -3 to 3
Outputs:
- layer_out: bfloat16 [4, 6144, 1024], P(None, ('dp', 'head'))
- grad_input: float32 [4, 6144, 1024], P(None, ('dp', 'head'))
- grad_conditioning: float32 [4, 1536, 1024], P(None, ('dp', 'head'))
- grad_up_gain: float32 [4, 1024], replicated
- grad_norm1_gain: float32 [1024], replicated
- grad_norm1_shift: float32 [1024], replicated
- grad_w_qkv: float32 [3, 1024, 1024], P(None, 'dp', 'head')
- grad_b_qv: float32 [2, 1024], replicated
- grad_w_out: float32 [1024, 1024], P('head', 'dp')
- grad_b_out: float32 [1024], replicated
- grad_norm2_gain: float32 [1024], replicated
- grad_norm2_shift: float32 [1024], replicated
- grad_w_fc1: float32 [1024, 4096], P('dp', 'head')
- grad_b_fc1: float32 [4096], replicated
- grad_w_fc2: float32 [4096, 1024], P('head', 'dp')
- grad_b_fc2: float32 [1024], replicated
The draws below stay inside these ranges and needn't reach their ends.
Inputs may be any that keep to these rules, and one draw needn't show every extreme that they name: `block_targets`: entry b of a micro-batch is -1 or a block below b in the same window; windows are runs of whole blocks and the first block of each has -1. In micro-batches of even index one window covers all 48 blocks and its last block names block 0; in the others no window is longer than 2048 tokens and the last block names the block before it.
All inputs are finite; a program needn't handle non-finite values.
Results may differ from the reference program's by a relative error of at most 0.015.
Values may be sent and summed in bfloat16 or wider, within the bound.
No kernel may reach another device: no remote copies, remote signals or barrier semaphores. Data moves between devices by JAX's collectives and lax.ppermute only.
A program may use at most 192 MiB of HBM per device.

```python
import math
import jax
import jax.numpy as jnp
from jax import lax

D = 1024
HEADS = 16
HEAD_DIM = 64
FF = 4096
BLOCK = 128
SHORT = 2048
UP = 4
MICRO = 4
MBTOK = 6144


def draw_block_targets(key, part):
    blocks = MBTOK // BLOCK
    spans = SHORT // BLOCK
    positions = jnp.arange(blocks, dtype=jnp.int32)
    flag_key, pick_key = jax.random.split(jax.random.fold_in(key, 17))
    coins = jax.random.randint(flag_key, (MICRO, blocks), 0, 4)
    begins = (coins == 0) | (positions % spans == 0)[None, :]
    parity = (jnp.arange(MICRO) % 2 == 0)[:, None]
    last_pos = (positions == blocks - 1)[None, :]
    odd_last = jnp.logical_not(parity) & last_pos
    begins = jnp.where(odd_last, False, begins)
    begins = jnp.where(parity, (positions == 0)[None, :], begins)
    marked = jnp.where(begins, positions[None, :], 0)
    window_start = lax.cummax(marked, axis=1)
    spread = positions[None, :] - window_start
    raw_bits = jax.random.randint(pick_key, (MICRO, blocks), 0, 1 << 20)
    chosen = window_start + raw_bits % jnp.maximum(spread, 1)
    chosen = jnp.where(spread > 0, chosen, -1)
    chosen = jnp.where(odd_last, blocks - 2, chosen)
    final_block = parity & last_pos
    chosen = jnp.where(final_block, 0, chosen)
    return chosen.astype(jnp.int32)


def level_of(stream_key, extent, pieces, least, high):
    level = 1.0
    for position, blocks in pieces:
        heights = jax.random.uniform(jax.random.fold_in(jax.random.fold_in(stream_key, 6), position), (blocks,), jnp.float32, least / len(pieces), high / len(pieces))
        level = level * jnp.repeat(jnp.exp(heights), extent[position] // blocks).reshape((-1,) + (1,) * (len(extent) - 1 - position))
    return level


def gaussian(own_key, extent, scale, bound, cuts=(), held_as=jnp.bfloat16):
    loudness = level_of(own_key, extent, cuts, -0.22, 0.18) if cuts else 1.0
    drawn = jax.random.normal(own_key, extent, jnp.float32) * scale * loudness
    return jnp.minimum(jnp.maximum(drawn, -bound), bound).astype(held_as)


def setup_inputs(seed: int = 0) -> dict:
    key_of = jax.random.split(jax.random.key(seed), 18)
    return {
        "activations": gaussian(key_of[0], (MICRO, MBTOK, D), 1.0, 6.0, ((1, 32),)),
        "conditioning": gaussian(key_of[1], (MICRO, MBTOK // UP, D), 0.5, 3.0, ((1, 32),)),
        "cotangent": gaussian(key_of[2], (MICRO, MBTOK, D), 1.0, 6.0, ((1, 32),)),
        "block_targets": draw_block_targets(jax.random.fold_in(key_of[17], 71), 0),
        "up_gain": gaussian(key_of[4], (UP, D), 1.0, 6.0, (), jnp.float32),
        "norm1_gain": jnp.clip(1.0 + 0.18 * jax.random.normal(key_of[5], (D,), jnp.float32), 0.1, 1.9),
        "norm1_shift": gaussian(key_of[6], (D,), 0.3, 1.75, (), jnp.float32),
        "w_qkv": gaussian(key_of[7], (3, D, D), D ** -0.5, 0.1875, ((2, 4),)),
        "b_qv": gaussian(key_of[8], (2, D), 0.5, 3.0, ((1, 4),), jnp.float32),
        "w_out": gaussian(key_of[9], (D, D), (D // 64) ** -0.5, 1.5, ((0, 4),)),
        "b_out": gaussian(key_of[10], (D,), 0.5, 3.0, (), jnp.float32),
        "norm2_gain": jnp.clip(1.0 + 0.18 * jax.random.normal(key_of[11], (D,), jnp.float32), 0.1, 1.9),
        "norm2_shift": gaussian(key_of[12], (D,), 0.3, 1.75, (), jnp.float32),
        "w_fc1": gaussian(key_of[13], (D, FF), D ** -0.5, 0.1875, ((1, 4),)),
        "b_fc1": gaussian(key_of[14], (FF,), 0.5, 3.0, ((0, 4),), jnp.float32),
        "w_fc2": gaussian(key_of[15], (FF, D), FF ** -0.5, 0.09375, ((0, 4),)),
        "b_fc2": gaussian(key_of[16], (D,), 0.5, 3.0, (), jnp.float32),
    }


epsilon = 1e-05
highest = lax.Precision.HIGHEST

@jax.custom_vjp
def low(v):
    return lax.optimization_barrier(v.astype(jnp.bfloat16)).astype(jnp.float32)

@jax.custom_vjp
def low_back(v):
    return v

def low_keep(v):
    return (low(v), None)

def low_pass(kept, grad):
    return (grad,)

def back_keep(v):
    return (v, None)

def back_low(kept, grad):
    return (low(grad),)
low.defvjp(low_keep, low_pass)
low_back.defvjp(back_keep, back_low)

def layer_norm(values, gain, shift):
    centered = values - lax.optimization_barrier(jnp.mean(values, axis=-1, keepdims=True))
    variance = lax.optimization_barrier(jnp.mean(centered * centered, axis=-1, keepdims=True))
    return centered * lax.rsqrt(variance + epsilon) * gain + shift

def block_attention(operands):
    queries, key_cat, value_cat, has_far = operands
    score_scale = 1.0 / math.sqrt(HEAD_DIM)
    scores = low_back(jnp.einsum('bqhd,bkhd->bhqk', queries, key_cat, precision=highest) * score_scale)
    causal = jnp.arange(BLOCK)[:, None] >= jnp.arange(BLOCK)[None, :]
    own_mask = jnp.broadcast_to(causal, (queries.shape[0], 1, BLOCK, BLOCK))
    far_mask = jnp.broadcast_to(has_far[:, None, None, None], own_mask.shape)
    allowed = jnp.concatenate([own_mask, far_mask], axis=-1)
    masked = jnp.where(allowed, scores, -1e+30)
    weights = low(jax.nn.softmax(masked, axis=-1))
    return jnp.einsum('bhqk,bkhd->bqhd', weights, value_cat, precision=highest)

def forward(tokens, coarse, params, targets):
    up_gain, norm1_gain, norm1_shift, w_qkv, b_qv, w_out, b_out, norm2_gain, norm2_shift, w_fc1, b_fc1, w_fc2, b_fc2 = params
    total_rows = tokens.shape[0]
    model_width = tokens.shape[1]
    joined = (tokens.reshape(-1, UP, model_width) + coarse[:, None, :] * up_gain[None]).reshape(total_rows, model_width)
    normed = low(layer_norm(joined, norm1_gain, norm1_shift))
    project = jnp.einsum('gd,tdc->tgc', normed, w_qkv, precision=highest)
    queries = low(low_back(project[0] + b_qv[0]))
    keys_all = low(low_back(project[1]))
    values_all = low(low_back(project[2] + b_qv[1]))
    blocks = total_rows // BLOCK
    shape_four = (blocks, BLOCK, HEADS, HEAD_DIM)
    q_blocks = queries.reshape(shape_four)
    k_blocks = keys_all.reshape(shape_four)
    v_blocks = values_all.reshape(shape_four)
    has_far = targets >= 0
    picked = jnp.clip(targets, 0, blocks - 1).astype(jnp.int32)
    key_cat = jnp.concatenate([k_blocks, k_blocks[picked]], axis=1)
    value_cat = jnp.concatenate([v_blocks, v_blocks[picked]], axis=1)
    groups = blocks // 4

    def grouped(array_in):
        return array_in.reshape((groups, 4) + array_in.shape[1:])
    attended = lax.map(jax.checkpoint(block_attention), (grouped(q_blocks), grouped(key_cat), grouped(value_cat), grouped(has_far)))
    attended = low(low_back(attended.reshape(total_rows, model_width)))
    residual = joined + low_back(jnp.dot(attended, w_out, precision=highest, preferred_element_type=jnp.float32) + b_out)
    normed_two = low(layer_norm(residual, norm2_gain, norm2_shift))
    hidden = low_back(jnp.dot(normed_two, w_fc1, precision=highest, preferred_element_type=jnp.float32) + b_fc1)
    activated = low(jax.nn.gelu(hidden, approximate=True))
    return residual + low_back(jnp.dot(activated, w_fc2, precision=highest, preferred_element_type=jnp.float32) + b_fc2)

def reference(activations, conditioning, cotangent, block_targets, up_gain, norm1_gain, norm1_shift, w_qkv, b_qv, w_out, b_out, norm2_gain, norm2_shift, w_fc1, b_fc1, w_fc2, b_fc2):
    params = tuple((argument.astype(jnp.float32) for argument in (up_gain, norm1_gain, norm1_shift, w_qkv, b_qv, w_out, b_out, norm2_gain, norm2_shift, w_fc1, b_fc1, w_fc2, b_fc2)))

    def per_batch(totals, inputs_now):
        tokens, coarse, incoming, targets = inputs_now

        def closed(tok_f, coarse_f, *weights_f):
            return forward(tok_f, coarse_f, weights_f, targets)
        result, pullback = jax.vjp(closed, tokens.astype(jnp.float32), coarse.astype(jnp.float32), *params)
        gradients = pullback(incoming.astype(jnp.float32))
        totals = tuple((acc_item + grad_item for acc_item, grad_item in zip(totals, gradients[2:])))
        return (totals, (result.astype(jnp.bfloat16), gradients[0], gradients[1]))
    start_totals = tuple((jnp.zeros_like(argument) for argument in params))
    totals, stacked = lax.scan(per_batch, start_totals, (activations, conditioning, cotangent, block_targets))
    return (stacked[0], stacked[1], stacked[2], totals[0], totals[1], totals[2], totals[3], totals[4], totals[5], totals[6], totals[7], totals[8], totals[9], totals[10], totals[11], totals[12])
```

```python
import functools
import math

import jax
import jax.numpy as jnp
from jax import lax
from jax.experimental import pallas as pl
from jax.experimental.pallas import tpu as pltpu
from jax.sharding import PartitionSpec as P

HEAD_DIM = 64
BLOCK = 128
UP = 4
PAIR = 2 * HEAD_DIM
NEGATIVE = -1e30
epsilon = 1e-05
f32 = jnp.float32
bf16 = jnp.bfloat16
ROOT_2_PI = math.sqrt(2.0 / math.pi)
ANY = pl.BlockSpec(memory_space=pl.ANY)


def xor_swap(value, axis, mask):
    size = lax.axis_size(axis)
    return lax.ppermute(value, axis, [(i, i ^ mask) for i in range(size)])


def norm_forward(values, gain, shift):
    centered = values - jnp.mean(values, axis=-1, keepdims=True)
    inverse = lax.rsqrt(jnp.mean(centered * centered, axis=-1, keepdims=True) + epsilon)
    standard = centered * inverse
    return (standard * gain + shift, standard, inverse)


def norm_backward(upstream, standard, inverse, gain):
    scaled = upstream * gain
    inner = (
        scaled
        - jnp.mean(scaled, axis=-1, keepdims=True)
        - standard * jnp.mean(scaled * standard, axis=-1, keepdims=True)
    )
    return (inner * inverse, jnp.sum(upstream * standard, axis=0), jnp.sum(upstream, axis=0))


def mm(left, right):
    return jnp.dot(left, right, preferred_element_type=f32)


def mm_nt(left, right):
    return lax.dot_general(left, right, (((1,), (1,)), ((), ())), preferred_element_type=f32)


def mm_tn(left, right):
    return lax.dot_general(left, right, (((0,), (0,)), ((), ())), preferred_element_type=f32)


def pair_probs(q_pair, k_cat, allowed):
    low_half = lax.broadcasted_iota(jnp.int32, (BLOCK, PAIR), 1) < HEAD_DIM
    zero = jnp.zeros_like(q_pair)
    q_stack = jnp.concatenate(
        [jnp.where(low_half, q_pair, zero), jnp.where(low_half, zero, q_pair)], axis=0
    )
    scores = mm_nt(k_cat, q_stack) * (1.0 / math.sqrt(HEAD_DIM))
    scores = jnp.where(allowed, scores, NEGATIVE)
    top = jnp.max(scores, axis=0, keepdims=True)
    raised = jnp.exp(scores - top)
    probs = raised * (1.0 / jnp.sum(raised, axis=0, keepdims=True))
    return q_stack, probs, low_half


def allowed_mask(far_flag):
    key_at = lax.broadcasted_iota(jnp.int32, (2 * BLOCK, 2 * BLOCK), 0)
    query_at = lax.broadcasted_iota(jnp.int32, (2 * BLOCK, 2 * BLOCK), 1)
    query_at = jnp.where(query_at >= BLOCK, query_at - BLOCK, query_at)
    first = jnp.where(far_flag > 0, BLOCK, 2 * BLOCK)
    return (key_at <= query_at) | (key_at >= first)


def attention_forward_kernel(pairs, has_far, q_ref, own_ref, far_ref, out_ref):
    allowed = allowed_mask(has_far[pl.program_id(0)])
    width = pairs * PAIR
    for p in range(pairs):
        cols = slice(p * PAIR, (p + 1) * PAIR)
        vcols = slice(width + p * PAIR, width + (p + 1) * PAIR)
        k_cat = jnp.concatenate([own_ref[:, cols], far_ref[:, cols]], axis=0)
        v_cat = jnp.concatenate([own_ref[:, vcols], far_ref[:, vcols]], axis=0)
        _, probs, low_half = pair_probs(q_ref[:, cols], k_cat, allowed)
        mixed = mm_tn(probs.astype(bf16), v_cat)
        out_ref[:, cols] = jnp.where(low_half, mixed[:BLOCK], mixed[BLOCK:]).astype(bf16)


def attention_backward_kernel(
    pairs, has_far, q_ref, own_ref, far_ref, grad_ref, dq_ref, down_ref, dfar_ref
):
    allowed = allowed_mask(has_far[pl.program_id(0)])
    width = pairs * PAIR
    scale = 1.0 / math.sqrt(HEAD_DIM)
    for p in range(pairs):
        cols = slice(p * PAIR, (p + 1) * PAIR)
        vcols = slice(width + p * PAIR, width + (p + 1) * PAIR)
        k_cat = jnp.concatenate([own_ref[:, cols], far_ref[:, cols]], axis=0)
        v_cat = jnp.concatenate([own_ref[:, vcols], far_ref[:, vcols]], axis=0)
        q_stack, probs, low_half = pair_probs(q_ref[:, cols], k_cat, allowed)
        grad = grad_ref[:, cols]
        zero = jnp.zeros_like(grad)
        grad_stack = jnp.concatenate(
            [jnp.where(low_half, grad, zero), jnp.where(low_half, zero, grad)], axis=0
        )
        grad_probs = mm_nt(v_cat, grad_stack)
        total = jnp.sum(probs * grad_probs, axis=0, keepdims=True)
        grad_scores = (probs * (grad_probs - total)).astype(bf16)
        dq = mm_tn(grad_scores, k_cat) * scale
        dq_ref[:, cols] = jnp.where(low_half, dq[:BLOCK], dq[BLOCK:]).astype(bf16)
        dk = (mm(grad_scores, q_stack) * scale).astype(bf16)
        dv = mm(probs.astype(bf16), grad_stack).astype(bf16)
        down_ref[:, cols] = dk[:BLOCK]
        dfar_ref[:, cols] = dk[BLOCK:]
        down_ref[:, vcols] = dv[:BLOCK]
        dfar_ref[:, vcols] = dv[BLOCK:]


def attention_call(kernel, has_far, blocked, outs):
    blocks = has_far.shape[0]
    row_block = lambda width: pl.BlockSpec((BLOCK, width), lambda b, flags: (b, 0))
    width = blocked[0].shape[1]
    return pl.pallas_call(
        functools.partial(kernel, width // PAIR),
        grid_spec=pltpu.PrefetchScalarGridSpec(
            num_scalar_prefetch=1,
            grid=(blocks,),
            in_specs=[row_block(a.shape[1]) for a in blocked],
            out_specs=[row_block(w) for w in outs],
        ),
        out_shape=[jax.ShapeDtypeStruct((blocks * BLOCK, w), bf16) for w in outs],
        compiler_params=pltpu.CompilerParams(vmem_limit_bytes=48 << 20),
        cost_estimate=pl.CostEstimate(
            flops=blocks * width * BLOCK * BLOCK * 16,
            bytes_accessed=blocks * BLOCK * width * 16,
            transcendentals=blocks * width * BLOCK * 4,
        ),
    )(has_far, *blocked)


def far_pick_kernel(where_a, where_b, a_ref, b_ref, out_ref):
    half = a_ref.shape[2]
    out_ref[0, :, :half] = a_ref[0]
    out_ref[0, :, half:] = b_ref[0]


def far_pick(table_a, table_b, where_a, where_b):
    count, half = where_a.shape[0], table_a.shape[2]
    spec = lambda which: pl.BlockSpec((1, BLOCK, half), lambda j, wa, wb: ((wa, wb)[which][j], 0, 0))
    return pl.pallas_call(
        far_pick_kernel,
        grid_spec=pltpu.PrefetchScalarGridSpec(
            num_scalar_prefetch=2,
            grid=(count,),
            in_specs=[spec(0), spec(1)],
            out_specs=pl.BlockSpec((1, BLOCK, 2 * half), lambda j, wa, wb: (j, 0, 0)),
        ),
        out_shape=jax.ShapeDtypeStruct((count, BLOCK, 2 * half), bf16),
        cost_estimate=pl.CostEstimate(
            flops=0, bytes_accessed=count * BLOCK * half * 8, transcendentals=0
        ),
    )(where_a, where_b, table_a, table_b)


def far_route_kernel(count, where_a, where_b, mine_ref, other_ref, a_ref, b_ref, acc_ref):
    step = pl.program_id(0)
    half = a_ref.shape[2]
    acc_ref[...] = jnp.zeros_like(acc_ref)
    for source, base in ((mine_ref, 0), (other_ref, count)):
        for j in range(count):

            @pl.when(where_a[base + j] == step)
            def _():
                acc_ref[:, :half] += source[j, :, :half].astype(f32)

            @pl.when(where_b[base + j] == step)
            def _():
                acc_ref[:, half:] += source[j, :, half:].astype(f32)

    a_ref[0] = acc_ref[:, :half].astype(bf16)
    b_ref[0] = acc_ref[:, half:].astype(bf16)


def far_route(mine, other, where_a, where_b, table):
    count, _, width = mine.shape
    whole = pl.BlockSpec(mine.shape, lambda k, wa, wb: (0, 0, 0))
    out = pl.BlockSpec((1, BLOCK, width // 2), lambda k, wa, wb: (k, 0, 0))
    shape = jax.ShapeDtypeStruct((table, BLOCK, width // 2), bf16)
    return pl.pallas_call(
        functools.partial(far_route_kernel, count),
        grid_spec=pltpu.PrefetchScalarGridSpec(
            num_scalar_prefetch=2,
            grid=(table,),
            in_specs=[whole, whole],
            out_specs=[out, out],
            scratch_shapes=[pltpu.VMEM((BLOCK, width), f32)],
        ),
        out_shape=[shape, shape],
        compiler_params=pltpu.CompilerParams(vmem_limit_bytes=32 << 20),
        cost_estimate=pl.CostEstimate(
            flops=0, bytes_accessed=table * BLOCK * width * 2, transcendentals=0
        ),
    )(where_a, where_b, mine, other)


def gather_strips(strip, masks):
    head_size = lax.axis_size("head")
    slots = jnp.stack(
        [
            lax.ppermute(strip, "head", [((i + s) % head_size, i) for i in range(head_size)])
            for s in range(1, head_size)
        ]
    )
    half = strip.shape[0] // 2
    out = []
    for color, order in ((0, masks), (1, masks[::-1])):
        held = slots[None, :, color * half : (color + 1) * half]
        for mask in order:
            held = jnp.concatenate([held, xor_swap(held, "dp", mask)], axis=0)
        out.append(held)
    return out + [xor_swap(held, "dp", 1) for held in out]


def relative_masks(masks):
    return [sum(m for bit, m in enumerate(masks) if k >> bit & 1) for k in range(1 << len(masks))]


def assemble_kernel(copies, n_in, dp_index, *refs):
    ins, outs, sem = refs[:n_in], refs[n_in:-1], refs[-1]
    me = dp_index[0]
    started = []
    for which, index, target, row_xor, half, c0, width, t0 in copies:
        src = ins[which]
        for at in index:
            src = src.at[at]
        if c0 is not None:
            src = src.at[:, pl.ds(c0, width)]
        dst = outs[target]
        if row_xor is not None:
            rows = src.shape[0]
            dst = dst.at[pl.ds(pl.multiple_of((me ^ row_xor) * 2 * rows + half * rows, rows), rows)]
        dst = dst.at[:, pl.ds(t0, width)]
        copy = pltpu.make_async_copy(src, dst, sem.at[len(started)])
        copy.start()
        started.append(copy)
    for copy in started:
        copy.wait()


def assemble(dp_index, ins, copies, shapes):
    return pl.pallas_call(
        functools.partial(assemble_kernel, copies, len(ins)),
        grid_spec=pltpu.PrefetchScalarGridSpec(
            num_scalar_prefetch=1,
            grid=(1,),
            in_specs=[ANY] * len(ins),
            out_specs=[ANY] * len(shapes),
            scratch_shapes=[pltpu.SemaphoreType.DMA((len(copies),))],
        ),
        out_shape=[jax.ShapeDtypeStruct(s, bf16) for s in shapes],
        cost_estimate=pl.CostEstimate(
            flops=0,
            bytes_accessed=sum(4 * math.prod(s) for s in shapes),
            transcendentals=0,
        ),
    )(dp_index, *ins)


def strip_copies(masks, slots, columns):
    out = []
    for which in range(4):
        order = masks if which % 2 == 0 else masks[::-1]
        for k, mask in enumerate(relative_masks(order)):
            for s in range(slots):
                for c0, width, target, place in columns:
                    out.append(
                        (which, (k, s), target, mask | (which // 2), which % 2, c0, width, place(s + 1))
                    )
    return out


def reduce_over_dp(left, right, masks, color):
    keep, send = left
    got = xor_swap(mm_tn(send, right).astype(bf16), "dp", 1)
    part = (mm_tn(keep, right) + got.astype(f32)).astype(bf16)
    bits = len(masks)
    width = part.shape[1]
    part = part.reshape((2,) * bits + (-1, width))
    order = masks if color == 0 else masks[::-1]
    axes = {mask: bits - 1 - i for i, mask in enumerate(masks)}
    live = list(masks)
    for step, mask in enumerate(order):
        axis = len(live) - 1 - live.index(mask)
        live.remove(mask)
        mine = lax.index_in_dim(part, 0, axis, keepdims=False)
        away = lax.index_in_dim(part, 1, axis, keepdims=False)
        got = xor_swap(away, "dp", mask)
        part = (mine.astype(f32) + got.astype(f32)).astype(bf16)
    return part


def reduce_over_head(parts):
    head_size = lax.axis_size("head")
    total = parts[0].astype(f32)
    for s in range(1, head_size):
        got = lax.ppermute(parts[s], "head", [(i, (i + s) % head_size) for i in range(head_size)])
        total = total + got.astype(f32)
    return total


def local(
    activations,
    conditioning,
    cotangent,
    block_targets,
    up_gain,
    norm1_gain,
    norm1_shift,
    w_qkv,
    b_qv,
    w_out,
    b_out,
    norm2_gain,
    norm2_shift,
    w_fc1,
    b_fc1,
    w_fc2,
    b_fc2,
):
    micro, rows, model = activations.shape
    head_cols = w_qkv.shape[2]
    hidden_cols = w_fc1.shape[1]
    dp_size, head_size = lax.axis_size("dp"), lax.axis_size("head")
    me, here = lax.axis_index("dp"), lax.axis_index("head")
    group = head_size // micro
    tokens = rows * micro
    blocks = tokens // BLOCK
    slab = model // dp_size
    masks = [1 << i for i in range(1, dp_size.bit_length() - 1)]
    remote = head_size - 1
    heads_all, hidden_all = head_cols * head_size, hidden_cols * head_size

    src_rank = here % micro
    my_micro, my_sub = here // group, here % group
    shifts = [
        [(hs * micro + hr, ((hr + s) % micro) * group + hs) for hs in range(group) for hr in range(micro)]
        for s in range(micro)
    ]

    def send(value, pairs):
        return value if all(a == b for a, b in pairs) else lax.ppermute(value, "head", pairs)

    def choose(options, index):
        out = options[-1]
        for k in range(len(options) - 1):
            out = jnp.where(index == k, options[k], out)
        return out

    def to_micro(value):
        got = [
            send(lax.dynamic_index_in_dim(value, (src_rank + s) % micro, 0, False), shifts[s])
            for s in range(micro)
        ]
        return [choose(got, (my_micro - p) % micro) for p in range(micro)]

    def from_micro(value):
        pieces = value.reshape(micro, rows, -1)
        got = [
            send(
                lax.dynamic_index_in_dim(pieces, (my_micro - s) % micro, 0, False),
                [(b, a) for a, b in shifts[s]],
            )
            for s in range(micro)
        ]
        return jnp.stack([choose(got, (m - src_rank) % micro) for m in range(micro)])

    packed = to_micro(jnp.concatenate([activations, conditioning], axis=1))
    acts = jnp.concatenate([p[:rows] for p in packed], axis=0)
    coarse = jnp.concatenate([p[rows:] for p in packed], axis=0).astype(f32)
    incoming = jnp.concatenate(to_micro(cotangent), axis=0)

    def my_slab(value, axis):
        return lax.dynamic_slice_in_dim(value, me * slab, slab, axis)

    strip_a = jnp.concatenate(
        [my_slab(w_qkv[0], 0), my_slab(w_qkv[1], 0), my_slab(w_qkv[2], 0), my_slab(w_out, 1).T],
        axis=1,
    )
    strip_f = jnp.concatenate([my_slab(w_fc1, 0), my_slab(w_fc2, 1).T], axis=1)
    dp_index = me.reshape(1).astype(jnp.int32)
    hc, fc = head_cols, hidden_cols
    got_a = gather_strips(strip_a, masks)
    own_a = [(4, (t,), 0 if t == 0 else 1, None, 0, 0, hc, (t == 2) * heads_all) for t in range(3)]
    own_a += [(5, (), 2, None, 0, 0, hc, 0)]
    w_query, w_kv, w_out_t = assemble(
        dp_index,
        got_a + [w_qkv, w_out.T],
        strip_copies(
            masks,
            remote,
            [
                (0, hc, 0, lambda s: s * hc),
                (hc, hc, 1, lambda s: s * hc),
                (2 * hc, hc, 1, lambda s: heads_all + s * hc),
                (3 * hc, hc, 2, lambda s: s * hc),
            ],
        )
        + own_a,
        [(model, heads_all), (model, 2 * heads_all), (model, heads_all)],
    )
    got_f = gather_strips(strip_f, masks)
    w_one, w_two_t = assemble(
        dp_index,
        got_f + [w_fc1, w_fc2.T],
        strip_copies(masks, remote, [(0, fc, 0, lambda s: s * fc), (fc, fc, 1, lambda s: s * fc)])
        + [(4, (), 0, None, 0, 0, fc, 0), (5, (), 1, None, 0, 0, fc, 0)],
        [(model, hidden_all), (model, hidden_all)],
    )
    small = jnp.concatenate([b_qv.reshape(-1), b_fc1])
    biases = [small] + [
        lax.ppermute(small, "head", [((i + s) % head_size, i) for i in range(head_size)])
        for s in range(1, head_size)
    ]
    bias_q = jnp.concatenate([b[:hc] for b in biases])
    bias_v = jnp.concatenate([b[hc : 2 * hc] for b in biases])
    bias_one = jnp.concatenate([b[2 * hc :] for b in biases])
    bias_kv = jnp.concatenate([jnp.zeros_like(bias_v), bias_v])

    joined = (
        acts.astype(f32).reshape(-1, UP, model) + coarse[:, None, :] * up_gain[None]
    ).reshape(tokens, model)
    normed_f, standard_one, inverse_one = norm_forward(joined, norm1_gain, norm1_shift)
    normed = normed_f.astype(bf16)

    stages_sub = [("head", 1 << i) for i in range(group.bit_length() - 1)]
    stage_lists = [
        stages_sub + [("dp", m) for m in masks],
        stages_sub + [("dp", m) for m in masks[::-1]],
    ]
    shaped = normed.reshape(blocks, BLOCK, model)
    half = model // 2
    tables = []
    for color in range(2):
        held = shaped[:, :, color * half : (color + 1) * half]
        for axis, mask in stage_lists[color]:
            held = jnp.concatenate([held, xor_swap(held, axis, mask)], axis=0)
        tables.append(held)
    table_blocks = tables[0].shape[0]
    table_row = lax.dynamic_index_in_dim(block_targets, my_micro, 0, False)

    def targets_of(device):
        return lax.dynamic_slice_in_dim(table_row, (device * group + my_sub) * blocks, blocks)

    targets = targets_of(me)
    targets_both = jnp.concatenate([targets, targets_of(me ^ 1)])
    owner = jnp.maximum(targets_both, 0) // blocks
    away = (owner // group) ^ me
    away_sub = (owner % group) ^ my_sub

    def table_index(stages):
        index = jnp.zeros_like(owner)
        for bit, (axis, mask) in enumerate(stages):
            far_bits = away if axis == "dp" else away_sub
            index = index + (((far_bits & mask) != 0).astype(jnp.int32) << bit)
        return index * blocks + jnp.maximum(targets_both, 0) % blocks

    index_a, index_b = table_index(stage_lists[0]), table_index(stage_lists[1])
    on_my_core = (away & 1) == 0
    picked = far_pick(tables[0], tables[1], index_a, index_b)
    passed = xor_swap(picked[blocks:], "dp", 1)
    far = jnp.where(on_my_core[:blocks, None, None], picked[:blocks], passed).reshape(tokens, model)
    has_far = (targets >= 0).astype(jnp.int32)

    queries = (mm(normed, w_query) + bias_q).astype(bf16)
    kv_own = (mm(normed, w_kv) + bias_kv).astype(bf16)
    kv_far = (mm(far, w_kv) + bias_kv).astype(bf16)
    (attended,) = attention_call(
        attention_forward_kernel, has_far, [queries, kv_own, kv_far], [heads_all]
    )
    residual = joined + (mm_nt(attended, w_out_t) + b_out)

    normed2_f, standard_two, inverse_two = norm_forward(residual, norm2_gain, norm2_shift)
    normed_two = normed2_f.astype(bf16)
    hidden = mm(normed_two, w_one) + bias_one
    inner = jnp.tanh(ROOT_2_PI * (hidden + 0.044715 * hidden * hidden * hidden))
    activated = (0.5 * hidden * (1.0 + inner)).astype(bf16)
    slope = (
        0.5 * (1.0 + inner)
        + 0.5 * hidden * (1.0 - inner * inner) * (ROOT_2_PI * (1.0 + 3 * 0.044715 * hidden * hidden))
    ).astype(bf16)
    layer_out = from_micro((residual + (mm_nt(activated, w_two_t) + b_fc2)).astype(bf16))

    position_masks = relative_masks(masks)
    order = jnp.array(position_masks + [m | 1 for m in position_masks], jnp.int32)
    column = jnp.arange(model, dtype=jnp.int32)
    source = (me ^ jnp.repeat(order, slab)) * slab + column % slab
    shuffle = (column[:, None] == source[None, :]).astype(bf16)

    def relative(value):
        moved = mm(value, shuffle).astype(bf16)
        return moved[:, : model // 2], moved[:, model // 2 :]

    incoming_f = incoming.astype(f32)
    grad_b2 = jnp.sum(incoming_f, axis=0)
    left_two = relative(incoming)
    hidden_half = hidden_all // 2
    part_two = [
        reduce_over_dp(left_two, activated[:, c * hidden_half : (c + 1) * hidden_half], masks, c)
        for c in range(2)
    ]
    grad_hidden = (mm(incoming, w_two_t) * slope.astype(f32)).astype(bf16)
    grad_b1 = jnp.sum(grad_hidden.astype(f32), axis=0)
    left_one = relative(normed_two)
    part_one = [
        reduce_over_dp(left_one, grad_hidden[:, c * hidden_half : (c + 1) * hidden_half], masks, c)
        for c in range(2)
    ]

    def slots_of(halves, width):
        whole = jnp.concatenate(halves, axis=1)
        return [whole[:, s * width : (s + 1) * width] for s in range(head_size)]

    grad_w2 = reduce_over_head(slots_of(part_two, fc)).T
    grad_w1 = reduce_over_head(slots_of(part_one, fc))

    grad_normed_two = mm_nt(grad_hidden, w_one)
    grad_res_part, grad_g2, grad_s2 = norm_backward(
        grad_normed_two, standard_two, inverse_two, norm2_gain
    )
    grad_residual = incoming_f + grad_res_part
    grad_branch = grad_residual.astype(bf16)
    grad_bo = jnp.sum(grad_branch.astype(f32), axis=0)
    grad_att = mm(grad_branch, w_out_t).astype(bf16)
    grad_q, grad_own, grad_far = attention_call(
        attention_backward_kernel,
        has_far,
        [queries, kv_own, kv_far, grad_att],
        [heads_all, 2 * heads_all, 2 * heads_all],
    )
    far_back = mm_nt(grad_far, w_kv).astype(bf16).reshape(blocks, BLOCK, model)
    far_other = xor_swap(far_back, "dp", 1)
    valid = on_my_core & (targets_both >= 0)
    route_a = jnp.where(valid, index_a, -1)
    route_b = jnp.where(valid, index_b, -1)
    returned = []
    for color, held in enumerate(far_route(far_back, far_other, route_a, route_b, table_blocks)):
        for axis, mask in stage_lists[color][::-1]:
            keep = held.shape[0] // 2
            got = xor_swap(held[keep:], axis, mask)
            held = held[:keep].astype(f32) + got.astype(f32)
            if keep > blocks:
                held = held.astype(bf16)
        returned.append(held)
    returned = jnp.concatenate(returned, axis=2).reshape(tokens, model).astype(f32)

    left_q, left_o = relative(normed), relative(grad_branch)
    left_kv = tuple(
        jnp.concatenate([a, b], axis=0) for a, b in zip(left_q, relative(far))
    )
    grad_kv = jnp.concatenate([grad_own, grad_far], axis=0)
    part_q = reduce_over_dp(left_q, grad_q, masks, 0)
    part_k = reduce_over_dp(left_kv, grad_kv[:, :heads_all], masks, 0)
    part_v = reduce_over_dp(left_kv, grad_kv[:, heads_all:], masks, 1)
    part_o = reduce_over_dp(left_o, attended, masks, 1)
    per_slot = [
        jnp.concatenate([p[:, s * hc : (s + 1) * hc] for p in (part_q, part_k, part_v, part_o)], axis=1)
        for s in range(head_size)
    ]
    grad_wa = reduce_over_head(per_slot)
    grad_wqkv = jnp.stack([grad_wa[:, t * hc : (t + 1) * hc] for t in range(3)])
    grad_wo = grad_wa[:, 3 * hc :].T
    grad_bq = jnp.sum(grad_q.astype(f32), axis=0)
    grad_bv = jnp.sum(grad_kv[:, heads_all:].astype(f32), axis=0)

    grad_normed = mm_nt(grad_q, w_query) + mm_nt(grad_own, w_kv) + returned
    grad_join_part, grad_g1, grad_s1 = norm_backward(
        grad_normed, standard_one, inverse_one, norm1_gain
    )
    grad_joined = grad_residual + grad_join_part
    grad_up = jnp.sum(grad_joined.reshape(-1, UP, model) * coarse[:, None, :], axis=0)
    grad_input = from_micro(grad_joined.astype(bf16)).astype(f32)
    grad_coarse = jnp.sum(grad_input.reshape(micro, -1, UP, model) * up_gain, axis=2)

    def absolute(value, width):
        return jnp.roll(value.reshape(head_size, width), here, axis=0).reshape(-1)

    pieces = [
        grad_up.reshape(-1),
        grad_g1,
        grad_s1,
        absolute(grad_bq, hc),
        absolute(grad_bv, hc),
        grad_bo,
        grad_g2,
        grad_s2,
        absolute(grad_b1, fc),
        grad_b2,
    ]
    sizes = [p.shape[0] for p in pieces]
    total = jnp.concatenate(pieces).reshape(-1, model)
    for axis, size in (("dp", dp_size), ("head", head_size)):
        for i in range(size.bit_length() - 1):
            total = total + xor_swap(total, axis, 1 << i)
    total = total.reshape(-1)
    sums, at = [], 0
    for size in sizes:
        sums.append(total[at : at + size])
        at += size
    s_up, s_g1, s_s1, s_bq, s_bv, s_bo, s_g2, s_s2, s_b1, s_b2 = sums
    return (
        layer_out,
        grad_input,
        grad_coarse,
        s_up.reshape(UP, model),
        s_g1,
        s_s1,
        grad_wqkv,
        jnp.stack([s_bq, s_bv]),
        grad_wo,
        s_bo,
        s_g2,
        s_s2,
        grad_w1,
        s_b1,
        grad_w2,
        s_b2,
    )


def solution(mesh):
    rows = P(None, ("dp", "head"), None)
    return jax.shard_map(
        local,
        mesh=mesh,
        in_specs=(
            rows,
            rows,
            rows,
            P(),
            P(),
            P(),
            P(),
            P(None, None, "head"),
            P(None, "head"),
            P("head", None),
            P(),
            P(),
            P(),
            P(None, "head"),
            P("head"),
            P("head", None),
            P(),
        ),
        out_specs=(
            rows,
            rows,
            rows,
            P(),
            P(),
            P(),
            P(None, "dp", "head"),
            P(),
            P("head", "dp"),
            P(),
            P(),
            P(),
            P("dp", "head"),
            P(),
            P("head", "dp"),
            P(),
        ),
        check_vma=False,
    )
```

```python
import functools
import math

import jax
import jax.numpy as jnp
from jax import lax
from jax.experimental import pallas as pl
from jax.experimental.pallas import tpu as pltpu
from jax.sharding import PartitionSpec as P

HEAD_DIM = 64
BLOCK = 128
UP = 4
PAIR = 2 * HEAD_DIM
NEGATIVE = -1e30
epsilon = 1e-05
f32 = jnp.float32
bf16 = jnp.bfloat16
ROOT_2_PI = math.sqrt(2.0 / math.pi)
ANY = pl.BlockSpec(memory_space=pl.ANY)


def xor_swap(value, axis, mask):
    size = lax.axis_size(axis)
    return lax.ppermute(value, axis, [(i, i ^ mask) for i in range(size)])


def norm_forward(values, gain, shift):
    centered = values - jnp.mean(values, axis=-1, keepdims=True)
    inverse = lax.rsqrt(jnp.mean(centered * centered, axis=-1, keepdims=True) + epsilon)
    standard = centered * inverse
    return (standard * gain + shift, standard, inverse)


def norm_backward(upstream, standard, inverse, gain):
    scaled = upstream * gain
    inner = (
        scaled
        - jnp.mean(scaled, axis=-1, keepdims=True)
        - standard * jnp.mean(scaled * standard, axis=-1, keepdims=True)
    )
    return (inner * inverse, jnp.sum(upstream * standard, axis=0), jnp.sum(upstream, axis=0))


def mm(left, right):
    return jnp.dot(left, right, preferred_element_type=f32)


def mm_nt(left, right):
    return lax.dot_general(left, right, (((1,), (1,)), ((), ())), preferred_element_type=f32)


def mm_tn(left, right):
    return lax.dot_general(left, right, (((0,), (0,)), ((), ())), preferred_element_type=f32)


def pair_probs(q_pair, k_cat, allowed):
    low_half = lax.broadcasted_iota(jnp.int32, (BLOCK, PAIR), 1) < HEAD_DIM
    zero = jnp.zeros_like(q_pair)
    q_stack = jnp.concatenate(
        [jnp.where(low_half, q_pair, zero), jnp.where(low_half, zero, q_pair)], axis=0
    )
    scores = mm_nt(k_cat, q_stack) * (1.0 / math.sqrt(HEAD_DIM))
    scores = jnp.where(allowed, scores, NEGATIVE)
    top = jnp.max(scores, axis=0, keepdims=True)
    raised = jnp.exp(scores - top)
    probs = raised * (1.0 / jnp.sum(raised, axis=0, keepdims=True))
    return q_stack, probs, low_half


def allowed_mask(far_flag):
    key_at = lax.broadcasted_iota(jnp.int32, (2 * BLOCK, 2 * BLOCK), 0)
    query_at = lax.broadcasted_iota(jnp.int32, (2 * BLOCK, 2 * BLOCK), 1)
    query_at = jnp.where(query_at >= BLOCK, query_at - BLOCK, query_at)
    first = jnp.where(far_flag > 0, BLOCK, 2 * BLOCK)
    return (key_at <= query_at) | (key_at >= first)


def attention_forward_kernel(pairs, has_far, q_ref, own_ref, far_ref, out_ref):
    allowed = allowed_mask(has_far[pl.program_id(0)])
    width = pairs * PAIR
    for p in range(pairs):
        cols = slice(p * PAIR, (p + 1) * PAIR)
        vcols = slice(width + p * PAIR, width + (p + 1) * PAIR)
        k_cat = jnp.concatenate([own_ref[:, cols], far_ref[:, cols]], axis=0)
        v_cat = jnp.concatenate([own_ref[:, vcols], far_ref[:, vcols]], axis=0)
        _, probs, low_half = pair_probs(q_ref[:, cols], k_cat, allowed)
        mixed = mm_tn(probs.astype(bf16), v_cat)
        out_ref[:, cols] = jnp.where(low_half, mixed[:BLOCK], mixed[BLOCK:]).astype(bf16)


def attention_backward_kernel(
    pairs, has_far, q_ref, own_ref, far_ref, grad_ref, dq_ref, down_ref, dfar_ref
):
    allowed = allowed_mask(has_far[pl.program_id(0)])
    width = pairs * PAIR
    scale = 1.0 / math.sqrt(HEAD_DIM)
    for p in range(pairs):
        cols = slice(p * PAIR, (p + 1) * PAIR)
        vcols = slice(width + p * PAIR, width + (p + 1) * PAIR)
        k_cat = jnp.concatenate([own_ref[:, cols], far_ref[:, cols]], axis=0)
        v_cat = jnp.concatenate([own_ref[:, vcols], far_ref[:, vcols]], axis=0)
        q_stack, probs, low_half = pair_probs(q_ref[:, cols], k_cat, allowed)
        grad = grad_ref[:, cols]
        zero = jnp.zeros_like(grad)
        grad_stack = jnp.concatenate(
            [jnp.where(low_half, grad, zero), jnp.where(low_half, zero, grad)], axis=0
        )
        grad_probs = mm_nt(v_cat, grad_stack)
        total = jnp.sum(probs * grad_probs, axis=0, keepdims=True)
        grad_scores = (probs * (grad_probs - total)).astype(bf16)
        dq = mm_tn(grad_scores, k_cat) * scale
        dq_ref[:, cols] = jnp.where(low_half, dq[:BLOCK], dq[BLOCK:]).astype(bf16)
        dk = (mm(grad_scores, q_stack) * scale).astype(bf16)
        dv = mm(probs.astype(bf16), grad_stack).astype(bf16)
        down_ref[:, cols] = dk[:BLOCK]
        dfar_ref[:, cols] = dk[BLOCK:]
        down_ref[:, vcols] = dv[:BLOCK]
        dfar_ref[:, vcols] = dv[BLOCK:]


def attention_call(kernel, has_far, blocked, outs):
    blocks = has_far.shape[0]
    row_block = lambda width: pl.BlockSpec((BLOCK, width), lambda b, flags: (b, 0))
    width = blocked[0].shape[1]
    return pl.pallas_call(
        functools.partial(kernel, width // PAIR),
        grid_spec=pltpu.PrefetchScalarGridSpec(
            num_scalar_prefetch=1,
            grid=(blocks,),
            in_specs=[row_block(a.shape[1]) for a in blocked],
            out_specs=[row_block(w) for w in outs],
        ),
        out_shape=[jax.ShapeDtypeStruct((blocks * BLOCK, w), bf16) for w in outs],
        compiler_params=pltpu.CompilerParams(vmem_limit_bytes=48 << 20),
        cost_estimate=pl.CostEstimate(
            flops=blocks * width * BLOCK * BLOCK * 16,
            bytes_accessed=blocks * BLOCK * width * 16,
            transcendentals=blocks * width * BLOCK * 4,
        ),
    )(has_far, *blocked)


def far_pick_kernel(where_a, where_b, a_ref, b_ref, out_ref):
    half = a_ref.shape[2]
    out_ref[0, :, :half] = a_ref[0]
    out_ref[0, :, half:] = b_ref[0]


def far_pick(table_a, table_b, where_a, where_b):
    count, half = where_a.shape[0], table_a.shape[2]
    spec = lambda which: pl.BlockSpec((1, BLOCK, half), lambda j, wa, wb: ((wa, wb)[which][j], 0, 0))
    return pl.pallas_call(
        far_pick_kernel,
        grid_spec=pltpu.PrefetchScalarGridSpec(
            num_scalar_prefetch=2,
            grid=(count,),
            in_specs=[spec(0), spec(1)],
            out_specs=pl.BlockSpec((1, BLOCK, 2 * half), lambda j, wa, wb: (j, 0, 0)),
        ),
        out_shape=jax.ShapeDtypeStruct((count, BLOCK, 2 * half), bf16),
        cost_estimate=pl.CostEstimate(
            flops=0, bytes_accessed=count * BLOCK * half * 8, transcendentals=0
        ),
    )(where_a, where_b, table_a, table_b)


def far_route_kernel(count, where_a, where_b, mine_ref, other_ref, a_ref, b_ref, acc_ref):
    step = pl.program_id(0)
    half = a_ref.shape[2]
    acc_ref[...] = jnp.zeros_like(acc_ref)
    for source, base in ((mine_ref, 0), (other_ref, count)):
        for j in range(count):

            @pl.when(where_a[base + j] == step)
            def _():
                acc_ref[:, :half] += source[j, :, :half].astype(f32)

            @pl.when(where_b[base + j] == step)
            def _():
                acc_ref[:, half:] += source[j, :, half:].astype(f32)

    a_ref[0] = acc_ref[:, :half].astype(bf16)
    b_ref[0] = acc_ref[:, half:].astype(bf16)


def far_route(mine, other, where_a, where_b, table):
    count, _, width = mine.shape
    whole = pl.BlockSpec(mine.shape, lambda k, wa, wb: (0, 0, 0))
    out = pl.BlockSpec((1, BLOCK, width // 2), lambda k, wa, wb: (k, 0, 0))
    shape = jax.ShapeDtypeStruct((table, BLOCK, width // 2), bf16)
    return pl.pallas_call(
        functools.partial(far_route_kernel, count),
        grid_spec=pltpu.PrefetchScalarGridSpec(
            num_scalar_prefetch=2,
            grid=(table,),
            in_specs=[whole, whole],
            out_specs=[out, out],
            scratch_shapes=[pltpu.VMEM((BLOCK, width), f32)],
        ),
        out_shape=[shape, shape],
        compiler_params=pltpu.CompilerParams(vmem_limit_bytes=32 << 20),
        cost_estimate=pl.CostEstimate(
            flops=0, bytes_accessed=table * BLOCK * width * 2, transcendentals=0
        ),
    )(where_a, where_b, mine, other)


def gather_strips(strip, masks):
    head_size = lax.axis_size("head")
    slots = jnp.stack(
        [
            lax.ppermute(strip, "head", [((i + s) % head_size, i) for i in range(head_size)])
            for s in range(1, head_size)
        ]
    )
    half = strip.shape[0] // 2
    out = []
    for color, order in ((0, masks), (1, masks[::-1])):
        held = slots[None, :, color * half : (color + 1) * half]
        for mask in order:
            held = jnp.concatenate([held, xor_swap(held, "dp", mask)], axis=0)
        out.append(held)
    return out + [xor_swap(held, "dp", 1) for held in out]


def relative_masks(masks):
    return [sum(m for bit, m in enumerate(masks) if k >> bit & 1) for k in range(1 << len(masks))]


def assemble_kernel(columns, n_own, n_out, dp_index, *refs):
    tables, own, outs = refs[:4], refs[4 : 4 + n_own], refs[4 + n_own :]
    slots, half = tables[0].shape[1], tables[0].shape[2]

    def fill(first, second):
        for color, table in enumerate((first, second)):
            rows = slice(color * half, (color + 1) * half)
            for c0, width, target, t0 in columns:
                for s in range(slots):
                    at = t0 + (s + 1) * width
                    outs[target][rows, at : at + width] = table[0, s, :, c0 : c0 + width]

    core = pl.program_id(0)

    @pl.when(core == 0)
    def _():
        fill(tables[0], tables[1])

    @pl.when(core == 1)
    def _():
        fill(tables[2], tables[3])

    for ref, (c0, width, target, t0) in zip(own, columns):
        outs[target][:, t0 : t0 + width] = ref[...]


def assemble(dp_index, tables, own, columns, masks, widths):
    bits = len(masks)
    count, slots, half, width = tables[0].shape
    model = 2 * count * 2 * half

    def reverse(k):
        return sum(((k >> i) & 1) << (bits - 1 - i) for i in range(bits))

    def table_spec(which):
        def index(core, k, dp):
            k = jnp.where(core == which // 2, k, 0 if which >= 2 else count - 1)
            return (reverse(k) if which % 2 else k, 0, 0, 0)

        return pl.BlockSpec((1, slots, half, width), index)

    def row(core, k, dp):
        return (dp[0] ^ ((k << 1) | core), 0)

    return pl.pallas_call(
        functools.partial(assemble_kernel, columns, len(own), len(widths)),
        grid_spec=pltpu.PrefetchScalarGridSpec(
            num_scalar_prefetch=1,
            grid=(2, count),
            in_specs=[table_spec(i) for i in range(4)]
            + [pl.BlockSpec((2 * half, o.shape[1]), row) for o in own],
            out_specs=[pl.BlockSpec((2 * half, w), row) for w in widths],
        ),
        out_shape=[jax.ShapeDtypeStruct((model, w), bf16) for w in widths],
        compiler_params=pltpu.CompilerParams(vmem_limit_bytes=48 << 20),
        cost_estimate=pl.CostEstimate(
            flops=0, bytes_accessed=4 * model * sum(widths), transcendentals=0
        ),
    )(dp_index, *tables, *own)


def reduce_over_dp(left, right, masks, color):
    keep, send = left
    got = xor_swap(mm_tn(send, right).astype(bf16), "dp", 1)
    part = (mm_tn(keep, right) + got.astype(f32)).astype(bf16)
    bits = len(masks)
    width = part.shape[1]
    part = part.reshape((2,) * bits + (-1, width))
    order = masks if color == 0 else masks[::-1]
    axes = {mask: bits - 1 - i for i, mask in enumerate(masks)}
    live = list(masks)
    for step, mask in enumerate(order):
        axis = len(live) - 1 - live.index(mask)
        live.remove(mask)
        mine = lax.index_in_dim(part, 0, axis, keepdims=False)
        away = lax.index_in_dim(part, 1, axis, keepdims=False)
        got = xor_swap(away, "dp", mask)
        part = (mine.astype(f32) + got.astype(f32)).astype(bf16)
    return part


def reduce_over_head(parts):
    head_size = lax.axis_size("head")
    total = parts[0].astype(f32)
    for s in range(1, head_size):
        got = lax.ppermute(parts[s], "head", [(i, (i + s) % head_size) for i in range(head_size)])
        total = total + got.astype(f32)
    return total


def local(
    activations,
    conditioning,
    cotangent,
    block_targets,
    up_gain,
    norm1_gain,
    norm1_shift,
    w_qkv,
    b_qv,
    w_out,
    b_out,
    norm2_gain,
    norm2_shift,
    w_fc1,
    b_fc1,
    w_fc2,
    b_fc2,
):
    micro, rows, model = activations.shape
    head_cols = w_qkv.shape[2]
    hidden_cols = w_fc1.shape[1]
    dp_size, head_size = lax.axis_size("dp"), lax.axis_size("head")
    me, here = lax.axis_index("dp"), lax.axis_index("head")
    group = head_size // micro
    tokens = rows * micro
    blocks = tokens // BLOCK
    slab = model // dp_size
    masks = [1 << i for i in range(1, dp_size.bit_length() - 1)]
    heads_all, hidden_all = head_cols * head_size, hidden_cols * head_size

    src_rank = here % micro
    my_micro, my_sub = here // group, here % group
    shifts = [
        [(hs * micro + hr, ((hr + s) % micro) * group + hs) for hs in range(group) for hr in range(micro)]
        for s in range(micro)
    ]

    def send(value, pairs):
        return value if all(a == b for a, b in pairs) else lax.ppermute(value, "head", pairs)

    def choose(options, index):
        out = options[-1]
        for k in range(len(options) - 1):
            out = jnp.where(index == k, options[k], out)
        return out

    def to_micro(value):
        got = [
            send(lax.dynamic_index_in_dim(value, (src_rank + s) % micro, 0, False), shifts[s])
            for s in range(micro)
        ]
        return [choose(got, (my_micro - p) % micro) for p in range(micro)]

    def from_micro(value):
        pieces = value.reshape(micro, rows, -1)
        got = [
            send(
                lax.dynamic_index_in_dim(pieces, (my_micro - s) % micro, 0, False),
                [(b, a) for a, b in shifts[s]],
            )
            for s in range(micro)
        ]
        return jnp.stack([choose(got, (m - src_rank) % micro) for m in range(micro)])

    packed = to_micro(jnp.concatenate([activations, conditioning], axis=1))
    acts = jnp.concatenate([p[:rows] for p in packed], axis=0)
    coarse = jnp.concatenate([p[rows:] for p in packed], axis=0).astype(f32)
    incoming = jnp.concatenate(to_micro(cotangent), axis=0)

    def my_slab(value, axis):
        return lax.dynamic_slice_in_dim(value, me * slab, slab, axis)

    strip_a = jnp.concatenate(
        [my_slab(w_qkv[0], 0), my_slab(w_qkv[1], 0), my_slab(w_qkv[2], 0), my_slab(w_out, 1).T],
        axis=1,
    )
    strip_f = jnp.concatenate([my_slab(w_fc1, 0), my_slab(w_fc2, 1).T], axis=1)
    dp_index = me.reshape(1).astype(jnp.int32)
    hc, fc = head_cols, hidden_cols
    got_a = gather_strips(strip_a, masks)
    w_query, w_kv, w_out_t = assemble(
        dp_index,
        got_a,
        [w_qkv[0], w_qkv[1], w_qkv[2], w_out.T],
        [(0, hc, 0, 0), (hc, hc, 1, 0), (2 * hc, hc, 1, heads_all), (3 * hc, hc, 2, 0)],
        masks,
        [heads_all, 2 * heads_all, heads_all],
    )
    got_f = gather_strips(strip_f, masks)
    w_one, w_two_t = assemble(
        dp_index,
        got_f,
        [w_fc1, w_fc2.T],
        [(0, fc, 0, 0), (fc, fc, 1, 0)],
        masks,
        [hidden_all, hidden_all],
    )
    small = jnp.concatenate([b_qv.reshape(-1), b_fc1])
    biases = [small] + [
        lax.ppermute(small, "head", [((i + s) % head_size, i) for i in range(head_size)])
        for s in range(1, head_size)
    ]
    bias_q = jnp.concatenate([b[:hc] for b in biases])
    bias_v = jnp.concatenate([b[hc : 2 * hc] for b in biases])
    bias_one = jnp.concatenate([b[2 * hc :] for b in biases])
    bias_kv = jnp.concatenate([jnp.zeros_like(bias_v), bias_v])

    joined = (
        acts.astype(f32).reshape(-1, UP, model) + coarse[:, None, :] * up_gain[None]
    ).reshape(tokens, model)
    normed_f, standard_one, inverse_one = norm_forward(joined, norm1_gain, norm1_shift)
    normed = normed_f.astype(bf16)

    stages_sub = [("head", 1 << i) for i in range(group.bit_length() - 1)]
    stage_lists = [
        stages_sub + [("dp", m) for m in masks],
        stages_sub + [("dp", m) for m in masks[::-1]],
    ]
    shaped = normed.reshape(blocks, BLOCK, model)
    half = model // 2
    tables = []
    for color in range(2):
        held = shaped[:, :, color * half : (color + 1) * half]
        for axis, mask in stage_lists[color]:
            held = jnp.concatenate([held, xor_swap(held, axis, mask)], axis=0)
        tables.append(held)
    table_blocks = tables[0].shape[0]
    table_row = lax.dynamic_index_in_dim(block_targets, my_micro, 0, False)

    def targets_of(device):
        return lax.dynamic_slice_in_dim(table_row, (device * group + my_sub) * blocks, blocks)

    targets = targets_of(me)
    targets_both = jnp.concatenate([targets, targets_of(me ^ 1)])
    owner = jnp.maximum(targets_both, 0) // blocks
    away = (owner // group) ^ me
    away_sub = (owner % group) ^ my_sub

    def table_index(stages):
        index = jnp.zeros_like(owner)
        for bit, (axis, mask) in enumerate(stages):
            far_bits = away if axis == "dp" else away_sub
            index = index + (((far_bits & mask) != 0).astype(jnp.int32) << bit)
        return index * blocks + jnp.maximum(targets_both, 0) % blocks

    index_a, index_b = table_index(stage_lists[0]), table_index(stage_lists[1])
    on_my_core = (away & 1) == 0
    picked = far_pick(tables[0], tables[1], index_a, index_b)
    passed = xor_swap(picked[blocks:], "dp", 1)
    far = jnp.where(on_my_core[:blocks, None, None], picked[:blocks], passed).reshape(tokens, model)
    has_far = (targets >= 0).astype(jnp.int32)

    queries = (mm(normed, w_query) + bias_q).astype(bf16)
    kv_own = (mm(normed, w_kv) + bias_kv).astype(bf16)
    kv_far = (mm(far, w_kv) + bias_kv).astype(bf16)
    (attended,) = attention_call(
        attention_forward_kernel, has_far, [queries, kv_own, kv_far], [heads_all]
    )
    residual = joined + (mm_nt(attended, w_out_t) + b_out)

    normed2_f, standard_two, inverse_two = norm_forward(residual, norm2_gain, norm2_shift)
    normed_two = normed2_f.astype(bf16)
    hidden = mm(normed_two, w_one) + bias_one
    inner = jnp.tanh(ROOT_2_PI * (hidden + 0.044715 * hidden * hidden * hidden))
    activated = (0.5 * hidden * (1.0 + inner)).astype(bf16)
    slope = (
        0.5 * (1.0 + inner)
        + 0.5 * hidden * (1.0 - inner * inner) * (ROOT_2_PI * (1.0 + 3 * 0.044715 * hidden * hidden))
    ).astype(bf16)
    layer_out = from_micro((residual + (mm_nt(activated, w_two_t) + b_fc2)).astype(bf16))

    position_masks = relative_masks(masks)
    order = jnp.array(position_masks + [m | 1 for m in position_masks], jnp.int32)
    column = jnp.arange(model, dtype=jnp.int32)
    source = (me ^ jnp.repeat(order, slab)) * slab + column % slab
    shuffle = (column[:, None] == source[None, :]).astype(bf16)

    def relative(value):
        moved = mm(value, shuffle).astype(bf16)
        return moved[:, : model // 2], moved[:, model // 2 :]

    incoming_f = incoming.astype(f32)
    grad_b2 = jnp.sum(incoming_f, axis=0)
    left_two = relative(incoming)
    hidden_half = hidden_all // 2
    part_two = [
        reduce_over_dp(left_two, activated[:, c * hidden_half : (c + 1) * hidden_half], masks, c)
        for c in range(2)
    ]
    grad_hidden = (mm(incoming, w_two_t) * slope.astype(f32)).astype(bf16)
    grad_b1 = jnp.sum(grad_hidden.astype(f32), axis=0)
    left_one = relative(normed_two)
    part_one = [
        reduce_over_dp(left_one, grad_hidden[:, c * hidden_half : (c + 1) * hidden_half], masks, c)
        for c in range(2)
    ]

    def slots_of(halves, width):
        whole = jnp.concatenate(halves, axis=1)
        return [whole[:, s * width : (s + 1) * width] for s in range(head_size)]

    grad_w2 = reduce_over_head(slots_of(part_two, fc)).T
    grad_w1 = reduce_over_head(slots_of(part_one, fc))

    grad_normed_two = mm_nt(grad_hidden, w_one)
    grad_res_part, grad_g2, grad_s2 = norm_backward(
        grad_normed_two, standard_two, inverse_two, norm2_gain
    )
    grad_residual = incoming_f + grad_res_part
    grad_branch = grad_residual.astype(bf16)
    grad_bo = jnp.sum(grad_branch.astype(f32), axis=0)
    grad_att = mm(grad_branch, w_out_t).astype(bf16)
    grad_q, grad_own, grad_far = attention_call(
        attention_backward_kernel,
        has_far,
        [queries, kv_own, kv_far, grad_att],
        [heads_all, 2 * heads_all, 2 * heads_all],
    )
    far_back = mm_nt(grad_far, w_kv).astype(bf16).reshape(blocks, BLOCK, model)
    far_other = xor_swap(far_back, "dp", 1)
    valid = on_my_core & (targets_both >= 0)
    route_a = jnp.where(valid, index_a, -1)
    route_b = jnp.where(valid, index_b, -1)
    returned = []
    for color, held in enumerate(far_route(far_back, far_other, route_a, route_b, table_blocks)):
        for axis, mask in stage_lists[color][::-1]:
            keep = held.shape[0] // 2
            got = xor_swap(held[keep:], axis, mask)
            held = held[:keep].astype(f32) + got.astype(f32)
            if keep > blocks:
                held = held.astype(bf16)
        returned.append(held)
    returned = jnp.concatenate(returned, axis=2).reshape(tokens, model).astype(f32)

    left_q, left_o = relative(normed), relative(grad_branch)
    left_kv = tuple(
        jnp.concatenate([a, b], axis=0) for a, b in zip(left_q, relative(far))
    )
    grad_kv = jnp.concatenate([grad_own, grad_far], axis=0)
    part_q = reduce_over_dp(left_q, grad_q, masks, 0)
    part_k = reduce_over_dp(left_kv, grad_kv[:, :heads_all], masks, 0)
    part_v = reduce_over_dp(left_kv, grad_kv[:, heads_all:], masks, 1)
    part_o = reduce_over_dp(left_o, attended, masks, 1)
    per_slot = [
        jnp.concatenate([p[:, s * hc : (s + 1) * hc] for p in (part_q, part_k, part_v, part_o)], axis=1)
        for s in range(head_size)
    ]
    grad_wa = reduce_over_head(per_slot)
    grad_wqkv = jnp.stack([grad_wa[:, t * hc : (t + 1) * hc] for t in range(3)])
    grad_wo = grad_wa[:, 3 * hc :].T
    grad_bq = jnp.sum(grad_q.astype(f32), axis=0)
    grad_bv = jnp.sum(grad_kv[:, heads_all:].astype(f32), axis=0)

    grad_normed = mm_nt(grad_q, w_query) + mm_nt(grad_own, w_kv) + returned
    grad_join_part, grad_g1, grad_s1 = norm_backward(
        grad_normed, standard_one, inverse_one, norm1_gain
    )
    grad_joined = grad_residual + grad_join_part
    grad_up = jnp.sum(grad_joined.reshape(-1, UP, model) * coarse[:, None, :], axis=0)
    grad_input = from_micro(grad_joined.astype(bf16)).astype(f32)
    grad_coarse = jnp.sum(grad_input.reshape(micro, -1, UP, model) * up_gain, axis=2)

    def absolute(value, width):
        return jnp.roll(value.reshape(head_size, width), here, axis=0).reshape(-1)

    pieces = [
        grad_up.reshape(-1),
        grad_g1,
        grad_s1,
        absolute(grad_bq, hc),
        absolute(grad_bv, hc),
        grad_bo,
        grad_g2,
        grad_s2,
        absolute(grad_b1, fc),
        grad_b2,
    ]
    sizes = [p.shape[0] for p in pieces]
    total = jnp.concatenate(pieces).reshape(-1, model)
    for axis, size in (("dp", dp_size), ("head", head_size)):
        for i in range(size.bit_length() - 1):
            total = total + xor_swap(total, axis, 1 << i)
    total = total.reshape(-1)
    sums, at = [], 0
    for size in sizes:
        sums.append(total[at : at + size])
        at += size
    s_up, s_g1, s_s1, s_bq, s_bv, s_bo, s_g2, s_s2, s_b1, s_b2 = sums
    return (
        layer_out,
        grad_input,
        grad_coarse,
        s_up.reshape(UP, model),
        s_g1,
        s_s1,
        grad_wqkv,
        jnp.stack([s_bq, s_bv]),
        grad_wo,
        s_bo,
        s_g2,
        s_s2,
        grad_w1,
        s_b1,
        grad_w2,
        s_b2,
    )


def solution(mesh):
    rows = P(None, ("dp", "head"), None)
    return jax.shard_map(
        local,
        mesh=mesh,
        in_specs=(
            rows,
            rows,
            rows,
            P(),
            P(),
            P(),
            P(),
            P(None, None, "head"),
            P(None, "head"),
            P("head", None),
            P(),
            P(),
            P(),
            P(None, "head"),
            P("head"),
            P("head", None),
            P(),
        ),
        out_specs=(
            rows,
            rows,
            rows,
            P(),
            P(),
            P(),
            P(None, "dp", "head"),
            P(),
            P("head", "dp"),
            P(),
            P(),
            P(),
            P("dp", "head"),
            P(),
            P("head", "dp"),
            P(),
        ),
        check_vma=False,
    )
```

```python
import functools
import math

import jax
import jax.numpy as jnp
from jax import lax
from jax.experimental import pallas as pl
from jax.experimental.pallas import tpu as pltpu
from jax.sharding import PartitionSpec as P

HEAD_DIM = 64
BLOCK = 128
UP = 4
HALVES = 2
VMEM_LIMIT = 58 << 20
PAIR = 2 * HEAD_DIM
NEGATIVE = -1e30
epsilon = 1e-05
f32 = jnp.float32
bf16 = jnp.bfloat16
ROOT_2_PI = math.sqrt(2.0 / math.pi)
LONG_COST = pl.CostEstimate(flops=1 << 36, bytes_accessed=1 << 26, transcendentals=0)


def xor_swap(value, axis, mask):
    size = lax.axis_size(axis)
    return lax.ppermute(value, axis, [(i, i ^ mask) for i in range(size)])


def pause_kernel(value_ref, out_ref):
    out_ref[...] = value_ref[...]


class Order:
    def __init__(self):
        self.last = ()
        self.token = None

    def __call__(self, *values):
        tied = lax.optimization_barrier(tuple(values) + self.last)[: len(values)]
        return tied[0] if len(values) == 1 else tied

    def mark(self, *values):
        self.last = values

    def pause(self):
        self.token = self(jnp.zeros((8, 128), f32) if self.token is None else self.token)
        self.token = pl.pallas_call(
            pause_kernel, out_shape=jax.ShapeDtypeStruct((8, 128), f32), cost_estimate=LONG_COST
        )(self.token)
        self.mark(self.token)


def norm_forward(values, gain, shift):
    centered = values - jnp.mean(values, axis=-1, keepdims=True)
    inverse = lax.rsqrt(jnp.mean(centered * centered, axis=-1, keepdims=True) + epsilon)
    standard = centered * inverse
    return (standard * gain + shift, standard, inverse)


def norm_backward(upstream, standard, inverse, gain):
    scaled = upstream * gain
    inner = (
        scaled
        - jnp.mean(scaled, axis=-1, keepdims=True)
        - standard * jnp.mean(scaled * standard, axis=-1, keepdims=True)
    )
    return (inner * inverse, jnp.sum(upstream * standard, axis=0), jnp.sum(upstream, axis=0))


def mm(left, right):
    return jnp.dot(left, right, preferred_element_type=f32)


def mm_nt(left, right):
    return lax.dot_general(left, right, (((1,), (1,)), ((), ())), preferred_element_type=f32)


def mm_tn(left, right):
    return lax.dot_general(left, right, (((0,), (0,)), ((), ())), preferred_element_type=f32)


def pair_probs(q_pair, k_cat, allowed):
    low_half = lax.broadcasted_iota(jnp.int32, (BLOCK, PAIR), 1) < HEAD_DIM
    zero = jnp.zeros_like(q_pair)
    q_stack = jnp.concatenate(
        [jnp.where(low_half, q_pair, zero), jnp.where(low_half, zero, q_pair)], axis=0
    )
    scores = mm_nt(k_cat, q_stack) * (1.0 / math.sqrt(HEAD_DIM))
    scores = jnp.where(allowed, scores, NEGATIVE)
    top = jnp.max(scores, axis=0, keepdims=True)
    raised = jnp.exp(scores - top)
    probs = raised * (1.0 / jnp.sum(raised, axis=0, keepdims=True))
    return q_stack, probs, low_half


def allowed_mask(far_flag):
    key_at = lax.broadcasted_iota(jnp.int32, (2 * BLOCK, 2 * BLOCK), 0)
    query_at = lax.broadcasted_iota(jnp.int32, (2 * BLOCK, 2 * BLOCK), 1)
    query_at = jnp.where(query_at >= BLOCK, query_at - BLOCK, query_at)
    first = jnp.where(far_flag > 0, BLOCK, 2 * BLOCK)
    return (key_at <= query_at) | (key_at >= first)


def pair_columns(p, width):
    return [slice(t * width + p * PAIR, t * width + (p + 1) * PAIR) for t in range(3)]


def key_value(own_ref, far_ref, columns, width):
    out = []
    for cols in columns[1:]:
        far_cols = slice(cols.start - width, cols.stop - width)
        out.append(jnp.concatenate([own_ref[:, cols], far_ref[:, far_cols]], axis=0))
    return out


def attention_forward_kernel(pairs, has_far, own_ref, far_ref, out_ref):
    allowed = allowed_mask(has_far[pl.program_id(0)])
    width = pairs * PAIR
    for p in range(pairs):
        columns = pair_columns(p, width)
        k_cat, v_cat = key_value(own_ref, far_ref, columns, width)
        _, probs, low_half = pair_probs(own_ref[:, columns[0]], k_cat, allowed)
        mixed = mm_tn(probs.astype(bf16), v_cat)
        out_ref[:, columns[0]] = jnp.where(low_half, mixed[:BLOCK], mixed[BLOCK:]).astype(bf16)


def attention_forward(has_far, own, far, width):
    blocks = has_far.shape[0]
    row_block = lambda array: pl.BlockSpec((BLOCK, array.shape[1]), lambda b, flags: (b, 0))
    shape = jax.ShapeDtypeStruct((blocks * BLOCK, width), bf16)
    return pl.pallas_call(
        functools.partial(attention_forward_kernel, width // PAIR),
        grid_spec=pltpu.PrefetchScalarGridSpec(
            num_scalar_prefetch=1,
            grid=(blocks,),
            in_specs=[row_block(own), row_block(far)],
            out_specs=row_block(shape),
        ),
        out_shape=shape,
        compiler_params=pltpu.CompilerParams(vmem_limit_bytes=16 << 20),
        cost_estimate=LONG_COST,
    )(has_far, own, far)


def attention_backward_kernel(pairs, has_far, own_ref, far_ref, grad_ref, out_ref):
    allowed = allowed_mask(has_far[pl.program_id(0)])
    width = pairs * PAIR
    scale = 1.0 / math.sqrt(HEAD_DIM)
    out_ref[1, :, :width] = jnp.zeros((BLOCK, width), bf16)
    for p in range(pairs):
        columns = pair_columns(p, width)
        k_cat, v_cat = key_value(own_ref, far_ref, columns, width)
        q_stack, probs, low_half = pair_probs(own_ref[:, columns[0]], k_cat, allowed)
        grad = grad_ref[:, columns[0]]
        zero = jnp.zeros_like(grad)
        grad_stack = jnp.concatenate(
            [jnp.where(low_half, grad, zero), jnp.where(low_half, zero, grad)], axis=0
        )
        grad_probs = mm_nt(v_cat, grad_stack)
        total = jnp.sum(probs * grad_probs, axis=0, keepdims=True)
        grad_scores = (probs * (grad_probs - total)).astype(bf16)
        dq = mm_tn(grad_scores, k_cat) * scale
        out_ref[0, :, columns[0]] = jnp.where(low_half, dq[:BLOCK], dq[BLOCK:]).astype(bf16)
        dk = (mm(grad_scores, q_stack) * scale).astype(bf16)
        dv = mm(probs.astype(bf16), grad_stack).astype(bf16)
        for half in range(2):
            rows = slice(half * BLOCK, (half + 1) * BLOCK)
            out_ref[half, :, columns[1]] = dk[rows]
            out_ref[half, :, columns[2]] = dv[rows]


def attention_backward(has_far, own, far, grad):
    blocks, width = has_far.shape[0], grad.shape[1]
    row_block = lambda array: pl.BlockSpec((BLOCK, array.shape[1]), lambda b, flags: (b, 0))
    return pl.pallas_call(
        functools.partial(attention_backward_kernel, width // PAIR),
        grid_spec=pltpu.PrefetchScalarGridSpec(
            num_scalar_prefetch=1,
            grid=(blocks,),
            in_specs=[row_block(own), row_block(far), row_block(grad)],
            out_specs=pl.BlockSpec((2, BLOCK, 3 * width), lambda b, flags: (0, b, 0)),
        ),
        out_shape=jax.ShapeDtypeStruct((2, blocks * BLOCK, 3 * width), bf16),
        compiler_params=pltpu.CompilerParams(vmem_limit_bytes=20 << 20),
        cost_estimate=LONG_COST,
    )(has_far, own, far, grad)


def join_kernel(rows, first, *refs):
    got, (tile_ref, gain_ref, shift_ref, joined_ref, normed_ref, coarse_ref, held_ref) = (
        refs[:-7],
        refs[-7:],
    )
    pieces = len(got)
    which = (first[0] + pieces - pl.program_id(0)) % pieces
    for s in range(pieces):

        @pl.when(which == s)
        def _():
            held_ref[...] = got[s][...]

    coarse = held_ref[rows:, :]
    coarse_ref[...] = coarse
    up_row = lax.broadcasted_iota(jnp.int32, (rows, rows // UP), 0) // UP
    up_col = lax.broadcasted_iota(jnp.int32, (rows, rows // UP), 1)
    spread = mm((up_row == up_col).astype(f32).astype(bf16), coarse)
    joined = held_ref[:rows, :].astype(f32) + spread * tile_ref[...]
    joined_ref[...] = joined
    normed_ref[...] = norm_forward(joined, gain_ref[...], shift_ref[...])[0].astype(bf16)


def join(first, got, tile, gain, shift):
    pieces, rows, model = len(got), tile.shape[0], tile.shape[1]
    small = rows // UP
    fixed = lambda array: pl.BlockSpec(array.shape, lambda p, f: (0, 0))
    piece = lambda count: pl.BlockSpec((count, model), lambda p, f: (p, 0))
    return pl.pallas_call(
        functools.partial(join_kernel, rows),
        grid_spec=pltpu.PrefetchScalarGridSpec(
            num_scalar_prefetch=1,
            grid=(pieces,),
            in_specs=[fixed(g) for g in got] + [fixed(tile), fixed(gain), fixed(shift)],
            out_specs=[piece(rows), piece(rows), piece(small)],
            scratch_shapes=[pltpu.VMEM((rows + small, model), bf16)],
        ),
        out_shape=[
            jax.ShapeDtypeStruct((pieces * rows, model), f32),
            jax.ShapeDtypeStruct((pieces * rows, model), bf16),
            jax.ShapeDtypeStruct((pieces * small, model), bf16),
        ],
        compiler_params=pltpu.CompilerParams(vmem_limit_bytes=16 << 20),
        cost_estimate=LONG_COST,
    )(first, *got, tile, gain, shift)


def fill_chunk(masks, me, tables, out_ref):
    half = tables[0].shape[2]
    for which, table in enumerate(tables):
        order = masks if which % 2 == 0 else masks[::-1]
        for k, mask in enumerate(relative_masks(order)):
            row = (me ^ (mask | (which // 2))) * 2 * half + (which % 2) * half
            out_ref[pl.ds(pl.multiple_of(row, half), half), :] = table[k, 0]


def load_chunk(masks, me, chunk, n_own, own_ref, tables, out_ref):
    @pl.when(chunk < n_own)
    def _():
        out_ref[...] = own_ref[...]

    @pl.when(chunk >= n_own)
    def _():
        fill_chunk(masks, me, tables, out_ref)


def by_parity(step, buffers, body):
    for parity in range(2):

        @pl.when(step % 2 == parity)
        def _():
            body(buffers[1 - parity], buffers[parity])


def scatter_rows(masks, color, me, value, held_ref):
    count = 2 << len(masks)
    slab = value.shape[0] // count
    last = len(masks) - 1
    for b in range(count):
        away = me ^ b
        at = (away & 1) << len(masks)
        for i, mask in enumerate(masks):
            place = last - i if isinstance(color, int) and color == 0 else i
            if not isinstance(color, int):
                place = jnp.where(color == 0, last - i, i)
            at = at + (((away >> (mask.bit_length() - 1)) & 1) << place)
        row = pl.multiple_of(at * slab, slab)
        held_ref[pl.ds(row, slab), :] = value[b * slab : (b + 1) * slab].astype(bf16)


def split_rows(held_ref, keep_ref, send_ref):
    half = held_ref.shape[0] // 2
    keep_ref[0] = held_ref[:half, :]
    send_ref[0] = held_ref[half:, :]


def feed_forward_kernel(masks, n_own, n, me, *refs):
    one_tables, two_tables = refs[:4], refs[4:8]
    (own_one, own_two, x_ref, bias_ref, residual_ref, last_ref, left_ref) = refs[8:15]
    slope_ref, out_ref, keep_ref, send_ref = refs[15:19]
    w_one, w_two, even_ref, odd_ref, act_ref, held_ref, acc_ref = refs[19:]
    step = pl.program_id(0)
    load_chunk(masks, me[0], jnp.minimum(step, n - 1), n_own, own_one, one_tables, w_one)
    load_chunk(masks, me[0], jnp.maximum(step - 1, 0), n_own, own_two, two_tables, w_two)
    ratio = ROOT_2_PI * 0.044715
    rows = x_ref.shape[0] // 2

    def body(before, now):
        for r in range(2):
            at = slice(r * rows, (r + 1) * rows)
            h = before[at, :]
            square = h * h
            gate = 0.5 + 0.5 * jnp.tanh(h * (ROOT_2_PI + ratio * square))
            act = (h * gate).astype(bf16)
            act_ref[at, :] = act
            slope_ref[at, :] = (
                gate * (1.0 + 2.0 * h * (1.0 - gate) * (ROOT_2_PI + 3.0 * ratio * square))
            ).astype(bf16)
            now[at, :] = mm(x_ref[at, :], w_one[...]) + bias_ref[...]
            acc_ref[at, :] += mm_nt(act, w_two[...])
        scatter_rows(masks, jnp.maximum(step - 1, 0) % n_own, me[0], mm(left_ref[...], act_ref[...]), held_ref)

    by_parity(step, (even_ref, odd_ref), body)
    split_rows(held_ref, keep_ref, send_ref)

    @pl.when(step == 0)
    def _():
        acc_ref[...] = jnp.zeros_like(acc_ref)

    @pl.when(step == n)
    def _():
        out_ref[...] = (residual_ref[...] + (acc_ref[...] + last_ref[...])).astype(bf16)


def feed_backward_kernel(masks, n_own, n, me, *refs):
    two_tables, one_tables = refs[:4], refs[4:8]
    own_two, own_one, g_ref, slope_ref, left_ref = refs[8:13]
    bias_ref, out_ref, keep_ref, send_ref = refs[13:17]
    w_two, w_one, even_ref, odd_ref, grad_ref, held_ref = refs[17:]
    step = pl.program_id(0)
    load_chunk(masks, me[0], jnp.minimum(step, n - 1), n_own, own_two, two_tables, w_two)
    load_chunk(masks, me[0], jnp.maximum(step - 1, 0), n_own, own_one, one_tables, w_one)
    rows = g_ref.shape[0] // 2

    def body(before, now):
        sums = []
        for r in range(2):
            at = slice(r * rows, (r + 1) * rows)
            grad = (before[at, :] * slope_ref[at, :].astype(f32)).astype(bf16)
            grad_ref[at, :] = grad
            sums.append(jnp.sum(grad.astype(f32), axis=0, keepdims=True))
            now[at, :] = mm(g_ref[at, :], w_two[...])
            out_ref[at, :] += mm_nt(grad, w_one[...])
        bias_ref[...] = sums[0] + sums[1]
        scatter_rows(masks, jnp.maximum(step - 1, 0) % n_own, me[0], mm(left_ref[...], grad_ref[...]), held_ref)

    by_parity(step, (even_ref, odd_ref), body)
    split_rows(held_ref, keep_ref, send_ref)

    @pl.when(step == 0)
    def _():
        out_ref[...] = jnp.zeros_like(out_ref)


def feed_call(kernel, masks, me, tables, own_first, own_second, first_part, arrays, outs, scratch):
    count, slots, half, both = tables[0].shape
    model, width = own_first.shape
    n_own = HALVES
    chunk = width // n_own
    n = n_own * (slots + 1)

    def at(j, lag):
        return jnp.clip(j - lag, 0, n - 1)

    def by_head(j, lag, me):
        c = at(j, lag)
        return ((c // n_own) ^ me[1]) * n_own + c % n_own

    def by_half(j, me):
        c = at(j, 1)
        return c % n_own * (slots + 1) + ((c // n_own) ^ me[1])

    def table_spec(part, lag):
        def index(j, me):
            c = jnp.maximum(at(j, lag), n_own)
            return (0, c // n_own - 1, 0, part * n_own + c % n_own)

        return pl.BlockSpec((count, 1, half, chunk), index)

    def own_spec(lag):
        return pl.BlockSpec((model, chunk), lambda j, me: (0, jnp.minimum(at(j, lag), n_own - 1)))

    def spec(array, lag):
        if lag is None:
            return pl.BlockSpec(array.shape, lambda j, me: (0, 0))
        lag, absolute = lag
        return pl.BlockSpec(
            (array.shape[0], chunk), lambda j, me: (0, by_head(j, lag, me) if absolute else at(j, lag))
        )

    rows = arrays[0][0].shape[0]
    weight = jax.ShapeDtypeStruct((n, model // 2, chunk), bf16)
    weight_spec = pl.BlockSpec((1, model // 2, chunk), lambda j, me: (by_half(j, me), 0, 0))
    return pl.pallas_call(
        functools.partial(kernel, masks, n_own, n),
        grid_spec=pltpu.PrefetchScalarGridSpec(
            num_scalar_prefetch=1,
            grid=(n + 1,),
            in_specs=[table_spec(first_part, 0)] * 4
            + [table_spec(1 - first_part, 1)] * 4
            + [own_spec(0), own_spec(1)]
            + [spec(a, lag) for a, lag in arrays],
            out_specs=[spec(o, lag) for o, lag in outs] + [weight_spec, weight_spec],
            scratch_shapes=[
                pltpu.VMEM((model, chunk), bf16),
                pltpu.VMEM((model, chunk), bf16),
                pltpu.VMEM((rows, chunk), f32),
                pltpu.VMEM((rows, chunk), f32),
                pltpu.VMEM((rows, chunk), bf16),
                pltpu.VMEM((model, chunk), bf16),
            ]
            + scratch,
        ),
        out_shape=[o for o, _ in outs] + [weight, weight],
        compiler_params=pltpu.CompilerParams(vmem_limit_bytes=54 << 20),
        cost_estimate=LONG_COST,
    )(me, *tables, *tables, own_first, own_second, *[a for a, _ in arrays])


def far_pick_kernel(limit, where_a, where_b, *refs):
    ins, outs = refs[:8], refs[8:]
    count, half = pl.num_programs(0), ins[0].shape[2]
    for who in range(2):
        for color, where_ref in enumerate((where_a, where_b)):
            held, got = ins[4 * who + 2 * color : 4 * who + 2 * color + 2]
            beyond = where_ref[pl.program_id(0) + who * count] >= limit
            outs[who][0, :, color * half : (color + 1) * half] = jnp.where(beyond, got[0], held[0])


def far_pick(tables, where_a, where_b):
    count = where_a.shape[0] // 2
    limit, _, half = tables[0][0].shape

    def spec(who, color):
        def index(j, wa, wb):
            return ((wa, wb)[color][j + who * count] % limit, 0, 0)

        return pl.BlockSpec((1, BLOCK, half), index)

    out = pl.BlockSpec((1, BLOCK, 2 * half), lambda j, wa, wb: (j, 0, 0))
    shape = jax.ShapeDtypeStruct((count, BLOCK, 2 * half), bf16)
    return pl.pallas_call(
        functools.partial(far_pick_kernel, limit),
        grid_spec=pltpu.PrefetchScalarGridSpec(
            num_scalar_prefetch=2,
            grid=(count,),
            in_specs=[spec(who, color) for who in range(2) for color in range(2) for _ in range(2)],
            out_specs=[out, out],
        ),
        out_shape=[shape, shape],
        compiler_params=pltpu.CompilerParams(vmem_limit_bytes=VMEM_LIMIT),
        cost_estimate=LONG_COST,
    )(where_a, where_b, *[t for _ in range(2) for table in tables for t in table])


def far_route_kernel(count, where_a, where_b, mine_ref, other_ref, *refs):
    outs, acc_ref = refs[:4], refs[4]
    half = outs[0].shape[2]
    acc_ref[...] = jnp.zeros_like(acc_ref)
    for part in range(2):
        step = pl.program_id(0) + part * pl.num_programs(0)
        for source, base in ((mine_ref, 0), (other_ref, count)):
            for j in range(count):

                @pl.when(where_a[base + j] == step)
                def _():
                    acc_ref[part, :, :half] += source[j, :, :half].astype(f32)

                @pl.when(where_b[base + j] == step)
                def _():
                    acc_ref[part, :, half:] += source[j, :, half:].astype(f32)

        outs[part][0] = acc_ref[part, :, :half].astype(bf16)
        outs[2 + part][0] = acc_ref[part, :, half:].astype(bf16)


def far_route(mine, other, where_a, where_b, limit):
    count, _, width = mine.shape
    whole = pl.BlockSpec(mine.shape, lambda k, wa, wb: (0, 0, 0))
    out = pl.BlockSpec((1, BLOCK, width // 2), lambda k, wa, wb: (k, 0, 0))
    shape = jax.ShapeDtypeStruct((limit, BLOCK, width // 2), bf16)
    return pl.pallas_call(
        functools.partial(far_route_kernel, count),
        grid_spec=pltpu.PrefetchScalarGridSpec(
            num_scalar_prefetch=2,
            grid=(limit,),
            in_specs=[whole, whole],
            out_specs=[out] * 4,
            scratch_shapes=[pltpu.VMEM((2, BLOCK, width), f32)],
        ),
        out_shape=[shape] * 4,
        compiler_params=pltpu.CompilerParams(vmem_limit_bytes=18 << 20),
        cost_estimate=LONG_COST,
    )(where_a, where_b, mine, other)


def leave_kernel(n_a, n_b, own_ref, joined_ref, res_ref, coarse_ref, gain_ref, *refs):
    part_a, part_b = refs[:n_a], refs[n_a : n_a + n_b]
    out_ref, up_ref, gain_out, shift_out = refs[n_a + n_b :]

    @pl.when(pl.program_id(0) == 0)
    def _():
        for ref in (up_ref, gain_out, shift_out):
            ref[...] = jnp.zeros_like(ref)

    back = jnp.concatenate(
        [sum(r[0].astype(f32) for r in parts) for parts in (part_a, part_b)], axis=1
    )
    upstream = own_ref[...] + back
    gain = gain_ref[...]
    joined = joined_ref[...]
    _, standard, inverse = norm_forward(joined, gain, gain)
    scaled = upstream * gain
    inner = (
        scaled
        - jnp.mean(scaled, axis=-1, keepdims=True)
        - standard * jnp.mean(scaled * standard, axis=-1, keepdims=True)
    )
    total = res_ref[...] + inner * inverse
    out_ref[...] = total.astype(bf16)
    gain_out[...] += jnp.sum(upstream * standard, axis=0, keepdims=True)
    shift_out[...] += jnp.sum(upstream, axis=0, keepdims=True)
    up_row = lax.broadcasted_iota(jnp.int32, (BLOCK, BLOCK // UP), 0) // UP
    up_col = lax.broadcasted_iota(jnp.int32, (BLOCK, BLOCK // UP), 1)
    weighted = total * mm((up_row == up_col).astype(f32).astype(bf16), coarse_ref[...])
    phase = lax.broadcasted_iota(jnp.int32, weighted.shape, 0) % UP
    for p in range(UP):
        picked = jnp.where(phase == p, weighted, 0.0)
        up_ref[p : p + 1, :] += jnp.sum(picked, axis=0, keepdims=True)


def leave(own, joined, residual, coarse, gain, part_a, part_b):
    tokens, model = own.shape
    rows = pl.BlockSpec((BLOCK, model), lambda b: (b, 0))
    fixed = lambda count: pl.BlockSpec((count, model), lambda b: (0, 0))
    part = pl.BlockSpec((1, BLOCK, model // 2), lambda b: (b, 0, 0))
    return pl.pallas_call(
        functools.partial(leave_kernel, len(part_a), len(part_b)),
        grid=(tokens // BLOCK,),
        in_specs=[rows, rows, rows, pl.BlockSpec((BLOCK // UP, model), lambda b: (b, 0)), fixed(1)]
        + [part] * (len(part_a) + len(part_b)),
        out_specs=[rows, fixed(UP), fixed(1), fixed(1)],
        out_shape=[
            jax.ShapeDtypeStruct((tokens, model), bf16),
            jax.ShapeDtypeStruct((UP, model), f32),
            jax.ShapeDtypeStruct((1, model), f32),
            jax.ShapeDtypeStruct((1, model), f32),
        ],
        compiler_params=pltpu.CompilerParams(vmem_limit_bytes=VMEM_LIMIT),
        cost_estimate=LONG_COST,
    )(own, joined, residual, coarse, gain, *part_a, *part_b)


def relative_masks(masks):
    return [sum(m for bit, m in enumerate(masks) if k >> bit & 1) for k in range(1 << len(masks))]


def assemble_kernel(columns, n_own, n_out, dp_index, *refs):
    tables, own, outs = refs[:4], refs[4 : 4 + n_own], refs[4 + n_own :]
    slots, half = tables[0].shape[1], tables[0].shape[2]

    def fill(first, second):
        for color, table in enumerate((first, second)):
            rows = slice(color * half, (color + 1) * half)
            for c0, width, target, t0 in columns:
                for s in range(slots):
                    at = t0 + (s + 1) * width
                    outs[target][rows, at : at + width] = table[0, s, :, c0 : c0 + width]

    core = pl.program_id(0)

    @pl.when(core == 0)
    def _():
        fill(tables[0], tables[1])

    @pl.when(core == 1)
    def _():
        fill(tables[2], tables[3])

    for ref, (c0, width, target, t0) in zip(own, columns):
        outs[target][:, t0 : t0 + width] = ref[...]


def assemble(dp_index, tables, own, columns, masks, widths):
    bits = len(masks)
    count, slots, half, width = tables[0].shape
    model = 2 * count * 2 * half

    def reverse(k):
        return sum(((k >> i) & 1) << (bits - 1 - i) for i in range(bits))

    def table_spec(which):
        def index(core, k, dp):
            k = jnp.where(core == which // 2, k, 0 if which >= 2 else count - 1)
            return (reverse(k) if which % 2 else k, 0, 0, 0)

        return pl.BlockSpec((1, slots, half, width), index)

    def row(core, k, dp):
        return (dp[0] ^ ((k << 1) | core), 0)

    return pl.pallas_call(
        functools.partial(assemble_kernel, columns, len(own), len(widths)),
        grid_spec=pltpu.PrefetchScalarGridSpec(
            num_scalar_prefetch=1,
            grid=(2, count),
            in_specs=[table_spec(i) for i in range(4)]
            + [pl.BlockSpec((2 * half, o.shape[1]), row) for o in own],
            out_specs=[pl.BlockSpec((2 * half, w), row) for w in widths],
        ),
        out_shape=[jax.ShapeDtypeStruct((model, w), bf16) for w in widths],
        compiler_params=pltpu.CompilerParams(vmem_limit_bytes=16 << 20),
        cost_estimate=LONG_COST,
    )(dp_index, *tables, *own)


def attention_weights_kernel(masks, heads, me, own_t, far_t, branch_t, grad_own, grad_far, attended, *refs):
    keep_ref, send_ref, total_ref, held_ref = refs
    tile = pl.program_id(0)
    kind = tile // heads

    @pl.when(kind == 0)
    def _():
        total_ref[...] = mm(own_t[...], grad_own[...])

    @pl.when((kind == 1) | (kind == 2))
    def _():
        total_ref[...] = mm(own_t[...], grad_own[...]) + mm(far_t[...], grad_far[...])

    @pl.when(kind == 3)
    def _():
        total_ref[...] = mm(branch_t[...], attended[...])

    for color in range(2):

        @pl.when(kind // 2 == color)
        def _():
            scatter_rows(masks, color, me[0], total_ref[...], held_ref)

    split_rows(held_ref, keep_ref, send_ref)


def attention_weights(masks, me, own_t, far_t, branch_t, grad, attended, width):
    model, tokens = own_t.shape
    heads = attended.shape[1] // width
    whole = pl.BlockSpec((model, tokens), lambda j, me: (0, 0))
    part = lambda p: pl.BlockSpec(
        (None, tokens, width), lambda j, me: (p, 0, jnp.minimum(j, 3 * heads - 1))
    )
    out = pl.BlockSpec((1, model // 2, width), lambda j, me: (j, 0, 0))
    shape = jax.ShapeDtypeStruct((4 * heads, model // 2, width), bf16)
    return pl.pallas_call(
        functools.partial(attention_weights_kernel, masks, heads),
        grid_spec=pltpu.PrefetchScalarGridSpec(
            num_scalar_prefetch=1,
            grid=(4 * heads,),
            in_specs=[whole] * 3
            + [
                part(0),
                part(1),
                pl.BlockSpec((tokens, width), lambda j, me: (0, jnp.maximum(j - 3 * heads, 0))),
            ],
            out_specs=[out, out],
            scratch_shapes=[pltpu.VMEM((model, width), f32), pltpu.VMEM((model, width), bf16)],
        ),
        out_shape=[shape, shape],
        compiler_params=pltpu.CompilerParams(vmem_limit_bytes=24 << 20),
        cost_estimate=LONG_COST,
    )(me, own_t, far_t, branch_t, grad, grad, attended)


class DpSum:
    def __init__(self, tie, terms, order):
        self.tie, self.terms, self.order = tie, list(terms), order
        self.rows = terms[0].shape[1]

    def upto(self, low, high):
        first, *others = self.terms
        total = self.tie(first)[:, low:high].astype(f32)
        for value in others:
            total = total + value[:, low:high].astype(f32)
        total = total.astype(bf16)
        self.tie.mark(total)
        return total

    def stage(self, step):
        sent = self.upto(self.rows >> (step + 1), self.rows >> step)
        self.terms.append(xor_swap(sent, "dp", self.order[step]))

    def final(self):
        return self.upto(0, self.rows >> len(self.order))


def local(
    activations,
    conditioning,
    cotangent,
    block_targets,
    up_gain,
    norm1_gain,
    norm1_shift,
    w_qkv,
    b_qv,
    w_out,
    b_out,
    norm2_gain,
    norm2_shift,
    w_fc1,
    b_fc1,
    w_fc2,
    b_fc2,
):
    micro, rows, model = activations.shape
    head_cols = w_qkv.shape[2]
    hidden_cols = w_fc1.shape[1]
    dp_size, head_size = lax.axis_size("dp"), lax.axis_size("head")
    me, here = lax.axis_index("dp"), lax.axis_index("head")
    group = head_size // micro
    tokens = rows * micro
    blocks = tokens // BLOCK
    slab = model // dp_size
    masks = [1 << i for i in range(1, dp_size.bit_length() - 1)]
    heads_all, hidden_all = head_cols * head_size, hidden_cols * head_size

    src_rank = here % micro
    my_micro, my_sub = here // group, here % group
    shifts = [
        [(hs * micro + hr, ((hr + s) % micro) * group + hs) for hs in range(group) for hr in range(micro)]
        for s in range(micro)
    ]

    def send(value, pairs):
        return value if all(a == b for a, b in pairs) else lax.ppermute(value, "head", pairs)

    def choose(options, index):
        out = options[-1]
        for k in range(len(options) - 1):
            out = jnp.where(index == k, options[k], out)
        return out

    def to_micro(value):
        return [
            lax.dynamic_index_in_dim(value, (src_rank + s) % micro, 0, False) for s in range(micro)
        ]

    def sent(pieces, *others):
        pieces = lax.optimization_barrier(tuple(pieces) + others)[: len(pieces)]
        return [send(piece, pairs) for piece, pairs in zip(pieces, shifts)]

    def in_rank_order(got):
        return jnp.concatenate([choose(got, (my_micro - p) % micro) for p in range(micro)], axis=0)

    def from_micro(value):
        pieces = value.reshape(micro, rows, -1)
        return [
            lax.dynamic_index_in_dim(pieces, (my_micro - s) % micro, 0, False) for s in range(micro)
        ]

    def back(pieces):
        return [send(piece, [(b, a) for a, b in pairs]) for piece, pairs in zip(pieces, shifts)]

    def in_micro_order(got):
        return jnp.stack([choose(got, (m - src_rank) % micro) for m in range(micro)])

    def my_slab(value, axis):
        return lax.dynamic_slice_in_dim(value, me * slab, slab, axis)

    tie = Order()
    hc, fc = head_cols, hidden_cols
    half = model // 2

    small = jnp.concatenate([b_qv.reshape(-1), b_fc1])
    per_row = 4 * hc
    small_rows = -(-small.shape[0] // per_row)
    padded = jnp.pad(small, (0, small_rows * per_row - small.shape[0])).reshape(small_rows, per_row)
    thirds, rest = [], padded
    for _ in range(3):
        third = lax.reduce_precision(rest, 8, 7)
        thirds.append(third.astype(bf16))
        rest = rest - third
    extra = jnp.pad(jnp.concatenate(thirds), ((0, 16 - 3 * small_rows), (0, 0)))
    strip_a = jnp.concatenate(
        [my_slab(w_qkv[0], 0), my_slab(w_qkv[1], 0), my_slab(w_qkv[2], 0), my_slab(w_out, 1).T],
        axis=1,
    )
    strip_a = jnp.concatenate([strip_a, extra], axis=0)
    tie.mark(strip_a)
    head_masks = [1 << i for i in range(head_size.bit_length() - 1)]
    head_places = [0]
    for mask in head_masks[::-1]:
        head_places = head_places + [p ^ mask for p in head_places]

    def over_head(strip):
        held = strip[None]
        for mask in head_masks[::-1]:
            held = jnp.concatenate([held, xor_swap(held, "head", mask)], axis=0)
        return [held[head_places.index(s)] for s in range(1, head_size)]

    slots_a = over_head(strip_a)
    strip_f = jnp.concatenate([my_slab(tie(w_fc1), 0), my_slab(w_fc2, 1).T], axis=1)
    own_two_t = tie(w_fc2).T
    own_out_t = tie(w_out).T
    up_tile = jnp.broadcast_to(tie(up_gain)[None], (rows // UP, UP, model)).reshape(rows, model)
    acts_out = to_micro(tie(jnp.concatenate([activations, conditioning], axis=1)))
    cot_out = to_micro(tie(cotangent))
    tie.mark(strip_f, own_two_t, own_out_t, up_tile, *acts_out, *cot_out)
    dp_orders = (masks, masks[::-1])
    dp_index = jnp.stack([me, here]).astype(jnp.int32)

    def colors_of(slots):
        rows_half = slab // 2
        held = [
            jnp.stack([v[c * rows_half : (c + 1) * rows_half] for v in slots])[None] for c in (0, 1)
        ]
        tie.mark(*held)
        return held

    def swap_stage(held, step):
        return [xor_swap(v, "dp", order[step]) for v, order in zip(held, dp_orders)]

    def widen(held, got):
        wider = [jnp.concatenate([a, b], axis=0) for a, b in zip(tie(*held), got)]
        tie.mark(*wider)
        return wider

    held_a = colors_of(tie(*slots_a))
    got_a = swap_stage(held_a, 0)
    got_acts = sent(acts_out, *held_a)
    for step in range(1, len(masks)):
        held_a = widen(held_a, got_a)
        got_a = swap_stage(held_a, step)
    held_a = widen(held_a, got_a)
    tables_a = held_a + [xor_swap(v, "dp", 1) for v in held_a]
    joined, normed, coarse = join(
        my_micro.reshape(1).astype(jnp.int32),
        tie(*got_acts),
        up_tile,
        norm1_gain.reshape(1, -1),
        norm1_shift.reshape(1, -1),
    )
    tie.mark(normed)

    stages_sub = [("head", 1 << i) for i in range(group.bit_length() - 1)]
    stage_lists = [stages_sub + [("dp", m) for m in order] for order in dp_orders]
    stages = len(stage_lists[0])
    shaped = tie(normed).reshape(blocks, BLOCK, model)
    far_held = [shaped[:, :, c * half : (c + 1) * half] for c in (0, 1)]
    tie.mark(*far_held)
    far_got = [xor_swap(v, *stage_lists[c][0]) for c, v in enumerate(far_held)]
    for step in range(1, stages):
        far_held = widen(far_held, far_got)
        far_got = [xor_swap(v, *stage_lists[c][step]) for c, v in enumerate(far_held)]
    limit = far_held[0].shape[0]
    table_row = lax.dynamic_index_in_dim(block_targets, my_micro, 0, False)

    def targets_of(device):
        return lax.dynamic_slice_in_dim(table_row, (device * group + my_sub) * blocks, blocks)

    targets = targets_of(me)
    targets_both = jnp.concatenate([targets, targets_of(me ^ 1)])
    owner = jnp.maximum(targets_both, 0) // blocks
    away = (owner // group) ^ me
    away_sub = (owner % group) ^ my_sub

    def table_index(stage_list):
        index = jnp.zeros_like(owner)
        for bit, (axis, mask) in enumerate(stage_list):
            far_bits = away if axis == "dp" else away_sub
            index = index + (((far_bits & mask) != 0).astype(jnp.int32) << bit)
        return index * blocks + jnp.maximum(targets_both, 0) % blocks

    index_a, index_b = table_index(stage_lists[0]), table_index(stage_lists[1])
    on_my_core = (away & 1) == 0
    has_far = (targets >= 0).astype(jnp.int32)
    valid = on_my_core & (targets_both >= 0)
    route_a = jnp.where(valid, index_a, -1)
    route_b = jnp.where(valid, index_b, -1)

    biases = [small]
    for value in slots_a:
        rows3 = value[slab : slab + 3 * small_rows].astype(f32).reshape(3, -1)
        biases.append(rows3[0] + rows3[1] + rows3[2])
    bias_q = jnp.concatenate([b[:hc] for b in biases])
    bias_v = jnp.concatenate([b[hc : 2 * hc] for b in biases])
    bias_one = jnp.concatenate([b[2 * hc : 2 * hc + fc] for b in biases])
    bias_kv = jnp.concatenate([jnp.zeros_like(bias_v), bias_v])
    w_qkv_all, w_out_t = assemble(
        dp_index,
        list(tie(*tables_a)),
        [w_qkv[0], w_qkv[1], w_qkv[2], own_out_t],
        [(t * hc, hc, 0, t * heads_all) for t in range(3)] + [(3 * hc, hc, 1, 0)],
        masks,
        [3 * heads_all, heads_all],
    )
    tie.mark(w_qkv_all, w_out_t)
    strip_f = tie(strip_f)
    slots_f = over_head(strip_f)
    qkv = (mm(normed, w_qkv_all) + jnp.concatenate([bias_q, bias_kv])).astype(bf16)
    tie.mark(qkv)

    kept, passed = far_pick(list(zip(tie(*far_held), far_got)), index_a, index_b)
    tie.mark(kept, passed)
    passed_got = xor_swap(passed, "dp", 1)
    held_f = colors_of(tie(*slots_f))
    got_f = swap_stage(held_f, 0)
    got_cot = sent(cot_out, passed_got)
    passed = passed_got
    for step in range(1, len(masks)):
        held_f = widen(held_f, got_f)
        got_f = swap_stage(held_f, step)
    far = jnp.where(on_my_core[:blocks, None, None], tie(kept), passed).reshape(tokens, model)
    kv_far = (mm(far, w_qkv_all[:, heads_all:]) + bias_kv).astype(bf16)
    tie.mark(kv_far)
    attended = attention_forward(has_far, qkv, tie(kv_far), heads_all)
    tie.mark(attended, *got_cot[1::2])
    residual = joined + (mm_nt(tie(attended), w_out_t) + b_out)
    normed2_f, standard_two, inverse_two = norm_forward(residual, norm2_gain, norm2_shift)
    normed_two = normed2_f.astype(bf16)
    tie.mark(residual, normed_two)

    incoming = in_rank_order(tie(*got_cot))
    incoming_f = incoming.astype(f32)
    grad_b2 = jnp.sum(incoming_f, axis=0, keepdims=True)
    normed_t, far_t = tie(normed).T, tie(far).T
    incoming_t, normed_two_t = incoming.T, tie(normed_two).T
    tie.mark(grad_b2, normed_t, far_t, incoming_t, normed_two_t)
    held_f = widen(held_f, got_f)
    tables_f = held_f + [xor_swap(v, "dp", 1) for v in held_f]

    shape = jax.ShapeDtypeStruct
    slope, out, keep_two, send_two = feed_call(
        feed_forward_kernel,
        masks,
        dp_index,
        tables_f,
        w_fc1,
        own_two_t,
        0,
        [
            (normed_two, None),
            (bias_one.reshape(1, -1), (0, False)),
            (residual, None),
            (b_fc2.reshape(1, -1), None),
            (incoming_t, None),
        ],
        [(shape((tokens, hidden_all), bf16), (1, False)), (shape((tokens, model), bf16), None)],
        [pltpu.VMEM((tokens, model), f32)],
    )
    tie.mark(slope)
    got_two = xor_swap(send_two, "dp", 1)
    out_pieces = from_micro(tie(out))
    tie.mark(*out_pieces)
    got_out = back(out_pieces)

    reversed_bits = [
        sum(m for m, back_m in zip(head_masks, head_masks[::-1]) if p & back_m) for p in range(head_size)
    ]

    class HeadSum:
        def __init__(self, piece):
            self.held = jnp.stack([piece(here ^ p) for p in reversed_bits])
            tie.mark(self.held)
            self.masks = list(head_masks)
            self.send()

        def send(self):
            half = self.held.shape[0] // 2
            self.got = xor_swap(self.held[half:], "head", self.masks.pop(0))

        def step(self):
            tie.pause()
            half = self.held.shape[0] // 2
            total = tie(self.held)[:half].astype(f32) + self.got.astype(f32)
            if half == 1:
                return total[0]
            self.held = total.astype(bf16)
            tie.mark(self.held)
            self.send()
            return None

        def finish(self):
            out = None
            while out is None:
                out = self.step()
            return out

    grad_b1, grad_normed_two, keep_one, send_one = feed_call(
        feed_backward_kernel,
        masks,
        dp_index,
        tables_f,
        own_two_t,
        w_fc1,
        1,
        [(tie(incoming), None), (slope, (1, False)), (normed_two_t, None)],
        [(shape((1, hidden_all), f32), (1, True)), (shape((tokens, model), f32), None)],
        [],
    )
    tie.mark(grad_b1)
    got_one = xor_swap(send_one, "dp", 1)

    def halves(keep, got):
        return [
            DpSum(tie, [v[c * head_size : (c + 1) * head_size] for v in (keep, got)], dp_orders[c])
            for c in range(HALVES)
        ]

    sums_two = halves(keep_two, got_two)
    for part in sums_two:
        part.stage(0)
    grad_res_part, grad_g2, grad_s2 = norm_backward(
        tie(grad_normed_two), standard_two, inverse_two, norm2_gain
    )
    grad_residual = incoming_f + grad_res_part
    grad_branch = grad_residual.astype(bf16)
    grad_bo = jnp.sum(grad_branch.astype(f32), axis=0)
    grad_att = mm(grad_branch, w_out_t).astype(bf16)
    tie.mark(grad_att)
    grad_qkv = attention_backward(has_far, qkv, kv_far, tie(grad_att))
    tie.mark(grad_qkv, *[part.terms[-1] for part in sums_two], *got_out)
    sums_one = halves(keep_one, got_one)
    far_back = (
        mm_nt(tie(grad_qkv)[1, :, heads_all:], w_qkv_all[:, heads_all:])
        .astype(bf16)
        .reshape(blocks, BLOCK, model)
    )
    tie.mark(far_back)
    far_other = xor_swap(far_back, "dp", 1)
    for part in sums_one:
        part.stage(0)
    tie.mark(*tie.last, far_other)
    for step in range(1, len(masks)):
        for c in range(HALVES):
            pair = (sums_two[c], sums_one[c])
            low, high = pair[0].rows >> (step + 1), pair[0].rows >> step
            moved = jnp.concatenate([part.upto(low, high) for part in pair], axis=0)
            tie.mark(moved)
            moved = xor_swap(moved, "dp", dp_orders[c][step])
            for part, value in zip(pair, (moved[:head_size], moved[head_size:])):
                part.terms.append(value)
    layer_out = in_micro_order(tie(*got_out))
    branch_t = tie(grad_branch).T
    tie.mark(layer_out, branch_t)
    tie.pause()
    routed = far_route(tie(far_back), far_other, route_a, route_b, limit)
    tie.mark(*routed)
    terms = [[routed[0]], [routed[2]]]
    for color in range(2):
        axis, mask = stage_lists[color][-1]
        terms[color].append(xor_swap(routed[2 * color + 1], axis, mask))
    keep_att, send_att = attention_weights(
        masks, dp_index, normed_t, far_t, branch_t, tie(grad_qkv), attended, hc
    )
    tie.mark(send_att)
    got_att = xor_swap(send_att, "dp", 1)
    ends_f = [part.final() for part in sums_two + sums_one]
    sum_f = HeadSum(
        lambda a: jnp.stack([lax.dynamic_index_in_dim(v, a, 0, False) for v in ends_f])
    )
    grad_own = mm_nt(tie(grad_qkv)[0], w_qkv_all)
    grad_bq = jnp.sum(tie(grad_qkv)[0, :, :heads_all].astype(f32), axis=0)
    grad_bv = jnp.sum(tie(grad_qkv)[:, :, 2 * heads_all :].astype(f32), axis=(0, 1))
    tie.mark(grad_own, grad_bq, grad_bv)
    for step in range(stages - 2, -1, -1):
        low, high = blocks << step, blocks << (step + 1)
        moved = []
        tie.pause()
        for color in range(2):
            value = sum(t[low:high].astype(f32) for t in tie(*terms[color]))
            moved.append(value.astype(bf16))
        tie.mark(*moved)
        for color in range(2):
            terms[color].append(xor_swap(moved[color], *stage_lists[color][step]))
    groups = 2 * head_size
    sums_att = [
        DpSum(tie, [v[c * groups : (c + 1) * groups] for v in (keep_att, got_att)], dp_orders[c])
        for c in (0, 1)
    ]
    for part in sums_att:
        part.stage(0)
    tie.pause()
    grad_input, grad_up, grad_g1, grad_s1 = leave(
        tie(grad_own), joined, grad_residual, coarse, norm1_gain.reshape(1, -1), *terms
    )

    by_slot = jnp.concatenate([grad_bq.reshape(-1, hc), grad_bv.reshape(-1, hc)], axis=1)
    by_head = jnp.concatenate(
        [choose([by_slot[s] for s in range(head_size)], a ^ here) for a in range(head_size)]
    )
    total = jnp.concatenate(
        [grad_up, grad_g1, grad_s1]
        + [v.reshape(1, -1) for v in (grad_bo, grad_g2, grad_s2)]
        + [grad_b2, grad_b1.reshape(-1, model), by_head.reshape(-1, model)]
    )
    in_pieces = from_micro(tie(grad_input))
    tie.mark(*in_pieces)
    got_input = back(in_pieces)
    for step in range(1, len(masks)):
        tie.pause()
        for part in sums_att:
            part.stage(step)
    tie.pause()
    ends = [part.final().reshape(2, head_size, slab, hc) for part in sums_att]
    sum_att = HeadSum(
        lambda a: jnp.concatenate(
            [lax.dynamic_index_in_dim(v, a ^ here, 1, False) for v in ends], axis=0
        )
    )
    sum_f.step()
    tie.pause()
    got_input = tie(*got_input)
    grad_input = in_micro_order(got_input).astype(f32)
    grad_coarse = jnp.sum(grad_input.reshape(micro, -1, UP, model) * up_gain, axis=2)
    tie.mark(grad_input, grad_coarse)
    sum_att.step()
    for axis, mask in [("dp", m) for m in [1] + masks] + [("head", m) for m in head_masks]:
        total = tie(total)
        tie.mark(total)
        got = xor_swap(total, axis, mask)
        tie.pause()
        total = tie(total) + got
    grad_wf = sum_f.finish()
    grad_wa = sum_att.finish()
    grad_w2 = jnp.concatenate([grad_wf[c].T for c in range(HALVES)], axis=0)
    grad_w1 = jnp.concatenate([grad_wf[HALVES + c] for c in range(HALVES)], axis=1)
    grad_wqkv, grad_wo = grad_wa[:3], grad_wa[3].T
    s_g1, s_s1, s_bo, s_g2, s_s2, s_b2 = [total[UP + i] for i in range(6)]
    hidden_rows = hidden_all // model
    s_b1 = total[UP + 6 : UP + 6 + hidden_rows].reshape(-1)
    by_head = total[UP + 6 + hidden_rows :].reshape(head_size, 2 * hc)
    s_bq, s_bv = by_head[:, :hc].reshape(-1), by_head[:, hc:].reshape(-1)
    return (
        layer_out,
        grad_input,
        grad_coarse,
        total[:UP],
        s_g1,
        s_s1,
        grad_wqkv,
        jnp.stack([s_bq, s_bv]),
        grad_wo,
        s_bo,
        s_g2,
        s_s2,
        grad_w1,
        s_b1,
        grad_w2,
        s_b2,
    )


def solution(mesh):
    rows = P(None, ("dp", "head"), None)
    return jax.shard_map(
        local,
        mesh=mesh,
        in_specs=(
            rows,
            rows,
            rows,
            P(),
            P(),
            P(),
            P(),
            P(None, None, "head"),
            P(None, "head"),
            P("head", None),
            P(),
            P(),
            P(),
            P(None, "head"),
            P("head"),
            P("head", None),
            P(),
        ),
        out_specs=(
            rows,
            rows,
            rows,
            P(),
            P(),
            P(),
            P(None, "dp", "head"),
            P(),
            P("head", "dp"),
            P(),
            P(),
            P(),
            P("dp", "head"),
            P(),
            P("head", "dp"),
            P(),
        ),
        check_vma=False,
    )
```

```python
import functools
import math

import jax
import jax.numpy as jnp
from jax import lax
from jax.experimental import pallas as pl
from jax.experimental.pallas import tpu as pltpu
from jax.sharding import PartitionSpec as P

HEAD_DIM = 64
BLOCK = 128
UP = 4
HALVES = 2
VMEM_LIMIT = 58 << 20
STEPS = ["tokens_out", "feed", "two_first", "norm", "attention", "wait_two", "far_back", "one_first", "pause", "hidden_rest", "branch", "pause", "route", "weights", "hidden_head", "own", "pause", "far_rest", "att_first", "layer", "pause", "leave", "att_rest", "small", "tokens_back", "pause", "pause", "hidden_step", "att_head", "tokens_end", "pause", "att_step", "small_step", "small_end"]
PAIR = 2 * HEAD_DIM
NEGATIVE = -1e30
epsilon = 1e-05
f32 = jnp.float32
bf16 = jnp.bfloat16
ROOT_2_PI = math.sqrt(2.0 / math.pi)
LONG_COST = pl.CostEstimate(flops=1 << 36, bytes_accessed=1 << 26, transcendentals=0)


def xor_swap(value, axis, mask):
    size = lax.axis_size(axis)
    return lax.ppermute(value, axis, [(i, i ^ mask) for i in range(size)])


def pause_kernel(value_ref, out_ref):
    out_ref[...] = value_ref[...]


class Order:
    def __init__(self):
        self.last = ()
        self.token = None

    def __call__(self, *values):
        tied = lax.optimization_barrier(tuple(values) + self.last)[: len(values)]
        return tied[0] if len(values) == 1 else tied

    def mark(self, *values):
        self.last = values

    def flush(self):
        tied = self(jnp.zeros((8, 128), f32) if self.token is None else self.token)
        self.token = xor_swap(tied, "dp", 1)
        self.mark(self.token)

    def pause(self):
        self.token = self(jnp.zeros((8, 128), f32) if self.token is None else self.token)
        self.token = pl.pallas_call(
            pause_kernel, out_shape=jax.ShapeDtypeStruct((8, 128), f32), cost_estimate=LONG_COST
        )(self.token)
        self.mark(self.token)


def norm_forward(values, gain, shift):
    centered = values - jnp.mean(values, axis=-1, keepdims=True)
    inverse = lax.rsqrt(jnp.mean(centered * centered, axis=-1, keepdims=True) + epsilon)
    standard = centered * inverse
    return (standard * gain + shift, standard, inverse)


def norm_backward(upstream, standard, inverse, gain):
    scaled = upstream * gain
    inner = (
        scaled
        - jnp.mean(scaled, axis=-1, keepdims=True)
        - standard * jnp.mean(scaled * standard, axis=-1, keepdims=True)
    )
    return (inner * inverse, jnp.sum(upstream * standard, axis=0), jnp.sum(upstream, axis=0))


def mm(left, right):
    return jnp.dot(left, right, preferred_element_type=f32)


def mm_nt(left, right):
    return lax.dot_general(left, right, (((1,), (1,)), ((), ())), preferred_element_type=f32)


def mm_tn(left, right):
    return lax.dot_general(left, right, (((0,), (0,)), ((), ())), preferred_element_type=f32)


def pair_probs(q_pair, k_cat, allowed):
    low_half = lax.broadcasted_iota(jnp.int32, (BLOCK, PAIR), 1) < HEAD_DIM
    zero = jnp.zeros_like(q_pair)
    q_stack = jnp.concatenate(
        [jnp.where(low_half, q_pair, zero), jnp.where(low_half, zero, q_pair)], axis=0
    )
    scores = mm_nt(k_cat, q_stack) * (1.0 / math.sqrt(HEAD_DIM))
    scores = jnp.where(allowed, scores, NEGATIVE)
    top = jnp.max(scores, axis=0, keepdims=True)
    raised = jnp.exp(scores - top)
    probs = raised * (1.0 / jnp.sum(raised, axis=0, keepdims=True))
    return q_stack, probs, low_half


def allowed_mask(far_flag):
    key_at = lax.broadcasted_iota(jnp.int32, (2 * BLOCK, 2 * BLOCK), 0)
    query_at = lax.broadcasted_iota(jnp.int32, (2 * BLOCK, 2 * BLOCK), 1)
    query_at = jnp.where(query_at >= BLOCK, query_at - BLOCK, query_at)
    first = jnp.where(far_flag > 0, BLOCK, 2 * BLOCK)
    return (key_at <= query_at) | (key_at >= first)


def pair_columns(p, width):
    return [slice(t * width + p * PAIR, t * width + (p + 1) * PAIR) for t in range(3)]


def key_value(own_ref, far_ref, columns, width):
    out = []
    for cols in columns[1:]:
        far_cols = slice(cols.start - width, cols.stop - width)
        out.append(jnp.concatenate([own_ref[:, cols], far_ref[:, far_cols]], axis=0))
    return out


def attention_forward_kernel(pairs, has_far, own_ref, far_ref, out_ref):
    allowed = allowed_mask(has_far[pl.program_id(0)])
    width = pairs * PAIR
    for p in range(pairs):
        columns = pair_columns(p, width)
        k_cat, v_cat = key_value(own_ref, far_ref, columns, width)
        _, probs, low_half = pair_probs(own_ref[:, columns[0]], k_cat, allowed)
        mixed = mm_tn(probs.astype(bf16), v_cat)
        out_ref[:, columns[0]] = jnp.where(low_half, mixed[:BLOCK], mixed[BLOCK:]).astype(bf16)


def attention_forward(has_far, own, far, width):
    blocks = has_far.shape[0]
    row_block = lambda array: pl.BlockSpec((BLOCK, array.shape[1]), lambda b, flags: (b, 0))
    shape = jax.ShapeDtypeStruct((blocks * BLOCK, width), bf16)
    return pl.pallas_call(
        functools.partial(attention_forward_kernel, width // PAIR),
        grid_spec=pltpu.PrefetchScalarGridSpec(
            num_scalar_prefetch=1,
            grid=(blocks,),
            in_specs=[row_block(own), row_block(far)],
            out_specs=row_block(shape),
        ),
        out_shape=shape,
        compiler_params=pltpu.CompilerParams(vmem_limit_bytes=16 << 20),
        cost_estimate=LONG_COST,
    )(has_far, own, far)


def attention_backward_kernel(pairs, has_far, own_ref, far_ref, grad_ref, out_ref):
    allowed = allowed_mask(has_far[pl.program_id(0)])
    width = pairs * PAIR
    scale = 1.0 / math.sqrt(HEAD_DIM)
    out_ref[1, :, :width] = jnp.zeros((BLOCK, width), bf16)
    for p in range(pairs):
        columns = pair_columns(p, width)
        k_cat, v_cat = key_value(own_ref, far_ref, columns, width)
        q_stack, probs, low_half = pair_probs(own_ref[:, columns[0]], k_cat, allowed)
        grad = grad_ref[:, columns[0]]
        zero = jnp.zeros_like(grad)
        grad_stack = jnp.concatenate(
            [jnp.where(low_half, grad, zero), jnp.where(low_half, zero, grad)], axis=0
        )
        grad_probs = mm_nt(v_cat, grad_stack)
        total = jnp.sum(probs * grad_probs, axis=0, keepdims=True)
        grad_scores = (probs * (grad_probs - total)).astype(bf16)
        dq = mm_tn(grad_scores, k_cat) * scale
        out_ref[0, :, columns[0]] = jnp.where(low_half, dq[:BLOCK], dq[BLOCK:]).astype(bf16)
        dk = (mm(grad_scores, q_stack) * scale).astype(bf16)
        dv = mm(probs.astype(bf16), grad_stack).astype(bf16)
        for half in range(2):
            rows = slice(half * BLOCK, (half + 1) * BLOCK)
            out_ref[half, :, columns[1]] = dk[rows]
            out_ref[half, :, columns[2]] = dv[rows]


def attention_backward(has_far, own, far, grad):
    blocks, width = has_far.shape[0], grad.shape[1]
    row_block = lambda array: pl.BlockSpec((BLOCK, array.shape[1]), lambda b, flags: (b, 0))
    return pl.pallas_call(
        functools.partial(attention_backward_kernel, width // PAIR),
        grid_spec=pltpu.PrefetchScalarGridSpec(
            num_scalar_prefetch=1,
            grid=(blocks,),
            in_specs=[row_block(own), row_block(far), row_block(grad)],
            out_specs=pl.BlockSpec((2, BLOCK, 3 * width), lambda b, flags: (0, b, 0)),
        ),
        out_shape=jax.ShapeDtypeStruct((2, blocks * BLOCK, 3 * width), bf16),
        compiler_params=pltpu.CompilerParams(vmem_limit_bytes=20 << 20),
        cost_estimate=LONG_COST,
    )(has_far, own, far, grad)


def join_kernel(rows, first, *refs):
    got, (tile_ref, gain_ref, shift_ref, joined_ref, normed_ref, coarse_ref, held_ref) = (
        refs[:-7],
        refs[-7:],
    )
    pieces = len(got)
    which = (first[0] + pieces - pl.program_id(0)) % pieces
    for s in range(pieces):

        @pl.when(which == s)
        def _():
            held_ref[...] = got[s][...]

    coarse = held_ref[rows:, :]
    coarse_ref[...] = coarse
    up_row = lax.broadcasted_iota(jnp.int32, (rows, rows // UP), 0) // UP
    up_col = lax.broadcasted_iota(jnp.int32, (rows, rows // UP), 1)
    spread = mm((up_row == up_col).astype(f32).astype(bf16), coarse)
    joined = held_ref[:rows, :].astype(f32) + spread * tile_ref[...]
    joined_ref[...] = joined
    normed_ref[...] = norm_forward(joined, gain_ref[...], shift_ref[...])[0].astype(bf16)


def join(first, got, tile, gain, shift):
    pieces, rows, model = len(got), tile.shape[0], tile.shape[1]
    small = rows // UP
    fixed = lambda array: pl.BlockSpec(array.shape, lambda p, f: (0, 0))
    piece = lambda count: pl.BlockSpec((count, model), lambda p, f: (p, 0))
    return pl.pallas_call(
        functools.partial(join_kernel, rows),
        grid_spec=pltpu.PrefetchScalarGridSpec(
            num_scalar_prefetch=1,
            grid=(pieces,),
            in_specs=[fixed(g) for g in got] + [fixed(tile), fixed(gain), fixed(shift)],
            out_specs=[piece(rows), piece(rows), piece(small)],
            scratch_shapes=[pltpu.VMEM((rows + small, model), bf16)],
        ),
        out_shape=[
            jax.ShapeDtypeStruct((pieces * rows, model), f32),
            jax.ShapeDtypeStruct((pieces * rows, model), bf16),
            jax.ShapeDtypeStruct((pieces * small, model), bf16),
        ],
        compiler_params=pltpu.CompilerParams(vmem_limit_bytes=16 << 20),
        cost_estimate=LONG_COST,
    )(first, *got, tile, gain, shift)


def fill_chunk(masks, me, tables, out_ref):
    half, count = tables[0].shape[2], tables[0].shape[0]
    for which, table in enumerate(tables):
        core, color, late = which // 4, which // 2 % 2, which % 2
        order = masks if color == 0 else masks[::-1]
        for k, mask in enumerate(relative_masks(order)[late * count : (late + 1) * count]):
            row = (me ^ (mask | core)) * 2 * half + color * half
            out_ref[pl.ds(pl.multiple_of(row, half), half), :] = table[k, 0]


def load_chunk(masks, me, chunk, n_own, own_ref, tables, out_ref):
    @pl.when(chunk < n_own)
    def _():
        out_ref[...] = own_ref[...]

    @pl.when(chunk >= n_own)
    def _():
        fill_chunk(masks, me, tables, out_ref)


def by_parity(step, buffers, body):
    for parity in range(2):

        @pl.when(step % 2 == parity)
        def _():
            body(buffers[1 - parity], buffers[parity])


def scatter_rows(masks, color, me, value, held_ref):
    count = 2 << len(masks)
    slab = value.shape[0] // count
    last = len(masks) - 1
    for b in range(count):
        away = me ^ b
        at = (away & 1) << len(masks)
        for i, mask in enumerate(masks):
            place = last - i if isinstance(color, int) and color == 0 else i
            if not isinstance(color, int):
                place = jnp.where(color == 0, last - i, i)
            at = at + (((away >> (mask.bit_length() - 1)) & 1) << place)
        row = pl.multiple_of(at * slab, slab)
        held_ref[pl.ds(row, slab), :] = value[b * slab : (b + 1) * slab].astype(bf16)


def split_rows(held_ref, keep_ref, send_ref):
    half = held_ref.shape[0] // 2
    keep_ref[0] = held_ref[:half, :]
    send_ref[0] = held_ref[half:, :]


def feed_forward_kernel(masks, n_own, n, me, *refs):
    one_tables, two_tables, refs = refs[:8], refs[8:16], refs[16:]
    (own_one, own_two, x_ref, bias_ref, residual_ref, last_ref, left_ref) = refs[:7]
    slope_ref, out_ref, keep_ref, send_ref = refs[7:11]
    w_one, w_two, even_ref, odd_ref, act_ref, held_ref, acc_ref = refs[11:]
    step = pl.program_id(0)
    load_chunk(masks, me[0], jnp.minimum(step, n - 1), n_own, own_one, one_tables, w_one)
    load_chunk(masks, me[0], jnp.maximum(step - 1, 0), n_own, own_two, two_tables, w_two)
    ratio = ROOT_2_PI * 0.044715
    rows = x_ref.shape[0] // 2

    def body(before, now):
        for r in range(2):
            at = slice(r * rows, (r + 1) * rows)
            h = before[at, :]
            square = h * h
            gate = 0.5 + 0.5 * jnp.tanh(h * (ROOT_2_PI + ratio * square))
            act = (h * gate).astype(bf16)
            act_ref[at, :] = act
            slope_ref[at, :] = (
                gate * (1.0 + 2.0 * h * (1.0 - gate) * (ROOT_2_PI + 3.0 * ratio * square))
            ).astype(bf16)
            now[at, :] = mm(x_ref[at, :], w_one[...]) + bias_ref[...]
            acc_ref[at, :] += mm_nt(act, w_two[...])
        scatter_rows(masks, jnp.maximum(step - 1, 0) % n_own, me[0], mm(left_ref[...], act_ref[...]), held_ref)

    by_parity(step, (even_ref, odd_ref), body)
    split_rows(held_ref, keep_ref, send_ref)

    @pl.when(step == 0)
    def _():
        acc_ref[...] = jnp.zeros_like(acc_ref)

    @pl.when(step == n)
    def _():
        out_ref[...] = (residual_ref[...] + (acc_ref[...] + last_ref[...])).astype(bf16)


def feed_backward_kernel(masks, n_own, n, me, *refs):
    two_tables, one_tables, refs = refs[:8], refs[8:16], refs[16:]
    own_two, own_one, g_ref, slope_ref, left_ref = refs[:5]
    bias_ref, out_ref, keep_ref, send_ref = refs[5:9]
    w_two, w_one, even_ref, odd_ref, grad_ref, held_ref = refs[9:]
    step = pl.program_id(0)
    load_chunk(masks, me[0], jnp.minimum(step, n - 1), n_own, own_two, two_tables, w_two)
    load_chunk(masks, me[0], jnp.maximum(step - 1, 0), n_own, own_one, one_tables, w_one)
    rows = g_ref.shape[0] // 2

    def body(before, now):
        sums = []
        for r in range(2):
            at = slice(r * rows, (r + 1) * rows)
            grad = (before[at, :] * slope_ref[at, :].astype(f32)).astype(bf16)
            grad_ref[at, :] = grad
            sums.append(jnp.sum(grad.astype(f32), axis=0, keepdims=True))
            now[at, :] = mm(g_ref[at, :], w_two[...])
            out_ref[at, :] += mm_nt(grad, w_one[...])
        bias_ref[...] = sums[0] + sums[1]
        scatter_rows(masks, jnp.maximum(step - 1, 0) % n_own, me[0], mm(left_ref[...], grad_ref[...]), held_ref)

    by_parity(step, (even_ref, odd_ref), body)
    split_rows(held_ref, keep_ref, send_ref)

    @pl.when(step == 0)
    def _():
        out_ref[...] = jnp.zeros_like(out_ref)


def feed_call(kernel, masks, me, tables, own_first, own_second, first_part, arrays, outs, scratch):
    count, slots, half, both = tables[0].shape
    model, width = own_first.shape
    n_own = HALVES
    chunk = width // n_own
    n = n_own * (slots + 1)

    def at(j, lag):
        return jnp.clip(j - lag, 0, n - 1)

    def by_head(j, lag, me):
        c = at(j, lag)
        return ((c // n_own) ^ me[1]) * n_own + c % n_own

    def by_half(j, me):
        c = at(j, 1)
        return c % n_own * (slots + 1) + ((c // n_own) ^ me[1])

    def table_spec(part, lag):
        def index(j, me):
            c = jnp.maximum(at(j, lag), n_own)
            return (0, c // n_own - 1, 0, part * n_own + c % n_own)

        return pl.BlockSpec((count, 1, half, chunk), index)

    def own_spec(lag):
        return pl.BlockSpec((model, chunk), lambda j, me: (0, jnp.minimum(at(j, lag), n_own - 1)))

    def spec(array, lag):
        if lag is None:
            return pl.BlockSpec(array.shape, lambda j, me: (0, 0))
        lag, absolute = lag
        return pl.BlockSpec(
            (array.shape[0], chunk), lambda j, me: (0, by_head(j, lag, me) if absolute else at(j, lag))
        )

    rows = arrays[0][0].shape[0]
    weight = jax.ShapeDtypeStruct((n, model // 2, chunk), bf16)
    weight_spec = pl.BlockSpec((1, model // 2, chunk), lambda j, me: (by_half(j, me), 0, 0))
    return pl.pallas_call(
        functools.partial(kernel, masks, n_own, n),
        grid_spec=pltpu.PrefetchScalarGridSpec(
            num_scalar_prefetch=1,
            grid=(n + 1,),
            in_specs=[table_spec(first_part, 0)] * 8
            + [table_spec(1 - first_part, 1)] * 8
            + [own_spec(0), own_spec(1)]
            + [spec(a, lag) for a, lag in arrays],
            out_specs=[spec(o, lag) for o, lag in outs] + [weight_spec, weight_spec],
            scratch_shapes=[
                pltpu.VMEM((model, chunk), bf16),
                pltpu.VMEM((model, chunk), bf16),
                pltpu.VMEM((rows, chunk), f32),
                pltpu.VMEM((rows, chunk), f32),
                pltpu.VMEM((rows, chunk), bf16),
                pltpu.VMEM((model, chunk), bf16),
            ]
            + scratch,
        ),
        out_shape=[o for o, _ in outs] + [weight, weight],
        compiler_params=pltpu.CompilerParams(vmem_limit_bytes=54 << 20),
        cost_estimate=LONG_COST,
    )(me, *tables, *tables, own_first, own_second, *[a for a, _ in arrays])


def far_pick_kernel(limit, where_a, where_b, *refs):
    ins, outs = refs[:8], refs[8:]
    count, half = pl.num_programs(0), ins[0].shape[2]
    for who in range(2):
        for color, where_ref in enumerate((where_a, where_b)):
            held, got = ins[4 * who + 2 * color : 4 * who + 2 * color + 2]
            beyond = where_ref[pl.program_id(0) + who * count] >= limit
            outs[who][0, :, color * half : (color + 1) * half] = jnp.where(beyond, got[0], held[0])


def far_pick(tables, where_a, where_b):
    count = where_a.shape[0] // 2
    limit, _, half = tables[0][0].shape

    def spec(who, color):
        def index(j, wa, wb):
            return ((wa, wb)[color][j + who * count] % limit, 0, 0)

        return pl.BlockSpec((1, BLOCK, half), index)

    out = pl.BlockSpec((1, BLOCK, 2 * half), lambda j, wa, wb: (j, 0, 0))
    shape = jax.ShapeDtypeStruct((count, BLOCK, 2 * half), bf16)
    return pl.pallas_call(
        functools.partial(far_pick_kernel, limit),
        grid_spec=pltpu.PrefetchScalarGridSpec(
            num_scalar_prefetch=2,
            grid=(count,),
            in_specs=[spec(who, color) for who in range(2) for color in range(2) for _ in range(2)],
            out_specs=[out, out],
        ),
        out_shape=[shape, shape],
        compiler_params=pltpu.CompilerParams(vmem_limit_bytes=VMEM_LIMIT),
        cost_estimate=LONG_COST,
    )(where_a, where_b, *[t for _ in range(2) for table in tables for t in table])


def far_route_kernel(count, where_a, where_b, mine_ref, other_ref, *refs):
    outs, acc_ref = refs[:4], refs[4]
    half = outs[0].shape[2]
    acc_ref[...] = jnp.zeros_like(acc_ref)
    for part in range(2):
        step = pl.program_id(0) + part * pl.num_programs(0)
        for source, base in ((mine_ref, 0), (other_ref, count)):
            for j in range(count):

                @pl.when(where_a[base + j] == step)
                def _():
                    acc_ref[part, :, :half] += source[j, :, :half].astype(f32)

                @pl.when(where_b[base + j] == step)
                def _():
                    acc_ref[part, :, half:] += source[j, :, half:].astype(f32)

        outs[part][0] = acc_ref[part, :, :half].astype(bf16)
        outs[2 + part][0] = acc_ref[part, :, half:].astype(bf16)


def far_route(mine, other, where_a, where_b, limit):
    count, _, width = mine.shape
    whole = pl.BlockSpec(mine.shape, lambda k, wa, wb: (0, 0, 0))
    out = pl.BlockSpec((1, BLOCK, width // 2), lambda k, wa, wb: (k, 0, 0))
    shape = jax.ShapeDtypeStruct((limit, BLOCK, width // 2), bf16)
    return pl.pallas_call(
        functools.partial(far_route_kernel, count),
        grid_spec=pltpu.PrefetchScalarGridSpec(
            num_scalar_prefetch=2,
            grid=(limit,),
            in_specs=[whole, whole],
            out_specs=[out] * 4,
            scratch_shapes=[pltpu.VMEM((2, BLOCK, width), f32)],
        ),
        out_shape=[shape] * 4,
        compiler_params=pltpu.CompilerParams(vmem_limit_bytes=18 << 20),
        cost_estimate=LONG_COST,
    )(where_a, where_b, mine, other)


def leave_kernel(n_a, n_b, own_ref, joined_ref, res_ref, coarse_ref, gain_ref, *refs):
    part_a, part_b = refs[:n_a], refs[n_a : n_a + n_b]
    out_ref, up_ref, gain_out, shift_out = refs[n_a + n_b :]

    @pl.when(pl.program_id(0) == 0)
    def _():
        for ref in (up_ref, gain_out, shift_out):
            ref[...] = jnp.zeros_like(ref)

    back = jnp.concatenate(
        [sum(r[0].astype(f32) for r in parts) for parts in (part_a, part_b)], axis=1
    )
    upstream = own_ref[...] + back
    gain = gain_ref[...]
    joined = joined_ref[...]
    _, standard, inverse = norm_forward(joined, gain, gain)
    scaled = upstream * gain
    inner = (
        scaled
        - jnp.mean(scaled, axis=-1, keepdims=True)
        - standard * jnp.mean(scaled * standard, axis=-1, keepdims=True)
    )
    total = res_ref[...] + inner * inverse
    out_ref[...] = total.astype(bf16)
    gain_out[...] += jnp.sum(upstream * standard, axis=0, keepdims=True)
    shift_out[...] += jnp.sum(upstream, axis=0, keepdims=True)
    up_row = lax.broadcasted_iota(jnp.int32, (BLOCK, BLOCK // UP), 0) // UP
    up_col = lax.broadcasted_iota(jnp.int32, (BLOCK, BLOCK // UP), 1)
    weighted = total * mm((up_row == up_col).astype(f32).astype(bf16), coarse_ref[...])
    phase = lax.broadcasted_iota(jnp.int32, weighted.shape, 0) % UP
    for p in range(UP):
        picked = jnp.where(phase == p, weighted, 0.0)
        up_ref[p : p + 1, :] += jnp.sum(picked, axis=0, keepdims=True)


def leave(own, joined, residual, coarse, gain, part_a, part_b):
    tokens, model = own.shape
    rows = pl.BlockSpec((BLOCK, model), lambda b: (b, 0))
    fixed = lambda count: pl.BlockSpec((count, model), lambda b: (0, 0))
    part = pl.BlockSpec((1, BLOCK, model // 2), lambda b: (b, 0, 0))
    return pl.pallas_call(
        functools.partial(leave_kernel, len(part_a), len(part_b)),
        grid=(tokens // BLOCK,),
        in_specs=[rows, rows, rows, pl.BlockSpec((BLOCK // UP, model), lambda b: (b, 0)), fixed(1)]
        + [part] * (len(part_a) + len(part_b)),
        out_specs=[rows, fixed(UP), fixed(1), fixed(1)],
        out_shape=[
            jax.ShapeDtypeStruct((tokens, model), bf16),
            jax.ShapeDtypeStruct((UP, model), f32),
            jax.ShapeDtypeStruct((1, model), f32),
            jax.ShapeDtypeStruct((1, model), f32),
        ],
        compiler_params=pltpu.CompilerParams(vmem_limit_bytes=VMEM_LIMIT),
        cost_estimate=LONG_COST,
    )(own, joined, residual, coarse, gain, *part_a, *part_b)


def relative_masks(masks):
    return [sum(m for bit, m in enumerate(masks) if k >> bit & 1) for k in range(1 << len(masks))]


def assemble_kernel(columns, n_own, n_out, dp_index, *refs):
    tables, own, outs = refs[:4], refs[4 : 4 + n_own], refs[4 + n_own :]
    slots, half = tables[0].shape[1], tables[0].shape[2]

    def fill(first, second):
        for color, table in enumerate((first, second)):
            rows = slice(color * half, (color + 1) * half)
            for c0, width, target, t0 in columns:
                for s in range(slots):
                    at = t0 + (s + 1) * width
                    outs[target][rows, at : at + width] = table[0, s, :, c0 : c0 + width]

    core = pl.program_id(0)

    @pl.when(core == 0)
    def _():
        fill(tables[0], tables[1])

    @pl.when(core == 1)
    def _():
        fill(tables[2], tables[3])

    for ref, (c0, width, target, t0) in zip(own, columns):
        outs[target][:, t0 : t0 + width] = ref[...]


def assemble(dp_index, tables, own, columns, masks, widths):
    bits = len(masks)
    count, slots, half, width = tables[0].shape
    model = 2 * count * 2 * half

    def reverse(k):
        return sum(((k >> i) & 1) << (bits - 1 - i) for i in range(bits))

    def table_spec(which):
        def index(core, k, dp):
            k = jnp.where(core == which // 2, k, 0 if which >= 2 else count - 1)
            return (reverse(k) if which % 2 else k, 0, 0, 0)

        return pl.BlockSpec((1, slots, half, width), index)

    def row(core, k, dp):
        return (dp[0] ^ ((k << 1) | core), 0)

    return pl.pallas_call(
        functools.partial(assemble_kernel, columns, len(own), len(widths)),
        grid_spec=pltpu.PrefetchScalarGridSpec(
            num_scalar_prefetch=1,
            grid=(2, count),
            in_specs=[table_spec(i) for i in range(4)]
            + [pl.BlockSpec((2 * half, o.shape[1]), row) for o in own],
            out_specs=[pl.BlockSpec((2 * half, w), row) for w in widths],
        ),
        out_shape=[jax.ShapeDtypeStruct((model, w), bf16) for w in widths],
        compiler_params=pltpu.CompilerParams(vmem_limit_bytes=16 << 20),
        cost_estimate=LONG_COST,
    )(dp_index, *tables, *own)


def attention_weights_kernel(masks, heads, me, own_t, far_t, branch_t, grad_own, grad_far, attended, *refs):
    keep_ref, send_ref, total_ref, held_ref = refs
    tile = pl.program_id(0)
    kind = tile // heads

    @pl.when(kind == 0)
    def _():
        total_ref[...] = mm(own_t[...], grad_own[...])

    @pl.when((kind == 1) | (kind == 2))
    def _():
        total_ref[...] = mm(own_t[...], grad_own[...]) + mm(far_t[...], grad_far[...])

    @pl.when(kind == 3)
    def _():
        total_ref[...] = mm(branch_t[...], attended[...])

    for color in range(2):

        @pl.when(kind // 2 == color)
        def _():
            scatter_rows(masks, color, me[0], total_ref[...], held_ref)

    split_rows(held_ref, keep_ref, send_ref)


def attention_weights(masks, me, own_t, far_t, branch_t, grad, attended, width):
    model, tokens = own_t.shape
    heads = attended.shape[1] // width
    whole = pl.BlockSpec((model, tokens), lambda j, me: (0, 0))
    part = lambda p: pl.BlockSpec(
        (None, tokens, width), lambda j, me: (p, 0, jnp.minimum(j, 3 * heads - 1))
    )
    out = pl.BlockSpec((1, model // 2, width), lambda j, me: (j, 0, 0))
    shape = jax.ShapeDtypeStruct((4 * heads, model // 2, width), bf16)
    return pl.pallas_call(
        functools.partial(attention_weights_kernel, masks, heads),
        grid_spec=pltpu.PrefetchScalarGridSpec(
            num_scalar_prefetch=1,
            grid=(4 * heads,),
            in_specs=[whole] * 3
            + [
                part(0),
                part(1),
                pl.BlockSpec((tokens, width), lambda j, me: (0, jnp.maximum(j - 3 * heads, 0))),
            ],
            out_specs=[out, out],
            scratch_shapes=[pltpu.VMEM((model, width), f32), pltpu.VMEM((model, width), bf16)],
        ),
        out_shape=[shape, shape],
        compiler_params=pltpu.CompilerParams(vmem_limit_bytes=24 << 20),
        cost_estimate=LONG_COST,
    )(me, own_t, far_t, branch_t, grad, grad, attended)


class DpSum:
    def __init__(self, tie, terms, order, group, count):
        self.tie, self.order = tie, order
        self.terms = [(value, group) for value in terms]
        self.count, self.rows = count, terms[0].shape[1]

    def upto(self, low, high):
        values = self.tie(*[value for value, _ in self.terms])
        total = 0.0
        for value, (_, group) in zip(values, self.terms):
            total = total + value[group : group + self.count, low:high].astype(f32)
        total = total.astype(bf16)
        self.tie.mark(total)
        return total

    def stage(self, step):
        sent = self.upto(self.rows >> (step + 1), self.rows >> step)
        self.terms.append((xor_swap(sent, "dp", self.order[step]), 0))

    def final(self):
        return self.upto(0, self.rows >> len(self.order))


def local(
    activations,
    conditioning,
    cotangent,
    block_targets,
    up_gain,
    norm1_gain,
    norm1_shift,
    w_qkv,
    b_qv,
    w_out,
    b_out,
    norm2_gain,
    norm2_shift,
    w_fc1,
    b_fc1,
    w_fc2,
    b_fc2,
):
    micro, rows, model = activations.shape
    head_cols = w_qkv.shape[2]
    hidden_cols = w_fc1.shape[1]
    dp_size, head_size = lax.axis_size("dp"), lax.axis_size("head")
    me, here = lax.axis_index("dp"), lax.axis_index("head")
    group = head_size // micro
    tokens = rows * micro
    blocks = tokens // BLOCK
    slab = model // dp_size
    masks = [1 << i for i in range(1, dp_size.bit_length() - 1)]
    heads_all, hidden_all = head_cols * head_size, hidden_cols * head_size

    src_rank = here % micro
    my_micro, my_sub = here // group, here % group
    shifts = [
        [(hs * micro + hr, ((hr + s) % micro) * group + hs) for hs in range(group) for hr in range(micro)]
        for s in range(micro)
    ]

    def send(value, pairs):
        return value if all(a == b for a, b in pairs) else lax.ppermute(value, "head", pairs)

    def choose(options, index):
        out = options[-1]
        for k in range(len(options) - 1):
            out = jnp.where(index == k, options[k], out)
        return out

    def to_micro(value):
        return [
            lax.dynamic_index_in_dim(value, (src_rank + s) % micro, 0, False) for s in range(micro)
        ]

    def sent(pieces, *others):
        pieces = lax.optimization_barrier(tuple(pieces) + others)[: len(pieces)]
        return [send(piece, pairs) for piece, pairs in zip(pieces, shifts)]

    def in_rank_order(got):
        return jnp.concatenate([choose(got, (my_micro - p) % micro) for p in range(micro)], axis=0)

    def from_micro(value):
        pieces = value.reshape(micro, rows, -1)
        return [
            lax.dynamic_index_in_dim(pieces, (my_micro - s) % micro, 0, False) for s in range(micro)
        ]

    def back(pieces):
        return [send(piece, [(b, a) for a, b in pairs]) for piece, pairs in zip(pieces, shifts)]

    def in_micro_order(got):
        return jnp.stack([choose(got, (m - src_rank) % micro) for m in range(micro)])

    def my_slab(value, axis):
        return lax.dynamic_slice_in_dim(value, me * slab, slab, axis)

    tie = Order()
    hc, fc = head_cols, hidden_cols
    half = model // 2

    small = jnp.concatenate([b_qv.reshape(-1), b_fc1])
    per_row = 4 * hc
    small_rows = -(-small.shape[0] // per_row)
    padded = jnp.pad(small, (0, small_rows * per_row - small.shape[0])).reshape(small_rows, per_row)
    thirds, rest = [], padded
    for _ in range(3):
        third = lax.reduce_precision(rest, 8, 7)
        thirds.append(third.astype(bf16))
        rest = rest - third
    extra = jnp.pad(jnp.concatenate(thirds), ((0, 16 - 3 * small_rows), (0, 0)))
    strip_a = jnp.concatenate(
        [my_slab(w_qkv[0], 0), my_slab(w_qkv[1], 0), my_slab(w_qkv[2], 0), my_slab(w_out, 1).T],
        axis=1,
    )
    strip_a = jnp.concatenate([strip_a, extra], axis=0)
    tie.mark(strip_a)
    head_masks = [1 << i for i in range(head_size.bit_length() - 1)]
    head_places = [0]
    for mask in head_masks[::-1]:
        head_places = head_places + [p ^ mask for p in head_places]

    class HeadGather:
        def __init__(self, strip):
            self.held, self.masks = strip[None], head_masks[::-1]
            self.send()

        def send(self):
            self.got = xor_swap(self.held, "head", self.masks.pop(0))

        def step(self):
            self.held = jnp.concatenate([tie(self.held), self.got], axis=0)
            tie.mark(self.held)
            if self.masks:
                self.send()
                return True
            return False

        def slots(self):
            while self.step():
                tie.pause()
            return [self.held[head_places.index(s)] for s in range(1, head_size)]

    gather_a = HeadGather(strip_a)
    acts_out = to_micro(tie(jnp.concatenate([activations, conditioning], axis=1)))
    tie.mark(*acts_out)
    tie.pause()
    gather_a.step()
    strip_f = jnp.concatenate([my_slab(tie(w_fc1), 0), my_slab(w_fc2, 1).T], axis=1)
    own_two_t = tie(w_fc2).T
    own_out_t = tie(w_out).T
    up_tile = jnp.broadcast_to(tie(up_gain)[None], (rows // UP, UP, model)).reshape(rows, model)
    cot_out = to_micro(tie(cotangent))
    tie.mark(strip_f, own_two_t, own_out_t, up_tile, *cot_out)
    tie.pause()
    slots_a = gather_a.slots()
    dp_orders = (masks, masks[::-1])
    dp_index = jnp.stack([me, here]).astype(jnp.int32)

    def colors_of(slots):
        rows_half = slab // 2
        held = [
            jnp.stack([v[c * rows_half : (c + 1) * rows_half] for v in slots])[None] for c in (0, 1)
        ]
        tie.mark(*held)
        return held

    def swap_stage(held, step):
        return [xor_swap(v, "dp", order[step]) for v, order in zip(held, dp_orders)]

    def widen(held, got):
        wider = [jnp.concatenate([a, b], axis=0) for a, b in zip(tie(*held), got)]
        tie.mark(*wider)
        return wider

    held_a = colors_of(tie(*slots_a))
    got_a = swap_stage(held_a, 0)
    got_acts = sent(acts_out, *held_a)
    for step in range(1, len(masks)):
        tie.pause()
        held_a = widen(held_a, got_a)
        got_a = swap_stage(held_a, step)
    tie.pause()
    held_a = widen(held_a, got_a)
    tables_a = held_a + [xor_swap(v, "dp", 1) for v in held_a]
    joined, normed, coarse = join(
        my_micro.reshape(1).astype(jnp.int32),
        tie(*got_acts),
        up_tile,
        norm1_gain.reshape(1, -1),
        norm1_shift.reshape(1, -1),
    )
    tie.mark(normed)

    stages_sub = [("head", 1 << i) for i in range(group.bit_length() - 1)]
    stage_lists = [stages_sub + [("dp", m) for m in order] for order in dp_orders]
    stages = len(stage_lists[0])
    shaped = tie(normed).reshape(blocks, BLOCK, model)
    far_held = [shaped[:, :, c * half : (c + 1) * half] for c in (0, 1)]
    tie.mark(*far_held)
    far_got = [xor_swap(v, *stage_lists[c][0]) for c, v in enumerate(far_held)]
    gather_f = HeadGather(tie(strip_f))
    for step in range(1, stages):
        tie.pause()
        far_held = widen(far_held, far_got)
        far_got = [xor_swap(v, *stage_lists[c][step]) for c, v in enumerate(far_held)]
    gather_f.step()
    limit = far_held[0].shape[0]
    table_row = lax.dynamic_index_in_dim(block_targets, my_micro, 0, False)

    def targets_of(device):
        return lax.dynamic_slice_in_dim(table_row, (device * group + my_sub) * blocks, blocks)

    targets = targets_of(me)
    targets_both = jnp.concatenate([targets, targets_of(me ^ 1)])
    owner = jnp.maximum(targets_both, 0) // blocks
    away = (owner // group) ^ me
    away_sub = (owner % group) ^ my_sub

    def table_index(stage_list):
        index = jnp.zeros_like(owner)
        for bit, (axis, mask) in enumerate(stage_list):
            far_bits = away if axis == "dp" else away_sub
            index = index + (((far_bits & mask) != 0).astype(jnp.int32) << bit)
        return index * blocks + jnp.maximum(targets_both, 0) % blocks

    index_a, index_b = table_index(stage_lists[0]), table_index(stage_lists[1])
    on_my_core = (away & 1) == 0
    has_far = (targets >= 0).astype(jnp.int32)
    valid = on_my_core & (targets_both >= 0)
    route_a = jnp.where(valid, index_a, -1)
    route_b = jnp.where(valid, index_b, -1)

    biases = [small]
    for value in slots_a:
        rows3 = value[slab : slab + 3 * small_rows].astype(f32).reshape(3, -1)
        biases.append(rows3[0] + rows3[1] + rows3[2])
    bias_q = jnp.concatenate([b[:hc] for b in biases])
    bias_v = jnp.concatenate([b[hc : 2 * hc] for b in biases])
    bias_one = jnp.concatenate([b[2 * hc : 2 * hc + fc] for b in biases])
    bias_kv = jnp.concatenate([jnp.zeros_like(bias_v), bias_v])
    w_qkv_all, w_out_t = assemble(
        dp_index,
        list(tie(*tables_a)),
        [w_qkv[0], w_qkv[1], w_qkv[2], own_out_t],
        [(t * hc, hc, 0, t * heads_all) for t in range(3)] + [(3 * hc, hc, 1, 0)],
        masks,
        [3 * heads_all, heads_all],
    )
    tie.mark(w_qkv_all, w_out_t)
    qkv = (mm(normed, w_qkv_all) + jnp.concatenate([bias_q, bias_kv])).astype(bf16)
    tie.mark(qkv)

    tie.pause()
    kept, passed = far_pick(list(zip(tie(*far_held), far_got)), index_a, index_b)
    tie.mark(kept, passed)
    passed_got = xor_swap(passed, "dp", 1)
    tie.pause()
    held_f = colors_of(gather_f.slots())
    got_f = swap_stage(held_f, 0)
    got_cot = sent(cot_out, passed_got)
    passed = passed_got
    for step in range(1, len(masks)):
        tie.pause()
        held_f = widen(held_f, got_f)
        got_f = swap_stage(held_f, step)
    far = jnp.where(on_my_core[:blocks, None, None], tie(kept), passed).reshape(tokens, model)
    kv_far = (mm(far, w_qkv_all[:, heads_all:]) + bias_kv).astype(bf16)
    tie.mark(kv_far)
    attended = attention_forward(has_far, qkv, tie(kv_far), heads_all)
    tie.mark(attended, *got_cot[1::2])
    residual = joined + (mm_nt(tie(attended), w_out_t) + b_out)
    normed2_f, standard_two, inverse_two = norm_forward(residual, norm2_gain, norm2_shift)
    normed_two = normed2_f.astype(bf16)
    tie.mark(residual, normed_two)

    incoming = in_rank_order(tie(*got_cot))
    incoming_f = incoming.astype(f32)
    grad_b2 = jnp.sum(incoming_f, axis=0, keepdims=True)
    normed_t, far_t = tie(normed).T, tie(far).T
    incoming_t, normed_two_t = incoming.T, tie(normed_two).T
    tie.mark(grad_b2, normed_t, far_t, incoming_t, normed_two_t)
    tie.pause()
    got_f = list(tie(*got_f))
    tables_f = [v for pair in zip(held_f, got_f) for v in pair]
    held_core = [xor_swap(v, "dp", 1) for v in held_f]
    got_core = [xor_swap(v, "dp", 1) for v in got_f]
    tables_f += [v for pair in zip(held_core, got_core) for v in pair]

    shape = jax.ShapeDtypeStruct
    slope, out, keep_two, send_two = feed_call(
        feed_forward_kernel,
        masks,
        dp_index,
        tables_f,
        w_fc1,
        own_two_t,
        0,
        [
            (normed_two, None),
            (bias_one.reshape(1, -1), (0, False)),
            (residual, None),
            (b_fc2.reshape(1, -1), None),
            (incoming_t, None),
        ],
        [(shape((tokens, hidden_all), bf16), (1, False)), (shape((tokens, model), bf16), None)],
        [pltpu.VMEM((tokens, model), f32)],
    )
    tie.mark(slope)
    got_two = xor_swap(send_two, "dp", 1)

    reversed_bits = [
        sum(m for m, back_m in zip(head_masks, head_masks[::-1]) if p & back_m) for p in range(head_size)
    ]

    class HeadSum:
        def __init__(self, piece):
            self.held = jnp.stack([piece(here ^ p) for p in reversed_bits])
            tie.mark(self.held)
            self.masks = list(head_masks)
            self.send()

        def send(self):
            half = self.held.shape[0] // 2
            self.got = xor_swap(self.held[half:], "head", self.masks.pop(0))

        def step(self):
            half = self.held.shape[0] // 2
            total = tie(self.held)[:half].astype(f32) + self.got.astype(f32)
            if half == 1:
                return total[0]
            self.held = total.astype(bf16)
            tie.mark(self.held)
            self.send()
            return None

        def finish(self):
            out = None
            while out is None:
                out = self.step()
            return out

    class Steps:
        def tokens_out(self):
            out_pieces = from_micro(tie(out))
            tie.mark(*out_pieces)
            self.got_out = back(out_pieces)

        def feed(self):
            self.grad_b1, self.grad_two, self.keep_one, self.send_one = feed_call(
                feed_backward_kernel,
                masks,
                dp_index,
                tables_f,
                own_two_t,
                w_fc1,
                1,
                [(tie(incoming), None), (slope, (1, False)), (normed_two_t, None)],
                [(shape((1, hidden_all), f32), (1, True)), (shape((tokens, model), f32), None)],
                [],
            )
            tie.mark(self.grad_b1)
            self.got_one = xor_swap(self.send_one, "dp", 1)

        def halves(self, keep, got):
            return [
                DpSum(tie, (keep, got), dp_orders[c], c * head_size, head_size)
                for c in range(HALVES)
            ]

        def two_first(self):
            self.sums_two = self.halves(keep_two, got_two)
            for part in self.sums_two:
                part.stage(0)

        def norm(self):
            grad_res_part, self.grad_g2, self.grad_s2 = norm_backward(
                tie(self.grad_two), standard_two, inverse_two, norm2_gain
            )
            self.grad_residual = incoming_f + grad_res_part
            self.grad_branch = self.grad_residual.astype(bf16)
            self.grad_bo = jnp.sum(self.grad_branch.astype(f32), axis=0)
            self.grad_att = mm(self.grad_branch, w_out_t).astype(bf16)
            tie.mark(self.grad_att)

        def attention(self):
            self.grad_qkv = attention_backward(has_far, qkv, kv_far, tie(self.grad_att))
            tie.mark(self.grad_qkv)

        def one_first(self):
            self.sums_one = self.halves(self.keep_one, self.got_one)
            for part in self.sums_one:
                part.stage(0)

        def far_back(self):
            self.far_rows = (
                mm_nt(tie(self.grad_qkv)[1, :, heads_all:], w_qkv_all[:, heads_all:])
                .astype(bf16)
                .reshape(blocks, BLOCK, model)
            )
            tie.mark(self.far_rows)
            self.far_other = xor_swap(self.far_rows, "dp", 1)

        def branch(self):
            self.branch_t = tie(self.grad_branch).T
            tie.mark(self.branch_t)

        def route(self):
            routed = far_route(tie(self.far_rows), self.far_other, route_a, route_b, limit)
            tie.mark(*routed)
            self.terms = [[routed[0]], [routed[2]]]
            for color in range(2):
                axis, mask = stage_lists[color][-1]
                self.terms[color].append(xor_swap(routed[2 * color + 1], axis, mask))

        def weights(self):
            keep, send_att = attention_weights(
                masks, dp_index, normed_t, far_t, self.branch_t, tie(self.grad_qkv), attended, hc
            )
            tie.mark(send_att)
            got = xor_swap(send_att, "dp", 1)
            groups = 2 * head_size
            self.sums_att = [
                DpSum(tie, (keep, got), dp_orders[c], c * groups, groups) for c in (0, 1)
            ]

        def own(self):
            self.grad_own = mm_nt(tie(self.grad_qkv)[0], w_qkv_all)
            self.grad_bq = jnp.sum(tie(self.grad_qkv)[0, :, :heads_all].astype(f32), axis=0)
            self.grad_bv = jnp.sum(
                tie(self.grad_qkv)[:, :, 2 * heads_all :].astype(f32), axis=(0, 1)
            )
            tie.mark(self.grad_own, self.grad_bq, self.grad_bv)

        def hidden_rest(self):
            for step in range(1, len(masks)):
                for c in range(HALVES):
                    pair = (self.sums_two[c], self.sums_one[c])
                    low, high = pair[0].rows >> (step + 1), pair[0].rows >> step
                    moved = jnp.concatenate([part.upto(low, high) for part in pair], axis=0)
                    tie.mark(moved)
                    moved = xor_swap(moved, "dp", dp_orders[c][step])
                    for i, part in enumerate(pair):
                        part.terms.append((moved, i * head_size))

        def hidden_head(self):
            ends = [part.final() for part in self.sums_two + self.sums_one]
            self.sum_f = HeadSum(
                lambda a: jnp.stack([lax.dynamic_index_in_dim(v, a, 0, False) for v in ends])
            )

        def hidden_step(self):
            self.sum_f.step()

        def far_rest(self):
            for step in range(stages - 2, -1, -1):
                low, high = blocks << step, blocks << (step + 1)
                moved = []
                for color in range(2):
                    value = sum(t[low:high].astype(f32) for t in tie(*self.terms[color]))
                    moved.append(value.astype(bf16))
                tie.mark(*moved)
                for color in range(2):
                    self.terms[color].append(xor_swap(moved[color], *stage_lists[color][step]))

        def att_first(self):
            for part in self.sums_att:
                part.stage(0)

        def att_rest(self):
            for step in range(1, len(masks)):
                for part in self.sums_att:
                    part.stage(step)

        def att_head(self):
            ends = [part.final().reshape(2, head_size, slab, hc) for part in self.sums_att]
            self.sum_att = HeadSum(
                lambda a: jnp.concatenate(
                    [lax.dynamic_index_in_dim(v, a ^ here, 1, False) for v in ends], axis=0
                )
            )

        def att_step(self):
            self.sum_att.step()

        def leave(self):
            self.grad_input, self.grad_up, self.grad_g1, self.grad_s1 = leave(
                tie(self.grad_own),
                joined,
                self.grad_residual,
                coarse,
                norm1_gain.reshape(1, -1),
                *self.terms,
            )
            tie.mark(self.grad_input)

        def tokens_back(self):
            in_pieces = from_micro(tie(self.grad_input))
            tie.mark(*in_pieces)
            self.got_input = back(in_pieces)

        def tokens_end(self):
            self.grad_input = in_micro_order(tie(*self.got_input)).astype(f32)
            self.grad_coarse = jnp.sum(
                self.grad_input.reshape(micro, -1, UP, model) * up_gain, axis=2
            )
            tie.mark(self.grad_input, self.grad_coarse)

        def small(self):
            by_slot = jnp.concatenate(
                [self.grad_bq.reshape(-1, hc), self.grad_bv.reshape(-1, hc)], axis=1
            )
            by_head = jnp.concatenate(
                [choose([by_slot[s] for s in range(head_size)], a ^ here) for a in range(head_size)]
            )
            self.total = jnp.concatenate(
                [tie(self.grad_up), self.grad_g1, self.grad_s1]
                + [v.reshape(1, -1) for v in (self.grad_bo, self.grad_g2, self.grad_s2)]
                + [grad_b2, self.grad_b1.reshape(-1, model), by_head.reshape(-1, model)]
            )
            tie.mark(self.total)
            self.small_stages = [("dp", m) for m in [1] + masks] + [("head", m) for m in head_masks]
            self.small_got = None

        def small_step(self):
            if self.small_got is not None:
                self.total = tie(self.total) + self.small_got
                tie.mark(self.total)
                self.small_got = None
            if self.small_stages:
                self.small_got = xor_swap(self.total, *self.small_stages.pop(0))

        def small_end(self):
            self.small_step()
            while self.small_got is not None:
                tie.pause()
                self.small_step()

        def layer(self):
            self.layer_out = in_micro_order(tie(*self.got_out))
            tie.mark(self.layer_out)

        def wait_out(self):
            tie.mark(*tie.last, *self.got_out)

        def wait_two(self):
            tie.mark(*tie.last, *[part.terms[-1][0] for part in self.sums_two])

        def wait_one(self):
            tie.mark(*tie.last, *[part.terms[-1][0] for part in self.sums_one])

        def wait_att(self):
            tie.mark(*tie.last, *[part.terms[-1][0] for part in self.sums_att])

        def wait_far(self):
            tie.mark(*tie.last, *[t[-1] for t in self.terms])

        def pause(self):
            tie.pause()

        def flush(self):
            tie.flush()

    it = Steps()
    for name in STEPS:
        getattr(it, name)()
    layer_out = it.layer_out
    grad_input, grad_coarse, total = it.grad_input, it.grad_coarse, it.total
    grad_wf, grad_wa = it.sum_f.finish(), it.sum_att.finish()
    grad_w2 = jnp.concatenate([grad_wf[c].T for c in range(HALVES)], axis=0)
    grad_w1 = jnp.concatenate([grad_wf[HALVES + c] for c in range(HALVES)], axis=1)
    grad_wqkv, grad_wo = grad_wa[:3], grad_wa[3].T
    s_g1, s_s1, s_bo, s_g2, s_s2, s_b2 = [total[UP + i] for i in range(6)]
    hidden_rows = hidden_all // model
    s_b1 = total[UP + 6 : UP + 6 + hidden_rows].reshape(-1)
    by_head = total[UP + 6 + hidden_rows :].reshape(head_size, 2 * hc)
    s_bq, s_bv = by_head[:, :hc].reshape(-1), by_head[:, hc:].reshape(-1)
    return (
        layer_out,
        grad_input,
        grad_coarse,
        total[:UP],
        s_g1,
        s_s1,
        grad_wqkv,
        jnp.stack([s_bq, s_bv]),
        grad_wo,
        s_bo,
        s_g2,
        s_s2,
        grad_w1,
        s_b1,
        grad_w2,
        s_b2,
    )


def solution(mesh):
    rows = P(None, ("dp", "head"), None)
    return jax.shard_map(
        local,
        mesh=mesh,
        in_specs=(
            rows,
            rows,
            rows,
            P(),
            P(),
            P(),
            P(),
            P(None, None, "head"),
            P(None, "head"),
            P("head", None),
            P(),
            P(),
            P(),
            P(None, "head"),
            P("head"),
            P("head", None),
            P(),
        ),
        out_specs=(
            rows,
            rows,
            rows,
            P(),
            P(),
            P(),
            P(None, "dp", "head"),
            P(),
            P("head", "dp"),
            P(),
            P(),
            P(),
            P("dp", "head"),
            P(),
            P("head", "dp"),
            P(),
        ),
        check_vma=False,
    )
```

```python
import functools
import math

import jax
import jax.numpy as jnp
from jax import lax
from jax.experimental import pallas as pl
from jax.experimental.pallas import tpu as pltpu
from jax.sharding import PartitionSpec as P

HEAD_DIM = 64
BLOCK = 128
UP = 4
HALVES = 2
VMEM_LIMIT = 58 << 20
STEPS = ["tokens_out", "feed", "two_first", "one_first", "norm", "attention", "far_back", "hidden_rest", "branch", "pause", "route", "weights", "hidden_head", "own", "pause", "far_rest", "att_first", "layer", "pause", "leave", "att_rest", "tokens_back", "pause", "pause", "pause", "small", "hidden_step", "att_head", "tokens_end", "pause", "att_step", "small_step", "small_end"]
PAIR = 2 * HEAD_DIM
NEGATIVE = -1e30
epsilon = 1e-05
f32 = jnp.float32
bf16 = jnp.bfloat16
ROOT_2_PI = math.sqrt(2.0 / math.pi)
LONG_COST = pl.CostEstimate(flops=1 << 36, bytes_accessed=1 << 26, transcendentals=0)


def xor_swap(value, axis, mask):
    size = lax.axis_size(axis)
    return lax.ppermute(value, axis, [(i, i ^ mask) for i in range(size)])


def pause_kernel(value_ref, out_ref):
    out_ref[...] = value_ref[...]


class Order:
    def __init__(self):
        self.last = ()
        self.token = None

    def __call__(self, *values):
        tied = lax.optimization_barrier(tuple(values) + self.last)[: len(values)]
        return tied[0] if len(values) == 1 else tied

    def mark(self, *values):
        self.last = values

    def flush(self):
        tied = self(jnp.zeros((8, 128), f32) if self.token is None else self.token)
        self.token = xor_swap(tied, "dp", 1)
        self.mark(self.token)

    def pause(self):
        self.token = self(jnp.zeros((8, 128), f32) if self.token is None else self.token)
        self.token = pl.pallas_call(
            pause_kernel, out_shape=jax.ShapeDtypeStruct((8, 128), f32), cost_estimate=LONG_COST
        )(self.token)
        self.mark(self.token)


def norm_forward(values, gain, shift):
    centered = values - jnp.mean(values, axis=-1, keepdims=True)
    inverse = lax.rsqrt(jnp.mean(centered * centered, axis=-1, keepdims=True) + epsilon)
    standard = centered * inverse
    return (standard * gain + shift, standard, inverse)


def norm_backward(upstream, standard, inverse, gain):
    scaled = upstream * gain
    inner = (
        scaled
        - jnp.mean(scaled, axis=-1, keepdims=True)
        - standard * jnp.mean(scaled * standard, axis=-1, keepdims=True)
    )
    return (inner * inverse, jnp.sum(upstream * standard, axis=0), jnp.sum(upstream, axis=0))


def mm(left, right):
    return jnp.dot(left, right, preferred_element_type=f32)


def mm_nt(left, right):
    return lax.dot_general(left, right, (((1,), (1,)), ((), ())), preferred_element_type=f32)


def mm_tn(left, right):
    return lax.dot_general(left, right, (((0,), (0,)), ((), ())), preferred_element_type=f32)


def pair_probs(q_pair, k_cat, allowed):
    low_half = lax.broadcasted_iota(jnp.int32, (BLOCK, PAIR), 1) < HEAD_DIM
    zero = jnp.zeros_like(q_pair)
    q_pair = q_pair * jnp.asarray(1.0 / math.sqrt(HEAD_DIM), q_pair.dtype)
    q_stack = jnp.concatenate(
        [jnp.where(low_half, q_pair, zero), jnp.where(low_half, zero, q_pair)], axis=0
    )
    scores = mm_nt(k_cat, q_stack)
    scores = jnp.where(allowed, scores, NEGATIVE)
    top = jnp.max(scores, axis=0, keepdims=True)
    raised = jnp.exp(scores - top)
    probs = raised * (1.0 / jnp.sum(raised, axis=0, keepdims=True))
    return q_stack, probs, low_half


def allowed_mask(far_flag):
    key_at = lax.broadcasted_iota(jnp.int32, (2 * BLOCK, 2 * BLOCK), 0)
    query_at = lax.broadcasted_iota(jnp.int32, (2 * BLOCK, 2 * BLOCK), 1)
    query_at = jnp.where(query_at >= BLOCK, query_at - BLOCK, query_at)
    first = jnp.where(far_flag > 0, BLOCK, 2 * BLOCK)
    return (key_at <= query_at) | (key_at >= first)


def pair_columns(p, width):
    return [slice(t * width + p * PAIR, t * width + (p + 1) * PAIR) for t in range(3)]


def key_value(own_ref, far_ref, columns, width):
    out = []
    for cols in columns[1:]:
        far_cols = slice(cols.start - width, cols.stop - width)
        out.append(jnp.concatenate([own_ref[:, cols], far_ref[:, far_cols]], axis=0))
    return out


def attention_forward_kernel(pairs, has_far, own_ref, far_ref, out_ref):
    allowed = allowed_mask(has_far[pl.program_id(0)])
    width = pairs * PAIR
    for p in range(pairs):
        columns = pair_columns(p, width)
        k_cat, v_cat = key_value(own_ref, far_ref, columns, width)
        _, probs, low_half = pair_probs(own_ref[:, columns[0]], k_cat, allowed)
        mixed = mm_tn(probs.astype(bf16), v_cat)
        out_ref[:, columns[0]] = jnp.where(low_half, mixed[:BLOCK], mixed[BLOCK:]).astype(bf16)


def attention_forward(has_far, own, far, width):
    blocks = has_far.shape[0]
    row_block = lambda array: pl.BlockSpec((BLOCK, array.shape[1]), lambda b, flags: (b, 0))
    shape = jax.ShapeDtypeStruct((blocks * BLOCK, width), bf16)
    return pl.pallas_call(
        functools.partial(attention_forward_kernel, width // PAIR),
        grid_spec=pltpu.PrefetchScalarGridSpec(
            num_scalar_prefetch=1,
            grid=(blocks,),
            in_specs=[row_block(own), row_block(far)],
            out_specs=row_block(shape),
        ),
        out_shape=shape,
        compiler_params=pltpu.CompilerParams(vmem_limit_bytes=16 << 20),
        cost_estimate=LONG_COST,
    )(has_far, own, far)


def attention_backward_kernel(pairs, has_far, own_ref, far_ref, grad_ref, out_ref):
    allowed = allowed_mask(has_far[pl.program_id(0)])
    width = pairs * PAIR
    scale = 1.0 / math.sqrt(HEAD_DIM)
    out_ref[1, :, :width] = jnp.zeros((BLOCK, width), bf16)
    for p in range(pairs):
        columns = pair_columns(p, width)
        k_cat, v_cat = key_value(own_ref, far_ref, columns, width)
        q_stack, probs, low_half = pair_probs(own_ref[:, columns[0]], k_cat, allowed)
        grad = grad_ref[:, columns[0]]
        zero = jnp.zeros_like(grad)
        grad_stack = jnp.concatenate(
            [jnp.where(low_half, grad, zero), jnp.where(low_half, zero, grad)], axis=0
        )
        grad_probs = mm_nt(v_cat, grad_stack)
        total = jnp.sum(probs * grad_probs, axis=0, keepdims=True)
        grad_scores = (probs * (grad_probs - total)).astype(bf16)
        dq = mm_tn(grad_scores, k_cat)
        dq = jnp.where(low_half, dq[:BLOCK], dq[BLOCK:]) * scale
        out_ref[0, :, columns[0]] = dq.astype(bf16)
        dk = mm(grad_scores, q_stack).astype(bf16)
        dv = mm(probs.astype(bf16), grad_stack).astype(bf16)
        for half in range(2):
            rows = slice(half * BLOCK, (half + 1) * BLOCK)
            out_ref[half, :, columns[1]] = dk[rows]
            out_ref[half, :, columns[2]] = dv[rows]


def attention_backward(has_far, own, far, grad):
    blocks, width = has_far.shape[0], grad.shape[1]
    row_block = lambda array: pl.BlockSpec((BLOCK, array.shape[1]), lambda b, flags: (b, 0))
    return pl.pallas_call(
        functools.partial(attention_backward_kernel, width // PAIR),
        grid_spec=pltpu.PrefetchScalarGridSpec(
            num_scalar_prefetch=1,
            grid=(blocks,),
            in_specs=[row_block(own), row_block(far), row_block(grad)],
            out_specs=pl.BlockSpec((2, BLOCK, 3 * width), lambda b, flags: (0, b, 0)),
        ),
        out_shape=jax.ShapeDtypeStruct((2, blocks * BLOCK, 3 * width), bf16),
        compiler_params=pltpu.CompilerParams(vmem_limit_bytes=20 << 20),
        cost_estimate=LONG_COST,
    )(has_far, own, far, grad)


def join_kernel(rows, first, *refs):
    got, (tile_ref, gain_ref, shift_ref, joined_ref, normed_ref, coarse_ref, held_ref) = (
        refs[:-7],
        refs[-7:],
    )
    pieces = len(got)
    which = (first[0] + pieces - pl.program_id(0)) % pieces
    for s in range(pieces):

        @pl.when(which == s)
        def _():
            held_ref[...] = got[s][...]

    coarse = held_ref[rows:, :]
    coarse_ref[...] = coarse
    up_row = lax.broadcasted_iota(jnp.int32, (rows, rows // UP), 0) // UP
    up_col = lax.broadcasted_iota(jnp.int32, (rows, rows // UP), 1)
    spread = mm((up_row == up_col).astype(f32).astype(bf16), coarse)
    joined = held_ref[:rows, :].astype(f32) + spread * tile_ref[...]
    joined_ref[...] = joined
    normed_ref[...] = norm_forward(joined, gain_ref[...], shift_ref[...])[0].astype(bf16)


def join(first, got, tile, gain, shift):
    pieces, rows, model = len(got), tile.shape[0], tile.shape[1]
    small = rows // UP
    fixed = lambda array: pl.BlockSpec(array.shape, lambda p, f: (0, 0))
    piece = lambda count: pl.BlockSpec((count, model), lambda p, f: (p, 0))
    return pl.pallas_call(
        functools.partial(join_kernel, rows),
        grid_spec=pltpu.PrefetchScalarGridSpec(
            num_scalar_prefetch=1,
            grid=(pieces,),
            in_specs=[fixed(g) for g in got] + [fixed(tile), fixed(gain), fixed(shift)],
            out_specs=[piece(rows), piece(rows), piece(small)],
            scratch_shapes=[pltpu.VMEM((rows + small, model), bf16)],
        ),
        out_shape=[
            jax.ShapeDtypeStruct((pieces * rows, model), f32),
            jax.ShapeDtypeStruct((pieces * rows, model), bf16),
            jax.ShapeDtypeStruct((pieces * small, model), bf16),
        ],
        compiler_params=pltpu.CompilerParams(vmem_limit_bytes=16 << 20),
        cost_estimate=LONG_COST,
    )(first, *got, tile, gain, shift)


def fill_chunk(masks, me, tables, out_ref):
    half, count = tables[0].shape[2], tables[0].shape[0]
    for which, table in enumerate(tables):
        core, color, late = which // 4, which // 2 % 2, which % 2
        order = masks if color == 0 else masks[::-1]
        for k, mask in enumerate(relative_masks(order)[late * count : (late + 1) * count]):
            row = (me ^ (mask | core)) * 2 * half + color * half
            out_ref[pl.ds(pl.multiple_of(row, half), half), :] = table[k, 0]


def load_chunk(masks, me, chunk, n_own, own_ref, tables, out_ref):
    @pl.when(chunk < n_own)
    def _():
        out_ref[...] = own_ref[...]

    @pl.when(chunk >= n_own)
    def _():
        fill_chunk(masks, me, tables, out_ref)


def by_stage(step, n, buffers, begin, body, end):
    @pl.when(step == 0)
    def _():
        begin(buffers[0])

    for parity in range(2):

        @pl.when((step % 2 == parity) & (step > 0) & (step < n))
        def _():
            body(buffers[1 - parity], buffers[parity])

    @pl.when(step == n)
    def _():
        end(buffers[(n + 1) % 2])


def scatter_rows(masks, color, me, value, held_ref):
    count = 2 << len(masks)
    slab = value.shape[0] // count
    last = len(masks) - 1
    for b in range(count):
        away = me ^ b
        at = (away & 1) << len(masks)
        for i, mask in enumerate(masks):
            place = last - i if isinstance(color, int) and color == 0 else i
            if not isinstance(color, int):
                place = jnp.where(color == 0, last - i, i)
            at = at + (((away >> (mask.bit_length() - 1)) & 1) << place)
        row = pl.multiple_of(at * slab, slab)
        held_ref[pl.ds(row, slab), :] = value[b * slab : (b + 1) * slab].astype(bf16)


def split_rows(held_ref, keep_ref, send_ref):
    half = held_ref.shape[0] // 2
    keep_ref[0] = held_ref[:half, :]
    send_ref[0] = held_ref[half:, :]


def feed_forward_kernel(masks, n_own, n, me, *refs):
    one_tables, two_tables, refs = refs[:8], refs[8:16], refs[16:]
    (own_one, own_two, x_ref, bias_ref, residual_ref, last_ref, left_ref) = refs[:7]
    slope_ref, out_ref, keep_ref, send_ref = refs[7:11]
    w_one, w_two, even_ref, odd_ref, act_ref, held_ref, acc_ref = refs[11:]
    step = pl.program_id(0)
    load_chunk(masks, me[0], jnp.minimum(step, n - 1), n_own, own_one, one_tables, w_one)
    load_chunk(masks, me[0], jnp.maximum(step - 1, 0), n_own, own_two, two_tables, w_two)
    ratio = ROOT_2_PI * 0.044715
    rows = x_ref.shape[0] // 3

    parts = [slice(r * rows, (r + 1) * rows) for r in range(3)]

    def finish(at, before):
        h = before[at, :]
        square = h * h
        gate = 0.5 + 0.5 * jnp.tanh(h * (ROOT_2_PI + ratio * square))
        act = (h * gate).astype(bf16)
        act_ref[at, :] = act
        slope_ref[at, :] = (
            gate * (1.0 + 2.0 * h * (1.0 - gate) * (ROOT_2_PI + 3.0 * ratio * square))
        ).astype(bf16)
        return act

    def start(at, now):
        now[at, :] = mm(x_ref[at, :], w_one[...]) + bias_ref[...]

    def gradient():
        color = jnp.maximum(step - 1, 0) % n_own
        scatter_rows(masks, color, me[0], mm(left_ref[...], act_ref[...]), held_ref)

    def begin(now):
        acc_ref[...] = jnp.zeros_like(acc_ref)
        for at in parts:
            start(at, now)

    def body(before, now):
        for at in parts:
            act = finish(at, before)
            start(at, now)
            acc_ref[at, :] += mm_nt(act, w_two[...])
        gradient()

    def end(before):
        for at in parts:
            act = finish(at, before)
            acc_ref[at, :] += mm_nt(act, w_two[...])
        gradient()

    by_stage(step, n, (even_ref, odd_ref), begin, body, end)
    split_rows(held_ref, keep_ref, send_ref)

    @pl.when(step == n)
    def _():
        out_ref[...] = (residual_ref[...] + (acc_ref[...] + last_ref[...])).astype(bf16)


def feed_backward_kernel(masks, n_own, n, me, *refs):
    two_tables, one_tables, refs = refs[:8], refs[8:16], refs[16:]
    own_two, own_one, g_ref, slope_ref, left_ref = refs[:5]
    bias_ref, out_ref, keep_ref, send_ref = refs[5:9]
    w_two, w_one, even_ref, odd_ref, grad_ref, held_ref = refs[9:]
    step = pl.program_id(0)
    load_chunk(masks, me[0], jnp.minimum(step, n - 1), n_own, own_two, two_tables, w_two)
    load_chunk(masks, me[0], jnp.maximum(step - 1, 0), n_own, own_one, one_tables, w_one)
    rows = g_ref.shape[0] // 2

    parts = [slice(r * rows, (r + 1) * rows) for r in range(2)]

    def start(at, now):
        now[at, :] = mm(g_ref[at, :], w_two[...])

    def finish(at, before):
        grad = (before[at, :] * slope_ref[at, :].astype(f32)).astype(bf16)
        grad_ref[at, :] = grad
        out_ref[at, :] += mm_nt(grad, w_one[...])
        return jnp.sum(grad.astype(f32), axis=0, keepdims=True)

    def gradient(sums):
        bias_ref[...] = sums[0] + sums[1]
        color = jnp.maximum(step - 1, 0) % n_own
        scatter_rows(masks, color, me[0], mm(left_ref[...], grad_ref[...]), held_ref)

    def begin(now):
        out_ref[...] = jnp.zeros_like(out_ref)
        for at in parts:
            start(at, now)

    def body(before, now):
        sums = []
        for at in parts:
            start(at, now)
            sums.append(finish(at, before))
        gradient(sums)

    def end(before):
        gradient([finish(at, before) for at in parts])

    by_stage(step, n, (even_ref, odd_ref), begin, body, end)
    split_rows(held_ref, keep_ref, send_ref)


def feed_call(kernel, masks, me, tables, own_first, own_second, first_part, arrays, outs, scratch):
    count, slots, half, both = tables[0].shape
    model, width = own_first.shape
    n_own = HALVES
    chunk = width // n_own
    n = n_own * (slots + 1)

    def at(j, lag):
        return jnp.clip(j - lag, 0, n - 1)

    def by_head(j, lag, me):
        c = at(j, lag)
        return ((c // n_own) ^ me[1]) * n_own + c % n_own

    def by_half(j, me):
        c = at(j, 1)
        return c % n_own * (slots + 1) + ((c // n_own) ^ me[1])

    def table_spec(part, lag):
        def index(j, me):
            c = jnp.maximum(at(j, lag), n_own)
            return (0, c // n_own - 1, 0, part * n_own + c % n_own)

        return pl.BlockSpec((count, 1, half, chunk), index)

    def own_spec(lag):
        return pl.BlockSpec((model, chunk), lambda j, me: (0, jnp.minimum(at(j, lag), n_own - 1)))

    def spec(array, lag):
        if lag is None:
            return pl.BlockSpec(array.shape, lambda j, me: (0, 0))
        lag, absolute = lag
        return pl.BlockSpec(
            (array.shape[0], chunk), lambda j, me: (0, by_head(j, lag, me) if absolute else at(j, lag))
        )

    rows = arrays[0][0].shape[0]
    weight = jax.ShapeDtypeStruct((n, model // 2, chunk), bf16)
    weight_spec = pl.BlockSpec((1, model // 2, chunk), lambda j, me: (by_half(j, me), 0, 0))
    return pl.pallas_call(
        functools.partial(kernel, masks, n_own, n),
        grid_spec=pltpu.PrefetchScalarGridSpec(
            num_scalar_prefetch=1,
            grid=(n + 1,),
            in_specs=[table_spec(first_part, 0)] * 8
            + [table_spec(1 - first_part, 1)] * 8
            + [own_spec(0), own_spec(1)]
            + [spec(a, lag) for a, lag in arrays],
            out_specs=[spec(o, lag) for o, lag in outs] + [weight_spec, weight_spec],
            scratch_shapes=[
                pltpu.VMEM((model, chunk), bf16),
                pltpu.VMEM((model, chunk), bf16),
                pltpu.VMEM((rows, chunk), f32),
                pltpu.VMEM((rows, chunk), f32),
                pltpu.VMEM((rows, chunk), bf16),
                pltpu.VMEM((model, chunk), bf16),
            ]
            + scratch,
        ),
        out_shape=[o for o, _ in outs] + [weight, weight],
        compiler_params=pltpu.CompilerParams(vmem_limit_bytes=54 << 20),
        cost_estimate=LONG_COST,
    )(me, *tables, *tables, own_first, own_second, *[a for a, _ in arrays])


def far_pick_kernel(limit, where_a, where_b, *refs):
    ins, outs = refs[:8], refs[8:]
    count, half = pl.num_programs(0), ins[0].shape[2]
    for who in range(2):
        for color, where_ref in enumerate((where_a, where_b)):
            held, got = ins[4 * who + 2 * color : 4 * who + 2 * color + 2]
            beyond = where_ref[pl.program_id(0) + who * count] >= limit
            outs[who][0, :, color * half : (color + 1) * half] = jnp.where(beyond, got[0], held[0])


def far_pick(tables, where_a, where_b):
    count = where_a.shape[0] // 2
    limit, _, half = tables[0][0].shape

    def spec(who, color):
        def index(j, wa, wb):
            return ((wa, wb)[color][j + who * count] % limit, 0, 0)

        return pl.BlockSpec((1, BLOCK, half), index)

    out = pl.BlockSpec((1, BLOCK, 2 * half), lambda j, wa, wb: (j, 0, 0))
    shape = jax.ShapeDtypeStruct((count, BLOCK, 2 * half), bf16)
    return pl.pallas_call(
        functools.partial(far_pick_kernel, limit),
        grid_spec=pltpu.PrefetchScalarGridSpec(
            num_scalar_prefetch=2,
            grid=(count,),
            in_specs=[spec(who, color) for who in range(2) for color in range(2) for _ in range(2)],
            out_specs=[out, out],
        ),
        out_shape=[shape, shape],
        compiler_params=pltpu.CompilerParams(vmem_limit_bytes=VMEM_LIMIT),
        cost_estimate=LONG_COST,
    )(where_a, where_b, *[t for _ in range(2) for table in tables for t in table])


def far_route_kernel(count, where_a, where_b, mine_ref, other_ref, *refs):
    outs, acc_ref = refs[:4], refs[4]
    half = outs[0].shape[2]
    acc_ref[...] = jnp.zeros_like(acc_ref)
    for part in range(2):
        step = pl.program_id(0) + part * pl.num_programs(0)
        for source, base in ((mine_ref, 0), (other_ref, count)):
            for j in range(count):

                @pl.when(where_a[base + j] == step)
                def _():
                    acc_ref[part, :, :half] += source[j, :, :half].astype(f32)

                @pl.when(where_b[base + j] == step)
                def _():
                    acc_ref[part, :, half:] += source[j, :, half:].astype(f32)

        outs[part][0] = acc_ref[part, :, :half].astype(bf16)
        outs[2 + part][0] = acc_ref[part, :, half:].astype(bf16)


def far_route(mine, other, where_a, where_b, limit):
    count, _, width = mine.shape
    whole = pl.BlockSpec(mine.shape, lambda k, wa, wb: (0, 0, 0))
    out = pl.BlockSpec((1, BLOCK, width // 2), lambda k, wa, wb: (k, 0, 0))
    shape = jax.ShapeDtypeStruct((limit, BLOCK, width // 2), bf16)
    return pl.pallas_call(
        functools.partial(far_route_kernel, count),
        grid_spec=pltpu.PrefetchScalarGridSpec(
            num_scalar_prefetch=2,
            grid=(limit,),
            in_specs=[whole, whole],
            out_specs=[out] * 4,
            scratch_shapes=[pltpu.VMEM((2, BLOCK, width), f32)],
        ),
        out_shape=[shape] * 4,
        compiler_params=pltpu.CompilerParams(vmem_limit_bytes=18 << 20),
        cost_estimate=LONG_COST,
    )(where_a, where_b, mine, other)


def leave_kernel(n_a, n_b, own_ref, joined_ref, res_ref, coarse_ref, gain_ref, *refs):
    part_a, part_b = refs[:n_a], refs[n_a : n_a + n_b]
    out_ref, up_ref, gain_out, shift_out = refs[n_a + n_b :]

    @pl.when(pl.program_id(0) == 0)
    def _():
        for ref in (up_ref, gain_out, shift_out):
            ref[...] = jnp.zeros_like(ref)

    back = jnp.concatenate(
        [sum(r[0].astype(f32) for r in parts) for parts in (part_a, part_b)], axis=1
    )
    upstream = own_ref[...] + back
    gain = gain_ref[...]
    joined = joined_ref[...]
    _, standard, inverse = norm_forward(joined, gain, gain)
    scaled = upstream * gain
    inner = (
        scaled
        - jnp.mean(scaled, axis=-1, keepdims=True)
        - standard * jnp.mean(scaled * standard, axis=-1, keepdims=True)
    )
    total = res_ref[...] + inner * inverse
    out_ref[...] = total.astype(bf16)
    gain_out[...] += jnp.sum(upstream * standard, axis=0, keepdims=True)
    shift_out[...] += jnp.sum(upstream, axis=0, keepdims=True)
    up_row = lax.broadcasted_iota(jnp.int32, (BLOCK, BLOCK // UP), 0) // UP
    up_col = lax.broadcasted_iota(jnp.int32, (BLOCK, BLOCK // UP), 1)
    weighted = total * mm((up_row == up_col).astype(f32).astype(bf16), coarse_ref[...])
    phase = lax.broadcasted_iota(jnp.int32, weighted.shape, 0) % UP
    for p in range(UP):
        picked = jnp.where(phase == p, weighted, 0.0)
        up_ref[p : p + 1, :] += jnp.sum(picked, axis=0, keepdims=True)


def leave(own, joined, residual, coarse, gain, part_a, part_b):
    tokens, model = own.shape
    rows = pl.BlockSpec((BLOCK, model), lambda b: (b, 0))
    fixed = lambda count: pl.BlockSpec((count, model), lambda b: (0, 0))
    part = pl.BlockSpec((1, BLOCK, model // 2), lambda b: (b, 0, 0))
    return pl.pallas_call(
        functools.partial(leave_kernel, len(part_a), len(part_b)),
        grid=(tokens // BLOCK,),
        in_specs=[rows, rows, rows, pl.BlockSpec((BLOCK // UP, model), lambda b: (b, 0)), fixed(1)]
        + [part] * (len(part_a) + len(part_b)),
        out_specs=[rows, fixed(UP), fixed(1), fixed(1)],
        out_shape=[
            jax.ShapeDtypeStruct((tokens, model), bf16),
            jax.ShapeDtypeStruct((UP, model), f32),
            jax.ShapeDtypeStruct((1, model), f32),
            jax.ShapeDtypeStruct((1, model), f32),
        ],
        compiler_params=pltpu.CompilerParams(vmem_limit_bytes=VMEM_LIMIT),
        cost_estimate=LONG_COST,
    )(own, joined, residual, coarse, gain, *part_a, *part_b)


def relative_masks(masks):
    return [sum(m for bit, m in enumerate(masks) if k >> bit & 1) for k in range(1 << len(masks))]


def assemble_kernel(columns, n_own, n_out, dp_index, *refs):
    tables, own, outs = refs[:4], refs[4 : 4 + n_own], refs[4 + n_own :]
    slots, half = tables[0].shape[1], tables[0].shape[2]

    def fill(first, second):
        for color, table in enumerate((first, second)):
            rows = slice(color * half, (color + 1) * half)
            for c0, width, target, t0 in columns:
                for s in range(slots):
                    at = t0 + (s + 1) * width
                    outs[target][rows, at : at + width] = table[0, s, :, c0 : c0 + width]

    core = pl.program_id(0)

    @pl.when(core == 0)
    def _():
        fill(tables[0], tables[1])

    @pl.when(core == 1)
    def _():
        fill(tables[2], tables[3])

    for ref, (c0, width, target, t0) in zip(own, columns):
        outs[target][:, t0 : t0 + width] = ref[...]


def assemble(dp_index, tables, own, columns, masks, widths):
    bits = len(masks)
    count, slots, half, width = tables[0].shape
    model = 2 * count * 2 * half

    def reverse(k):
        return sum(((k >> i) & 1) << (bits - 1 - i) for i in range(bits))

    def table_spec(which):
        def index(core, k, dp):
            k = jnp.where(core == which // 2, k, 0 if which >= 2 else count - 1)
            return (reverse(k) if which % 2 else k, 0, 0, 0)

        return pl.BlockSpec((1, slots, half, width), index)

    def row(core, k, dp):
        return (dp[0] ^ ((k << 1) | core), 0)

    return pl.pallas_call(
        functools.partial(assemble_kernel, columns, len(own), len(widths)),
        grid_spec=pltpu.PrefetchScalarGridSpec(
            num_scalar_prefetch=1,
            grid=(2, count),
            in_specs=[table_spec(i) for i in range(4)]
            + [pl.BlockSpec((2 * half, o.shape[1]), row) for o in own],
            out_specs=[pl.BlockSpec((2 * half, w), row) for w in widths],
        ),
        out_shape=[jax.ShapeDtypeStruct((model, w), bf16) for w in widths],
        compiler_params=pltpu.CompilerParams(vmem_limit_bytes=16 << 20),
        cost_estimate=LONG_COST,
    )(dp_index, *tables, *own)


def attention_weights_kernel(masks, heads, me, own_t, far_t, branch_t, grad_own, grad_far, attended, *refs):
    keep_ref, send_ref, total_ref, held_ref = refs
    tile = pl.program_id(0)
    kind = tile // heads

    @pl.when(kind == 0)
    def _():
        total_ref[...] = mm(own_t[...], grad_own[...])

    @pl.when((kind == 1) | (kind == 2))
    def _():
        total_ref[...] = mm(own_t[...], grad_own[...]) + mm(far_t[...], grad_far[...])

    @pl.when(kind == 3)
    def _():
        total_ref[...] = mm(branch_t[...], attended[...])

    for color in range(2):

        @pl.when(kind // 2 == color)
        def _():
            scatter_rows(masks, color, me[0], total_ref[...], held_ref)

    split_rows(held_ref, keep_ref, send_ref)


def attention_weights(masks, me, own_t, far_t, branch_t, grad, attended, width):
    model, tokens = own_t.shape
    heads = attended.shape[1] // width
    whole = pl.BlockSpec((model, tokens), lambda j, me: (0, 0))
    part = lambda p: pl.BlockSpec(
        (None, tokens, width), lambda j, me: (p, 0, jnp.minimum(j, 3 * heads - 1))
    )
    out = pl.BlockSpec((1, model // 2, width), lambda j, me: (j, 0, 0))
    shape = jax.ShapeDtypeStruct((4 * heads, model // 2, width), bf16)
    return pl.pallas_call(
        functools.partial(attention_weights_kernel, masks, heads),
        grid_spec=pltpu.PrefetchScalarGridSpec(
            num_scalar_prefetch=1,
            grid=(4 * heads,),
            in_specs=[whole] * 3
            + [
                part(0),
                part(1),
                pl.BlockSpec((tokens, width), lambda j, me: (0, jnp.maximum(j - 3 * heads, 0))),
            ],
            out_specs=[out, out],
            scratch_shapes=[pltpu.VMEM((model, width), f32), pltpu.VMEM((model, width), bf16)],
        ),
        out_shape=[shape, shape],
        compiler_params=pltpu.CompilerParams(vmem_limit_bytes=24 << 20),
        cost_estimate=LONG_COST,
    )(me, own_t, far_t, branch_t, grad, grad, attended)


class DpSum:
    def __init__(self, tie, terms, order, group, count):
        self.tie, self.order = tie, order
        self.terms = [(value, group) for value in terms]
        self.count, self.rows = count, terms[0].shape[1]

    def upto(self, low, high):
        values = self.tie(*[value for value, _ in self.terms])
        total = 0.0
        for value, (_, group) in zip(values, self.terms):
            total = total + value[group : group + self.count, low:high].astype(f32)
        total = total.astype(bf16)
        self.tie.mark(total)
        return total

    def stage(self, step):
        sent = self.upto(self.rows >> (step + 1), self.rows >> step)
        self.terms.append((xor_swap(sent, "dp", self.order[step]), 0))

    def final(self):
        return self.upto(0, self.rows >> len(self.order))


def local(
    activations,
    conditioning,
    cotangent,
    block_targets,
    up_gain,
    norm1_gain,
    norm1_shift,
    w_qkv,
    b_qv,
    w_out,
    b_out,
    norm2_gain,
    norm2_shift,
    w_fc1,
    b_fc1,
    w_fc2,
    b_fc2,
):
    micro, rows, model = activations.shape
    head_cols = w_qkv.shape[2]
    hidden_cols = w_fc1.shape[1]
    dp_size, head_size = lax.axis_size("dp"), lax.axis_size("head")
    me, here = lax.axis_index("dp"), lax.axis_index("head")
    group = head_size // micro
    tokens = rows * micro
    blocks = tokens // BLOCK
    slab = model // dp_size
    masks = [1 << i for i in range(1, dp_size.bit_length() - 1)]
    heads_all, hidden_all = head_cols * head_size, hidden_cols * head_size

    src_rank = here % micro
    my_micro, my_sub = here // group, here % group
    shifts = [
        [(hs * micro + hr, ((hr + s) % micro) * group + hs) for hs in range(group) for hr in range(micro)]
        for s in range(micro)
    ]

    def send(value, pairs):
        return value if all(a == b for a, b in pairs) else lax.ppermute(value, "head", pairs)

    def choose(options, index):
        out = options[-1]
        for k in range(len(options) - 1):
            out = jnp.where(index == k, options[k], out)
        return out

    def to_micro(value):
        return [
            lax.dynamic_index_in_dim(value, (src_rank + s) % micro, 0, False) for s in range(micro)
        ]

    def sent(pieces, *others):
        pieces = lax.optimization_barrier(tuple(pieces) + others)[: len(pieces)]
        return [send(piece, pairs) for piece, pairs in zip(pieces, shifts)]

    def in_rank_order(got):
        return jnp.concatenate([choose(got, (my_micro - p) % micro) for p in range(micro)], axis=0)

    def from_micro(value):
        pieces = value.reshape(micro, rows, -1)
        return [
            lax.dynamic_index_in_dim(pieces, (my_micro - s) % micro, 0, False) for s in range(micro)
        ]

    def back(pieces):
        return [send(piece, [(b, a) for a, b in pairs]) for piece, pairs in zip(pieces, shifts)]

    def in_micro_order(got):
        return jnp.stack([choose(got, (m - src_rank) % micro) for m in range(micro)])

    def my_slab(value, axis):
        return lax.dynamic_slice_in_dim(value, me * slab, slab, axis)

    tie = Order()
    hc, fc = head_cols, hidden_cols
    half = model // 2

    small = jnp.concatenate([b_qv.reshape(-1), b_fc1])
    per_row = 4 * hc
    small_rows = -(-small.shape[0] // per_row)
    padded = jnp.pad(small, (0, small_rows * per_row - small.shape[0])).reshape(small_rows, per_row)
    thirds, rest = [], padded
    for _ in range(3):
        third = lax.reduce_precision(rest, 8, 7)
        thirds.append(third.astype(bf16))
        rest = rest - third
    extra = jnp.pad(jnp.concatenate(thirds), ((0, 16 - 3 * small_rows), (0, 0)))
    strip_a = jnp.concatenate(
        [my_slab(w_qkv[0], 0), my_slab(w_qkv[1], 0), my_slab(w_qkv[2], 0), my_slab(w_out, 1).T],
        axis=1,
    )
    strip_a = jnp.concatenate([strip_a, extra], axis=0)
    tie.mark(strip_a)
    head_masks = [1 << i for i in range(head_size.bit_length() - 1)]
    head_places = [0]
    for mask in head_masks[::-1]:
        head_places = head_places + [p ^ mask for p in head_places]

    class HeadGather:
        def __init__(self, strip):
            self.held, self.masks = strip[None], head_masks[::-1]
            self.send()

        def send(self):
            self.got = xor_swap(self.held, "head", self.masks.pop(0))

        def step(self):
            self.held = jnp.concatenate([tie(self.held), self.got], axis=0)
            tie.mark(self.held)
            if self.masks:
                self.send()
                return True
            return False

        def slots(self):
            while self.step():
                tie.pause()
            return [self.held[head_places.index(s)] for s in range(1, head_size)]

    gather_a = HeadGather(strip_a)
    acts_out = to_micro(tie(jnp.concatenate([activations, conditioning], axis=1)))
    tie.mark(*acts_out)
    tie.pause()
    gather_a.step()
    strip_f = jnp.concatenate([my_slab(tie(w_fc1), 0), my_slab(w_fc2, 1).T], axis=1)
    own_two_t = tie(w_fc2).T
    own_out_t = tie(w_out).T
    up_tile = jnp.broadcast_to(tie(up_gain)[None], (rows // UP, UP, model)).reshape(rows, model)
    cot_out = to_micro(tie(cotangent))
    tie.mark(strip_f, own_two_t, own_out_t, up_tile, *cot_out)
    tie.pause()
    slots_a = gather_a.slots()
    dp_orders = (masks, masks[::-1])
    dp_index = jnp.stack([me, here]).astype(jnp.int32)

    def colors_of(slots):
        rows_half = slab // 2
        held = [
            jnp.stack([v[c * rows_half : (c + 1) * rows_half] for v in slots])[None] for c in (0, 1)
        ]
        tie.mark(*held)
        return held

    def swap_stage(held, step):
        return [xor_swap(v, "dp", order[step]) for v, order in zip(held, dp_orders)]

    def widen(held, got):
        wider = [jnp.concatenate([a, b], axis=0) for a, b in zip(tie(*held), got)]
        tie.mark(*wider)
        return wider

    held_a = colors_of(tie(*slots_a))
    got_a = swap_stage(held_a, 0)
    got_acts = sent(acts_out, *held_a)
    for step in range(1, len(masks)):
        tie.pause()
        held_a = widen(held_a, got_a)
        got_a = swap_stage(held_a, step)
    tie.pause()
    held_a = widen(held_a, got_a)
    tables_a = held_a + [xor_swap(v, "dp", 1) for v in held_a]
    joined, normed, coarse = join(
        my_micro.reshape(1).astype(jnp.int32),
        tie(*got_acts),
        up_tile,
        norm1_gain.reshape(1, -1),
        norm1_shift.reshape(1, -1),
    )
    tie.mark(normed)

    stages_sub = [("head", 1 << i) for i in range(group.bit_length() - 1)]
    stage_lists = [stages_sub + [("dp", m) for m in order] for order in dp_orders]
    stages = len(stage_lists[0])
    shaped = tie(normed).reshape(blocks, BLOCK, model)
    far_held = [shaped[:, :, c * half : (c + 1) * half] for c in (0, 1)]
    tie.mark(*far_held)
    far_got = [xor_swap(v, *stage_lists[c][0]) for c, v in enumerate(far_held)]
    gather_f = HeadGather(tie(strip_f))
    for step in range(1, stages):
        tie.pause()
        far_held = widen(far_held, far_got)
        far_got = [xor_swap(v, *stage_lists[c][step]) for c, v in enumerate(far_held)]
    gather_f.step()
    limit = far_held[0].shape[0]
    table_row = lax.dynamic_index_in_dim(block_targets, my_micro, 0, False)

    def targets_of(device):
        return lax.dynamic_slice_in_dim(table_row, (device * group + my_sub) * blocks, blocks)

    targets = targets_of(me)
    targets_both = jnp.concatenate([targets, targets_of(me ^ 1)])
    owner = jnp.maximum(targets_both, 0) // blocks
    away = (owner // group) ^ me
    away_sub = (owner % group) ^ my_sub

    def table_index(stage_list):
        index = jnp.zeros_like(owner)
        for bit, (axis, mask) in enumerate(stage_list):
            far_bits = away if axis == "dp" else away_sub
            index = index + (((far_bits & mask) != 0).astype(jnp.int32) << bit)
        return index * blocks + jnp.maximum(targets_both, 0) % blocks

    index_a, index_b = table_index(stage_lists[0]), table_index(stage_lists[1])
    on_my_core = (away & 1) == 0
    has_far = (targets >= 0).astype(jnp.int32)
    valid = on_my_core & (targets_both >= 0)
    route_a = jnp.where(valid, index_a, -1)
    route_b = jnp.where(valid, index_b, -1)

    biases = [small]
    for value in slots_a:
        rows3 = value[slab : slab + 3 * small_rows].astype(f32).reshape(3, -1)
        biases.append(rows3[0] + rows3[1] + rows3[2])
    bias_q = jnp.concatenate([b[:hc] for b in biases])
    bias_v = jnp.concatenate([b[hc : 2 * hc] for b in biases])
    bias_one = jnp.concatenate([b[2 * hc : 2 * hc + fc] for b in biases])
    bias_kv = jnp.concatenate([jnp.zeros_like(bias_v), bias_v])
    w_qkv_all, w_out_t = assemble(
        dp_index,
        list(tie(*tables_a)),
        [w_qkv[0], w_qkv[1], w_qkv[2], own_out_t],
        [(t * hc, hc, 0, t * heads_all) for t in range(3)] + [(3 * hc, hc, 1, 0)],
        masks,
        [3 * heads_all, heads_all],
    )
    tie.mark(w_qkv_all, w_out_t)
    qkv = (mm(normed, w_qkv_all) + jnp.concatenate([bias_q, bias_kv])).astype(bf16)
    tie.mark(qkv)

    tie.pause()
    kept, passed = far_pick(list(zip(tie(*far_held), far_got)), index_a, index_b)
    tie.mark(kept, passed)
    passed_got = xor_swap(passed, "dp", 1)
    tie.pause()
    held_f = colors_of(gather_f.slots())
    got_f = swap_stage(held_f, 0)
    got_cot = sent(cot_out, passed_got)
    passed = passed_got
    for step in range(1, len(masks)):
        tie.pause()
        held_f = widen(held_f, got_f)
        got_f = swap_stage(held_f, step)
    far = jnp.where(on_my_core[:blocks, None, None], tie(kept), passed).reshape(tokens, model)
    kv_far = (mm(far, w_qkv_all[:, heads_all:]) + bias_kv).astype(bf16)
    tie.mark(kv_far)
    attended = attention_forward(has_far, qkv, tie(kv_far), heads_all)
    tie.mark(attended, *got_cot[1::2])
    residual = joined + (mm_nt(tie(attended), w_out_t) + b_out)
    normed2_f, standard_two, inverse_two = norm_forward(residual, norm2_gain, norm2_shift)
    normed_two = normed2_f.astype(bf16)
    tie.mark(residual, normed_two)

    incoming = in_rank_order(tie(*got_cot))
    incoming_f = incoming.astype(f32)
    grad_b2 = jnp.sum(incoming_f, axis=0, keepdims=True)
    normed_t, far_t = tie(normed).T, tie(far).T
    incoming_t, normed_two_t = incoming.T, tie(normed_two).T
    tie.mark(grad_b2, normed_t, far_t, incoming_t, normed_two_t)
    tie.pause()
    got_f = list(tie(*got_f))
    tables_f = [v for pair in zip(held_f, got_f) for v in pair]
    held_core = [xor_swap(v, "dp", 1) for v in held_f]
    got_core = [xor_swap(v, "dp", 1) for v in got_f]
    tables_f += [v for pair in zip(held_core, got_core) for v in pair]

    shape = jax.ShapeDtypeStruct
    slope, out, keep_two, send_two = feed_call(
        feed_forward_kernel,
        masks,
        dp_index,
        tables_f,
        w_fc1,
        own_two_t,
        0,
        [
            (normed_two, None),
            (bias_one.reshape(1, -1), (0, False)),
            (residual, None),
            (b_fc2.reshape(1, -1), None),
            (incoming_t, None),
        ],
        [(shape((tokens, hidden_all), bf16), (1, False)), (shape((tokens, model), bf16), None)],
        [pltpu.VMEM((tokens, model), f32)],
    )
    tie.mark(slope)
    got_two = xor_swap(send_two, "dp", 1)

    reversed_bits = [
        sum(m for m, back_m in zip(head_masks, head_masks[::-1]) if p & back_m) for p in range(head_size)
    ]

    class HeadSum:
        def __init__(self, piece):
            self.held = jnp.stack([piece(here ^ p) for p in reversed_bits])
            tie.mark(self.held)
            self.masks = list(head_masks)
            self.send()

        def send(self):
            half = self.held.shape[0] // 2
            self.got = xor_swap(self.held[half:], "head", self.masks.pop(0))

        def step(self):
            half = self.held.shape[0] // 2
            total = tie(self.held)[:half].astype(f32) + self.got.astype(f32)
            if half == 1:
                return total[0]
            self.held = total.astype(bf16)
            tie.mark(self.held)
            self.send()
            return None

        def finish(self):
            out = None
            while out is None:
                out = self.step()
            return out

    class Steps:
        def tokens_out(self):
            out_pieces = from_micro(tie(out))
            tie.mark(*out_pieces)
            self.got_out = back(out_pieces)

        def feed(self):
            self.grad_b1, self.grad_two, self.keep_one, self.send_one = feed_call(
                feed_backward_kernel,
                masks,
                dp_index,
                tables_f,
                own_two_t,
                w_fc1,
                1,
                [(tie(incoming), None), (slope, (1, False)), (normed_two_t, None)],
                [(shape((1, hidden_all), f32), (1, True)), (shape((tokens, model), f32), None)],
                [],
            )
            tie.mark(self.grad_b1)
            self.got_one = xor_swap(self.send_one, "dp", 1)

        def halves(self, keep, got):
            return [
                DpSum(tie, (keep, got), dp_orders[c], c * head_size, head_size)
                for c in range(HALVES)
            ]

        def two_first(self):
            self.sums_two = self.halves(keep_two, got_two)
            for part in self.sums_two:
                part.stage(0)

        def norm(self):
            grad_res_part, self.grad_g2, self.grad_s2 = norm_backward(
                tie(self.grad_two), standard_two, inverse_two, norm2_gain
            )
            self.grad_residual = incoming_f + grad_res_part
            self.grad_branch = self.grad_residual.astype(bf16)
            self.grad_bo = jnp.sum(self.grad_branch.astype(f32), axis=0)
            self.grad_att = mm(self.grad_branch, w_out_t).astype(bf16)
            tie.mark(self.grad_att)

        def attention(self):
            self.grad_qkv = attention_backward(has_far, qkv, kv_far, tie(self.grad_att))
            tie.mark(self.grad_qkv)

        def one_first(self):
            self.sums_one = self.halves(self.keep_one, self.got_one)
            for part in self.sums_one:
                part.stage(0)

        def far_back(self):
            self.far_rows = (
                mm_nt(tie(self.grad_qkv)[1, :, heads_all:], w_qkv_all[:, heads_all:])
                .astype(bf16)
                .reshape(blocks, BLOCK, model)
            )
            tie.mark(self.far_rows)
            self.far_other = xor_swap(self.far_rows, "dp", 1)

        def branch(self):
            self.branch_t = tie(self.grad_branch).T
            tie.mark(self.branch_t)

        def route(self):
            routed = far_route(tie(self.far_rows), self.far_other, route_a, route_b, limit)
            tie.mark(*routed)
            self.terms = [[routed[0]], [routed[2]]]
            for color in range(2):
                axis, mask = stage_lists[color][-1]
                self.terms[color].append(xor_swap(routed[2 * color + 1], axis, mask))

        def weights(self):
            keep, send_att = attention_weights(
                masks, dp_index, normed_t, far_t, self.branch_t, tie(self.grad_qkv), attended, hc
            )
            tie.mark(send_att)
            got = xor_swap(send_att, "dp", 1)
            groups = 2 * head_size
            self.sums_att = [
                DpSum(tie, (keep, got), dp_orders[c], c * groups, groups) for c in (0, 1)
            ]

        def own(self):
            self.grad_own = mm_nt(tie(self.grad_qkv)[0], w_qkv_all)
            self.grad_bq = jnp.sum(tie(self.grad_qkv)[0, :, :heads_all].astype(f32), axis=0)
            self.grad_bv = jnp.sum(
                tie(self.grad_qkv)[:, :, 2 * heads_all :].astype(f32), axis=(0, 1)
            )
            tie.mark(self.grad_own, self.grad_bq, self.grad_bv)

        def hidden_rest(self):
            for step in range(1, len(masks)):
                for c in range(HALVES):
                    pair = (self.sums_two[c], self.sums_one[c])
                    low, high = pair[0].rows >> (step + 1), pair[0].rows >> step
                    moved = jnp.concatenate([part.upto(low, high) for part in pair], axis=0)
                    tie.mark(moved)
                    moved = xor_swap(moved, "dp", dp_orders[c][step])
                    for i, part in enumerate(pair):
                        part.terms.append((moved, i * head_size))

        def hidden_head(self):
            ends = [part.final() for part in self.sums_two + self.sums_one]
            self.sum_f = HeadSum(
                lambda a: jnp.stack([lax.dynamic_index_in_dim(v, a, 0, False) for v in ends])
            )

        def hidden_step(self):
            self.sum_f.step()

        def far_rest(self):
            for step in range(stages - 2, -1, -1):
                low, high = blocks << step, blocks << (step + 1)
                moved = []
                for color in range(2):
                    value = sum(t[low:high].astype(f32) for t in tie(*self.terms[color]))
                    moved.append(value.astype(bf16))
                tie.mark(*moved)
                for color in range(2):
                    self.terms[color].append(xor_swap(moved[color], *stage_lists[color][step]))

        def att_first(self):
            for part in self.sums_att:
                part.stage(0)

        def att_rest(self):
            for step in range(1, len(masks)):
                for part in self.sums_att:
                    part.stage(step)

        def att_head(self):
            ends = [part.final().reshape(2, head_size, slab, hc) for part in self.sums_att]
            self.sum_att = HeadSum(
                lambda a: jnp.concatenate(
                    [lax.dynamic_index_in_dim(v, a ^ here, 1, False) for v in ends], axis=0
                )
            )

        def att_step(self):
            self.sum_att.step()

        def leave(self):
            self.grad_input, self.grad_up, self.grad_g1, self.grad_s1 = leave(
                tie(self.grad_own),
                joined,
                self.grad_residual,
                coarse,
                norm1_gain.reshape(1, -1),
                *self.terms,
            )
            tie.mark(self.grad_input)

        def tokens_back(self):
            in_pieces = from_micro(tie(self.grad_input))
            tie.mark(*in_pieces)
            self.got_input = back(in_pieces)

        def tokens_end(self):
            self.grad_input = in_micro_order(tie(*self.got_input)).astype(f32)
            self.grad_coarse = jnp.sum(
                self.grad_input.reshape(micro, -1, UP, model) * up_gain, axis=2
            )
            tie.mark(self.grad_input, self.grad_coarse)

        def small(self):
            by_slot = jnp.concatenate(
                [self.grad_bq.reshape(-1, hc), self.grad_bv.reshape(-1, hc)], axis=1
            )
            by_head = jnp.concatenate(
                [choose([by_slot[s] for s in range(head_size)], a ^ here) for a in range(head_size)]
            )
            self.total = jnp.concatenate(
                [tie(self.grad_up), self.grad_g1, self.grad_s1]
                + [v.reshape(1, -1) for v in (self.grad_bo, self.grad_g2, self.grad_s2)]
                + [grad_b2, self.grad_b1.reshape(-1, model), by_head.reshape(-1, model)]
            )
            tie.mark(self.total)
            self.small_stages = [("dp", m) for m in [1] + masks] + [("head", m) for m in head_masks]
            self.small_got = None

        def small_step(self):
            if self.small_got is not None:
                self.total = tie(self.total) + self.small_got
                tie.mark(self.total)
                self.small_got = None
            if self.small_stages:
                self.small_got = xor_swap(self.total, *self.small_stages.pop(0))

        def small_end(self):
            self.small_step()
            while self.small_got is not None:
                tie.pause()
                self.small_step()

        def layer(self):
            self.layer_out = in_micro_order(tie(*self.got_out))
            tie.mark(self.layer_out)

        def wait_out(self):
            tie.mark(*tie.last, *self.got_out)

        def wait_two(self):
            tie.mark(*tie.last, *[part.terms[-1][0] for part in self.sums_two])

        def wait_one(self):
            tie.mark(*tie.last, *[part.terms[-1][0] for part in self.sums_one])

        def wait_att(self):
            tie.mark(*tie.last, *[part.terms[-1][0] for part in self.sums_att])

        def wait_far(self):
            tie.mark(*tie.last, *[t[-1] for t in self.terms])

        def pause(self):
            tie.pause()

        def flush(self):
            tie.flush()

    it = Steps()
    for name in STEPS:
        getattr(it, name)()
    layer_out = it.layer_out
    grad_input, grad_coarse, total = it.grad_input, it.grad_coarse, it.total
    grad_wf, grad_wa = it.sum_f.finish(), it.sum_att.finish()
    grad_w2 = jnp.concatenate([grad_wf[c].T for c in range(HALVES)], axis=0)
    grad_w1 = jnp.concatenate([grad_wf[HALVES + c] for c in range(HALVES)], axis=1)
    grad_wqkv, grad_wo = grad_wa[:3], grad_wa[3].T
    s_g1, s_s1, s_bo, s_g2, s_s2, s_b2 = [total[UP + i] for i in range(6)]
    hidden_rows = hidden_all // model
    s_b1 = total[UP + 6 : UP + 6 + hidden_rows].reshape(-1)
    by_head = total[UP + 6 + hidden_rows :].reshape(head_size, 2 * hc)
    s_bq, s_bv = by_head[:, :hc].reshape(-1), by_head[:, hc:].reshape(-1)
    return (
        layer_out,
        grad_input,
        grad_coarse,
        total[:UP],
        s_g1,
        s_s1,
        grad_wqkv,
        jnp.stack([s_bq, s_bv]),
        grad_wo,
        s_bo,
        s_g2,
        s_s2,
        grad_w1,
        s_b1,
        grad_w2,
        s_b2,
    )


def solution(mesh):
    rows = P(None, ("dp", "head"), None)
    return jax.shard_map(
        local,
        mesh=mesh,
        in_specs=(
            rows,
            rows,
            rows,
            P(),
            P(),
            P(),
            P(),
            P(None, None, "head"),
            P(None, "head"),
            P("head", None),
            P(),
            P(),
            P(),
            P(None, "head"),
            P("head"),
            P("head", None),
            P(),
        ),
        out_specs=(
            rows,
            rows,
            rows,
            P(),
            P(),
            P(),
            P(None, "dp", "head"),
            P(),
            P("head", "dp"),
            P(),
            P(),
            P(),
            P("dp", "head"),
            P(),
            P("head", "dp"),
            P(),
        ),
        check_vma=False,
    )
```

```python
import functools
import math

import jax
import jax.numpy as jnp
from jax import lax
from jax.experimental import pallas as pl
from jax.experimental.pallas import tpu as pltpu
from jax.sharding import PartitionSpec as P

HEAD_DIM = 64
BLOCK = 128
UP = 4
HALVES = 2
VMEM_LIMIT = 58 << 20
STEPS = ["tokens_out", "feed", "two_first", "one_first", "norm", "attention", "far_back", "hidden_rest", "branch", "pause", "route", "weights", "hidden_head", "own", "pause", "far_rest", "att_first", "layer", "pause", "leave", "att_rest", "tokens_back", "pause", "pause", "pause", "small", "hidden_step", "att_head", "tokens_end", "pause", "att_step", "small_step", "small_end"]
PAIR = 2 * HEAD_DIM
NEGATIVE = -1e30
epsilon = 1e-05
f32 = jnp.float32
bf16 = jnp.bfloat16
ROOT_2_PI = math.sqrt(2.0 / math.pi)
LONG_COST = pl.CostEstimate(flops=1 << 36, bytes_accessed=1 << 26, transcendentals=0)


def xor_swap(value, axis, mask):
    size = lax.axis_size(axis)
    return lax.ppermute(value, axis, [(i, i ^ mask) for i in range(size)])


def pause_kernel(value_ref, out_ref):
    out_ref[...] = value_ref[...]


class Order:
    def __init__(self):
        self.last = ()
        self.token = None

    def __call__(self, *values):
        tied = lax.optimization_barrier(tuple(values) + self.last)[: len(values)]
        return tied[0] if len(values) == 1 else tied

    def mark(self, *values):
        self.last = values

    def flush(self):
        tied = self(jnp.zeros((8, 128), f32) if self.token is None else self.token)
        self.token = xor_swap(tied, "dp", 1)
        self.mark(self.token)

    def pause(self):
        self.token = self(jnp.zeros((8, 128), f32) if self.token is None else self.token)
        self.token = pl.pallas_call(
            pause_kernel, out_shape=jax.ShapeDtypeStruct((8, 128), f32), cost_estimate=LONG_COST
        )(self.token)
        self.mark(self.token)


def norm_forward(values, gain, shift):
    centered = values - jnp.mean(values, axis=-1, keepdims=True)
    inverse = lax.rsqrt(jnp.mean(centered * centered, axis=-1, keepdims=True) + epsilon)
    standard = centered * inverse
    return (standard * gain + shift, standard, inverse)


def norm_backward(upstream, standard, inverse, gain):
    scaled = upstream * gain
    inner = (
        scaled
        - jnp.mean(scaled, axis=-1, keepdims=True)
        - standard * jnp.mean(scaled * standard, axis=-1, keepdims=True)
    )
    return (inner * inverse, jnp.sum(upstream * standard, axis=0), jnp.sum(upstream, axis=0))


def mm(left, right):
    return jnp.dot(left, right, preferred_element_type=f32)


def mm_nt(left, right):
    return lax.dot_general(left, right, (((1,), (1,)), ((), ())), preferred_element_type=f32)


def mm_tn(left, right):
    return lax.dot_general(left, right, (((0,), (0,)), ((), ())), preferred_element_type=f32)


def pair_probs(q_pair, k_cat, allowed):
    low_half = lax.broadcasted_iota(jnp.int32, (BLOCK, PAIR), 1) < HEAD_DIM
    zero = jnp.zeros_like(q_pair)
    q_pair = q_pair * jnp.asarray(1.0 / math.sqrt(HEAD_DIM), q_pair.dtype)
    q_stack = jnp.concatenate(
        [jnp.where(low_half, q_pair, zero), jnp.where(low_half, zero, q_pair)], axis=0
    )
    scores = mm_nt(k_cat, q_stack)
    scores = jnp.where(allowed, scores, NEGATIVE)
    top = jnp.max(scores, axis=0, keepdims=True)
    raised = jnp.exp(scores - top)
    probs = raised * (1.0 / jnp.sum(raised, axis=0, keepdims=True))
    return q_stack, probs, low_half


def allowed_mask(far_flag):
    key_at = lax.broadcasted_iota(jnp.int32, (2 * BLOCK, 2 * BLOCK), 0)
    query_at = lax.broadcasted_iota(jnp.int32, (2 * BLOCK, 2 * BLOCK), 1)
    query_at = jnp.where(query_at >= BLOCK, query_at - BLOCK, query_at)
    first = jnp.where(far_flag > 0, BLOCK, 2 * BLOCK)
    return (key_at <= query_at) | (key_at >= first)


def pair_columns(p, width):
    return [slice(t * width + p * PAIR, t * width + (p + 1) * PAIR) for t in range(3)]


def key_value(own_ref, far_ref, columns, width):
    out = []
    for cols in columns[1:]:
        far_cols = slice(cols.start - width, cols.stop - width)
        out.append(jnp.concatenate([own_ref[:, cols], far_ref[:, far_cols]], axis=0))
    return out


def attention_forward_kernel(pairs, has_far, own_ref, far_ref, out_ref):
    allowed = allowed_mask(has_far[pl.program_id(0)])
    width = pairs * PAIR
    for p in range(pairs):
        columns = pair_columns(p, width)
        k_cat, v_cat = key_value(own_ref, far_ref, columns, width)
        _, probs, low_half = pair_probs(own_ref[:, columns[0]], k_cat, allowed)
        mixed = mm_tn(probs.astype(bf16), v_cat)
        out_ref[:, columns[0]] = jnp.where(low_half, mixed[:BLOCK], mixed[BLOCK:]).astype(bf16)


def attention_forward(has_far, own, far, width):
    blocks = has_far.shape[0]
    row_block = lambda array: pl.BlockSpec((BLOCK, array.shape[1]), lambda b, flags: (b, 0))
    shape = jax.ShapeDtypeStruct((blocks * BLOCK, width), bf16)
    return pl.pallas_call(
        functools.partial(attention_forward_kernel, width // PAIR),
        grid_spec=pltpu.PrefetchScalarGridSpec(
            num_scalar_prefetch=1,
            grid=(blocks,),
            in_specs=[row_block(own), row_block(far)],
            out_specs=row_block(shape),
        ),
        out_shape=shape,
        compiler_params=pltpu.CompilerParams(vmem_limit_bytes=16 << 20),
        cost_estimate=LONG_COST,
    )(has_far, own, far)


def attention_backward_kernel(pairs, has_far, own_ref, far_ref, grad_ref, out_ref):
    allowed = allowed_mask(has_far[pl.program_id(0)])
    width = pairs * PAIR
    scale = 1.0 / math.sqrt(HEAD_DIM)
    out_ref[1, :, :width] = jnp.zeros((BLOCK, width), bf16)
    for p in range(pairs):
        columns = pair_columns(p, width)
        k_cat, v_cat = key_value(own_ref, far_ref, columns, width)
        q_stack, probs, low_half = pair_probs(own_ref[:, columns[0]], k_cat, allowed)
        grad = grad_ref[:, columns[0]]
        zero = jnp.zeros_like(grad)
        grad_stack = jnp.concatenate(
            [jnp.where(low_half, grad, zero), jnp.where(low_half, zero, grad)], axis=0
        )
        grad_probs = mm_nt(v_cat, grad_stack)
        total = jnp.sum(probs * grad_probs, axis=0, keepdims=True)
        grad_scores = (probs * (grad_probs - total)).astype(bf16)
        dq = mm_tn(grad_scores, k_cat)
        dq = jnp.where(low_half, dq[:BLOCK], dq[BLOCK:]) * scale
        out_ref[0, :, columns[0]] = dq.astype(bf16)
        dk = mm(grad_scores, q_stack).astype(bf16)
        dv = mm(probs.astype(bf16), grad_stack).astype(bf16)
        for half in range(2):
            rows = slice(half * BLOCK, (half + 1) * BLOCK)
            out_ref[half, :, columns[1]] = dk[rows]
            out_ref[half, :, columns[2]] = dv[rows]


def attention_backward(has_far, own, far, grad):
    blocks, width = has_far.shape[0], grad.shape[1]
    row_block = lambda array: pl.BlockSpec((BLOCK, array.shape[1]), lambda b, flags: (b, 0))
    return pl.pallas_call(
        functools.partial(attention_backward_kernel, width // PAIR),
        grid_spec=pltpu.PrefetchScalarGridSpec(
            num_scalar_prefetch=1,
            grid=(blocks,),
            in_specs=[row_block(own), row_block(far), row_block(grad)],
            out_specs=pl.BlockSpec((2, BLOCK, 3 * width), lambda b, flags: (0, b, 0)),
        ),
        out_shape=jax.ShapeDtypeStruct((2, blocks * BLOCK, 3 * width), bf16),
        compiler_params=pltpu.CompilerParams(vmem_limit_bytes=20 << 20),
        cost_estimate=LONG_COST,
    )(has_far, own, far, grad)


def join_kernel(rows, first, *refs):
    got, (tile_ref, gain_ref, shift_ref, joined_ref, normed_ref, coarse_ref, held_ref) = (
        refs[:-7],
        refs[-7:],
    )
    pieces = len(got)
    which = (first[0] + pieces - pl.program_id(0)) % pieces
    for s in range(pieces):

        @pl.when(which == s)
        def _():
            held_ref[...] = got[s][...]

    coarse = held_ref[rows:, :]
    coarse_ref[...] = coarse
    up_row = lax.broadcasted_iota(jnp.int32, (rows, rows // UP), 0) // UP
    up_col = lax.broadcasted_iota(jnp.int32, (rows, rows // UP), 1)
    spread = mm((up_row == up_col).astype(f32).astype(bf16), coarse)
    joined = held_ref[:rows, :].astype(f32) + spread * tile_ref[...]
    joined_ref[...] = joined
    normed_ref[...] = norm_forward(joined, gain_ref[...], shift_ref[...])[0].astype(bf16)


def join(first, got, tile, gain, shift):
    pieces, rows, model = len(got), tile.shape[0], tile.shape[1]
    small = rows // UP
    fixed = lambda array: pl.BlockSpec(array.shape, lambda p, f: (0, 0))
    piece = lambda count: pl.BlockSpec((count, model), lambda p, f: (p, 0))
    return pl.pallas_call(
        functools.partial(join_kernel, rows),
        grid_spec=pltpu.PrefetchScalarGridSpec(
            num_scalar_prefetch=1,
            grid=(pieces,),
            in_specs=[fixed(g) for g in got] + [fixed(tile), fixed(gain), fixed(shift)],
            out_specs=[piece(rows), piece(rows), piece(small)],
            scratch_shapes=[pltpu.VMEM((rows + small, model), bf16)],
        ),
        out_shape=[
            jax.ShapeDtypeStruct((pieces * rows, model), f32),
            jax.ShapeDtypeStruct((pieces * rows, model), bf16),
            jax.ShapeDtypeStruct((pieces * small, model), bf16),
        ],
        compiler_params=pltpu.CompilerParams(vmem_limit_bytes=16 << 20),
        cost_estimate=LONG_COST,
    )(first, *got, tile, gain, shift)


def fill_chunk(masks, me, tables, out_ref):
    half, count = tables[0].shape[2], tables[0].shape[0]
    for which, table in enumerate(tables):
        core, color, late = which // 4, which // 2 % 2, which % 2
        order = masks if color == 0 else masks[::-1]
        for k, mask in enumerate(relative_masks(order)[late * count : (late + 1) * count]):
            row = (me ^ (mask | core)) * 2 * half + color * half
            out_ref[pl.ds(pl.multiple_of(row, half), half), :] = table[k, 0]


def load_chunk(masks, me, chunk, n_own, own_ref, tables, out_ref):
    @pl.when(chunk < n_own)
    def _():
        out_ref[...] = own_ref[...]

    @pl.when(chunk >= n_own)
    def _():
        fill_chunk(masks, me, tables, out_ref)


def by_stage(step, n, buffers, begin, body, end):
    @pl.when(step == 0)
    def _():
        begin(buffers[0])

    for parity in range(2):

        @pl.when((step % 2 == parity) & (step > 0) & (step < n))
        def _():
            body(buffers[1 - parity], buffers[parity])

    @pl.when(step == n)
    def _():
        end(buffers[(n + 1) % 2])


def scatter_rows(masks, color, me, value, held_ref):
    count = 2 << len(masks)
    slab = value.shape[0] // count
    last = len(masks) - 1
    for b in range(count):
        away = me ^ b
        at = (away & 1) << len(masks)
        for i, mask in enumerate(masks):
            place = last - i if isinstance(color, int) and color == 0 else i
            if not isinstance(color, int):
                place = jnp.where(color == 0, last - i, i)
            at = at + (((away >> (mask.bit_length() - 1)) & 1) << place)
        row = pl.multiple_of(at * slab, slab)
        held_ref[pl.ds(row, slab), :] = value[b * slab : (b + 1) * slab].astype(bf16)


def split_rows(held_ref, keep_ref, send_ref):
    half = held_ref.shape[0] // 2
    keep_ref[0] = held_ref[:half, :]
    send_ref[0] = held_ref[half:, :]


def feed_forward_kernel(masks, n_own, n, me, *refs):
    one_tables, two_tables, refs = refs[:8], refs[8:16], refs[16:]
    (own_one, own_two, x_ref, bias_ref, residual_ref, last_ref, left_ref) = refs[:7]
    slope_ref, out_ref, keep_ref, send_ref = refs[7:11]
    w_one, w_two, even_ref, odd_ref, act_ref, held_ref, acc_ref = refs[11:]
    step = pl.program_id(0)
    load_chunk(masks, me[0], jnp.minimum(step, n - 1), n_own, own_one, one_tables, w_one)
    load_chunk(masks, me[0], jnp.maximum(step - 1, 0), n_own, own_two, two_tables, w_two)
    ratio = ROOT_2_PI * 0.044715
    rows = x_ref.shape[0] // 3

    parts = [slice(r * rows, (r + 1) * rows) for r in range(3)]

    def finish(at, before):
        h = before[at, :]
        square = h * h
        gate = 0.5 + 0.5 * jnp.tanh(h * (ROOT_2_PI + ratio * square))
        act = (h * gate).astype(bf16)
        act_ref[at, :] = act
        slope_ref[at, :] = (
            gate * (1.0 + 2.0 * h * (1.0 - gate) * (ROOT_2_PI + 3.0 * ratio * square))
        ).astype(bf16)
        return act

    def start(at, now):
        now[at, :] = mm(x_ref[at, :], w_one[...]) + bias_ref[...]

    def gradient():
        color = jnp.maximum(step - 1, 0) % n_own
        scatter_rows(masks, color, me[0], mm(left_ref[...], act_ref[...]), held_ref)

    def begin(now):
        acc_ref[...] = jnp.zeros_like(acc_ref)
        for at in parts:
            start(at, now)

    def body(before, now):
        for at in parts:
            act = finish(at, before)
            start(at, now)
            acc_ref[at, :] += mm_nt(act, w_two[...])
        gradient()

    def end(before):
        for at in parts:
            act = finish(at, before)
            acc_ref[at, :] += mm_nt(act, w_two[...])
        gradient()

    by_stage(step, n, (even_ref, odd_ref), begin, body, end)
    split_rows(held_ref, keep_ref, send_ref)

    @pl.when(step == n)
    def _():
        out_ref[...] = (residual_ref[...] + (acc_ref[...] + last_ref[...])).astype(bf16)


def feed_backward_kernel(masks, n_own, n, me, *refs):
    two_tables, one_tables, refs = refs[:8], refs[8:16], refs[16:]
    own_two, own_one, g_ref, slope_ref, left_ref = refs[:5]
    bias_ref, out_ref, keep_ref, send_ref = refs[5:9]
    w_two, w_one, even_ref, odd_ref, grad_ref, held_ref = refs[9:]
    step = pl.program_id(0)
    load_chunk(masks, me[0], jnp.minimum(step, n - 1), n_own, own_two, two_tables, w_two)
    load_chunk(masks, me[0], jnp.maximum(step - 1, 0), n_own, own_one, one_tables, w_one)
    rows = g_ref.shape[0] // 2

    parts = [slice(r * rows, (r + 1) * rows) for r in range(2)]

    def start(at, now):
        now[at, :] = mm(g_ref[at, :], w_two[...])

    def finish(at, before):
        grad = (before[at, :] * slope_ref[at, :].astype(f32)).astype(bf16)
        grad_ref[at, :] = grad
        out_ref[at, :] += mm_nt(grad, w_one[...])
        return jnp.sum(grad.astype(f32), axis=0, keepdims=True)

    def gradient(sums):
        bias_ref[...] = sums[0] + sums[1]
        color = jnp.maximum(step - 1, 0) % n_own
        scatter_rows(masks, color, me[0], mm(left_ref[...], grad_ref[...]), held_ref)

    def begin(now):
        out_ref[...] = jnp.zeros_like(out_ref)
        for at in parts:
            start(at, now)

    def body(before, now):
        sums = []
        for at in parts:
            start(at, now)
            sums.append(finish(at, before))
        gradient(sums)

    def end(before):
        gradient([finish(at, before) for at in parts])

    by_stage(step, n, (even_ref, odd_ref), begin, body, end)
    split_rows(held_ref, keep_ref, send_ref)


def feed_call(kernel, masks, me, tables, own_first, own_second, first_part, arrays, outs, scratch):
    count, slots, half, both = tables[0].shape
    model, width = own_first.shape
    n_own = HALVES
    chunk = width // n_own
    n = n_own * (slots + 1)

    def at(j, lag):
        return jnp.clip(j - lag, 0, n - 1)

    def by_head(j, lag, me):
        c = at(j, lag)
        return ((c // n_own) ^ me[1]) * n_own + c % n_own

    def by_half(j, me):
        c = at(j, 1)
        return c % n_own * (slots + 1) + ((c // n_own) ^ me[1])

    def table_spec(part, lag):
        def index(j, me):
            c = jnp.maximum(at(j, lag), n_own)
            return (0, c // n_own - 1, 0, part * n_own + c % n_own)

        return pl.BlockSpec((count, 1, half, chunk), index)

    def own_spec(lag):
        return pl.BlockSpec((model, chunk), lambda j, me: (0, jnp.minimum(at(j, lag), n_own - 1)))

    def spec(array, lag):
        if lag is None:
            return pl.BlockSpec(array.shape, lambda j, me: (0, 0))
        lag, absolute = lag
        return pl.BlockSpec(
            (array.shape[0], chunk), lambda j, me: (0, by_head(j, lag, me) if absolute else at(j, lag))
        )

    rows = arrays[0][0].shape[0]
    weight = jax.ShapeDtypeStruct((n, model // 2, chunk), bf16)
    weight_spec = pl.BlockSpec((1, model // 2, chunk), lambda j, me: (by_half(j, me), 0, 0))
    return pl.pallas_call(
        functools.partial(kernel, masks, n_own, n),
        grid_spec=pltpu.PrefetchScalarGridSpec(
            num_scalar_prefetch=1,
            grid=(n + 1,),
            in_specs=[table_spec(first_part, 0)] * 8
            + [table_spec(1 - first_part, 1)] * 8
            + [own_spec(0), own_spec(1)]
            + [spec(a, lag) for a, lag in arrays],
            out_specs=[spec(o, lag) for o, lag in outs] + [weight_spec, weight_spec],
            scratch_shapes=[
                pltpu.VMEM((model, chunk), bf16),
                pltpu.VMEM((model, chunk), bf16),
                pltpu.VMEM((rows, chunk), f32),
                pltpu.VMEM((rows, chunk), f32),
                pltpu.VMEM((rows, chunk), bf16),
                pltpu.VMEM((model, chunk), bf16),
            ]
            + scratch,
        ),
        out_shape=[o for o, _ in outs] + [weight, weight],
        compiler_params=pltpu.CompilerParams(vmem_limit_bytes=54 << 20),
        cost_estimate=LONG_COST,
    )(me, *tables, *tables, own_first, own_second, *[a for a, _ in arrays])


def far_pick_kernel(limit, where_a, where_b, *refs):
    ins, outs = refs[:8], refs[8:]
    count, half = pl.num_programs(0), ins[0].shape[2]
    for who in range(2):
        for color, where_ref in enumerate((where_a, where_b)):
            held, got = ins[4 * who + 2 * color : 4 * who + 2 * color + 2]
            beyond = where_ref[pl.program_id(0) + who * count] >= limit
            outs[who][0, :, color * half : (color + 1) * half] = jnp.where(beyond, got[0], held[0])


def far_pick(tables, where_a, where_b):
    count = where_a.shape[0] // 2
    limit, _, half = tables[0][0].shape

    def spec(who, color):
        def index(j, wa, wb):
            return ((wa, wb)[color][j + who * count] % limit, 0, 0)

        return pl.BlockSpec((1, BLOCK, half), index)

    out = pl.BlockSpec((1, BLOCK, 2 * half), lambda j, wa, wb: (j, 0, 0))
    shape = jax.ShapeDtypeStruct((count, BLOCK, 2 * half), bf16)
    return pl.pallas_call(
        functools.partial(far_pick_kernel, limit),
        grid_spec=pltpu.PrefetchScalarGridSpec(
            num_scalar_prefetch=2,
            grid=(count,),
            in_specs=[spec(who, color) for who in range(2) for color in range(2) for _ in range(2)],
            out_specs=[out, out],
        ),
        out_shape=[shape, shape],
        compiler_params=pltpu.CompilerParams(vmem_limit_bytes=VMEM_LIMIT),
        cost_estimate=LONG_COST,
    )(where_a, where_b, *[t for _ in range(2) for table in tables for t in table])


def far_route_kernel(count, where_a, where_b, mine_ref, other_ref, *refs):
    outs, acc_ref = refs[:4], refs[4]
    half = outs[0].shape[2]
    acc_ref[...] = jnp.zeros_like(acc_ref)
    for part in range(2):
        step = pl.program_id(0) + part * pl.num_programs(0)
        for source, base in ((mine_ref, 0), (other_ref, count)):
            for j in range(count):

                @pl.when(where_a[base + j] == step)
                def _():
                    acc_ref[part, :, :half] += source[j, :, :half].astype(f32)

                @pl.when(where_b[base + j] == step)
                def _():
                    acc_ref[part, :, half:] += source[j, :, half:].astype(f32)

        outs[part][0] = acc_ref[part, :, :half].astype(bf16)
        outs[2 + part][0] = acc_ref[part, :, half:].astype(bf16)


def far_route(mine, other, where_a, where_b, limit):
    count, _, width = mine.shape
    whole = pl.BlockSpec(mine.shape, lambda k, wa, wb: (0, 0, 0))
    out = pl.BlockSpec((1, BLOCK, width // 2), lambda k, wa, wb: (k, 0, 0))
    shape = jax.ShapeDtypeStruct((limit, BLOCK, width // 2), bf16)
    return pl.pallas_call(
        functools.partial(far_route_kernel, count),
        grid_spec=pltpu.PrefetchScalarGridSpec(
            num_scalar_prefetch=2,
            grid=(limit,),
            in_specs=[whole, whole],
            out_specs=[out] * 4,
            scratch_shapes=[pltpu.VMEM((2, BLOCK, width), f32)],
        ),
        out_shape=[shape] * 4,
        compiler_params=pltpu.CompilerParams(vmem_limit_bytes=18 << 20),
        cost_estimate=LONG_COST,
    )(where_a, where_b, mine, other)


def leave_kernel(n_a, n_b, own_ref, joined_ref, res_ref, coarse_ref, gain_ref, *refs):
    part_a, part_b = refs[:n_a], refs[n_a : n_a + n_b]
    out_ref, up_ref, gain_out, shift_out = refs[n_a + n_b :]

    @pl.when(pl.program_id(0) == 0)
    def _():
        for ref in (up_ref, gain_out, shift_out):
            ref[...] = jnp.zeros_like(ref)

    back = jnp.concatenate(
        [sum(r[0].astype(f32) for r in parts) for parts in (part_a, part_b)], axis=1
    )
    upstream = own_ref[...] + back
    gain = gain_ref[...]
    joined = joined_ref[...]
    _, standard, inverse = norm_forward(joined, gain, gain)
    scaled = upstream * gain
    inner = (
        scaled
        - jnp.mean(scaled, axis=-1, keepdims=True)
        - standard * jnp.mean(scaled * standard, axis=-1, keepdims=True)
    )
    total = res_ref[...] + inner * inverse
    out_ref[...] = total.astype(bf16)
    gain_out[...] += jnp.sum(upstream * standard, axis=0, keepdims=True)
    shift_out[...] += jnp.sum(upstream, axis=0, keepdims=True)
    up_row = lax.broadcasted_iota(jnp.int32, (BLOCK, BLOCK // UP), 0) // UP
    up_col = lax.broadcasted_iota(jnp.int32, (BLOCK, BLOCK // UP), 1)
    weighted = total * mm((up_row == up_col).astype(f32).astype(bf16), coarse_ref[...])
    phase = lax.broadcasted_iota(jnp.int32, weighted.shape, 0) % UP
    for p in range(UP):
        picked = jnp.where(phase == p, weighted, 0.0)
        up_ref[p : p + 1, :] += jnp.sum(picked, axis=0, keepdims=True)


def leave(own, joined, residual, coarse, gain, part_a, part_b):
    tokens, model = own.shape
    rows = pl.BlockSpec((BLOCK, model), lambda b: (b, 0))
    fixed = lambda count: pl.BlockSpec((count, model), lambda b: (0, 0))
    part = pl.BlockSpec((1, BLOCK, model // 2), lambda b: (b, 0, 0))
    return pl.pallas_call(
        functools.partial(leave_kernel, len(part_a), len(part_b)),
        grid=(tokens // BLOCK,),
        in_specs=[rows, rows, rows, pl.BlockSpec((BLOCK // UP, model), lambda b: (b, 0)), fixed(1)]
        + [part] * (len(part_a) + len(part_b)),
        out_specs=[rows, fixed(UP), fixed(1), fixed(1)],
        out_shape=[
            jax.ShapeDtypeStruct((tokens, model), bf16),
            jax.ShapeDtypeStruct((UP, model), f32),
            jax.ShapeDtypeStruct((1, model), f32),
            jax.ShapeDtypeStruct((1, model), f32),
        ],
        compiler_params=pltpu.CompilerParams(vmem_limit_bytes=VMEM_LIMIT),
        cost_estimate=LONG_COST,
    )(own, joined, residual, coarse, gain, *part_a, *part_b)


def relative_masks(masks):
    return [sum(m for bit, m in enumerate(masks) if k >> bit & 1) for k in range(1 << len(masks))]


def assemble_kernel(columns, n_own, n_out, dp_index, *refs):
    tables, own, outs = refs[:4], refs[4 : 4 + n_own], refs[4 + n_own :]
    slots, half = tables[0].shape[1], tables[0].shape[2]

    def fill(first, second):
        for color, table in enumerate((first, second)):
            rows = slice(color * half, (color + 1) * half)
            for c0, width, target, t0 in columns:
                for s in range(slots):
                    at = t0 + (s + 1) * width
                    outs[target][rows, at : at + width] = table[0, s, :, c0 : c0 + width]

    core = pl.program_id(0)

    @pl.when(core == 0)
    def _():
        fill(tables[0], tables[1])

    @pl.when(core == 1)
    def _():
        fill(tables[2], tables[3])

    for ref, (c0, width, target, t0) in zip(own, columns):
        outs[target][:, t0 : t0 + width] = ref[...]


def assemble(dp_index, tables, own, columns, masks, widths):
    bits = len(masks)
    count, slots, half, width = tables[0].shape
    model = 2 * count * 2 * half

    def reverse(k):
        return sum(((k >> i) & 1) << (bits - 1 - i) for i in range(bits))

    def table_spec(which):
        def index(core, k, dp):
            k = jnp.where(core == which // 2, k, 0 if which >= 2 else count - 1)
            return (reverse(k) if which % 2 else k, 0, 0, 0)

        return pl.BlockSpec((1, slots, half, width), index)

    def row(core, k, dp):
        return (dp[0] ^ ((k << 1) | core), 0)

    return pl.pallas_call(
        functools.partial(assemble_kernel, columns, len(own), len(widths)),
        grid_spec=pltpu.PrefetchScalarGridSpec(
            num_scalar_prefetch=1,
            grid=(2, count),
            in_specs=[table_spec(i) for i in range(4)]
            + [pl.BlockSpec((2 * half, o.shape[1]), row) for o in own],
            out_specs=[pl.BlockSpec((2 * half, w), row) for w in widths],
        ),
        out_shape=[jax.ShapeDtypeStruct((model, w), bf16) for w in widths],
        compiler_params=pltpu.CompilerParams(vmem_limit_bytes=16 << 20),
        cost_estimate=LONG_COST,
    )(dp_index, *tables, *own)


def attention_weights_kernel(masks, heads, me, own_t, far_t, branch_t, grad_own, grad_far, attended, *refs):
    keep_ref, send_ref, total_ref, held_ref = refs
    tile = pl.program_id(0)
    kind = tile // heads

    @pl.when(kind == 0)
    def _():
        total_ref[...] = mm(own_t[...], grad_own[...])

    @pl.when((kind == 1) | (kind == 2))
    def _():
        total_ref[...] = mm(own_t[...], grad_own[...]) + mm(far_t[...], grad_far[...])

    @pl.when(kind == 3)
    def _():
        total_ref[...] = mm(branch_t[...], attended[...])

    for color in range(2):

        @pl.when(kind // 2 == color)
        def _():
            scatter_rows(masks, color, me[0], total_ref[...], held_ref)

    split_rows(held_ref, keep_ref, send_ref)


def attention_weights(masks, me, own_t, far_t, branch_t, grad, attended, width):
    model, tokens = own_t.shape
    heads = attended.shape[1] // width
    whole = pl.BlockSpec((model, tokens), lambda j, me: (0, 0))
    part = lambda p: pl.BlockSpec(
        (None, tokens, width), lambda j, me: (p, 0, jnp.minimum(j, 3 * heads - 1))
    )
    out = pl.BlockSpec((1, model // 2, width), lambda j, me: (j, 0, 0))
    shape = jax.ShapeDtypeStruct((4 * heads, model // 2, width), bf16)
    return pl.pallas_call(
        functools.partial(attention_weights_kernel, masks, heads),
        grid_spec=pltpu.PrefetchScalarGridSpec(
            num_scalar_prefetch=1,
            grid=(4 * heads,),
            in_specs=[whole] * 3
            + [
                part(0),
                part(1),
                pl.BlockSpec((tokens, width), lambda j, me: (0, jnp.maximum(j - 3 * heads, 0))),
            ],
            out_specs=[out, out],
            scratch_shapes=[pltpu.VMEM((model, width), f32), pltpu.VMEM((model, width), bf16)],
        ),
        out_shape=[shape, shape],
        compiler_params=pltpu.CompilerParams(vmem_limit_bytes=24 << 20),
        cost_estimate=LONG_COST,
    )(me, own_t, far_t, branch_t, grad, grad, attended)


class DpSum:
    def __init__(self, tie, terms, order, group, count):
        self.tie, self.order = tie, order
        self.terms = [(value, group) for value in terms]
        self.count, self.rows = count, terms[0].shape[1]

    def upto(self, low, high):
        values = self.tie(*[value for value, _ in self.terms])
        total = 0.0
        for value, (_, group) in zip(values, self.terms):
            total = total + value[group : group + self.count, low:high].astype(f32)
        total = total.astype(bf16)
        self.tie.mark(total)
        return total

    def stage(self, step):
        sent = self.upto(self.rows >> (step + 1), self.rows >> step)
        self.terms.append((xor_swap(sent, "dp", self.order[step]), 0))

    def final(self):
        return self.upto(0, self.rows >> len(self.order))


def local(
    activations,
    conditioning,
    cotangent,
    block_targets,
    up_gain,
    norm1_gain,
    norm1_shift,
    w_qkv,
    b_qv,
    w_out,
    b_out,
    norm2_gain,
    norm2_shift,
    w_fc1,
    b_fc1,
    w_fc2,
    b_fc2,
):
    micro, rows, model = activations.shape
    head_cols = w_qkv.shape[2]
    hidden_cols = w_fc1.shape[1]
    dp_size, head_size = lax.axis_size("dp"), lax.axis_size("head")
    me, here = lax.axis_index("dp"), lax.axis_index("head")
    group = head_size // micro
    tokens = rows * micro
    blocks = tokens // BLOCK
    slab = model // dp_size
    masks = [1 << i for i in range(1, dp_size.bit_length() - 1)]
    heads_all, hidden_all = head_cols * head_size, hidden_cols * head_size

    src_rank = here % micro
    my_micro, my_sub = here // group, here % group
    shifts = [
        [(hs * micro + hr, ((hr + s) % micro) * group + hs) for hs in range(group) for hr in range(micro)]
        for s in range(micro)
    ]

    def send(value, pairs):
        return value if all(a == b for a, b in pairs) else lax.ppermute(value, "head", pairs)

    def choose(options, index):
        out = options[-1]
        for k in range(len(options) - 1):
            out = jnp.where(index == k, options[k], out)
        return out

    def to_micro(value):
        return [
            lax.dynamic_index_in_dim(value, (src_rank + s) % micro, 0, False) for s in range(micro)
        ]

    def sent(pieces, *others):
        pieces = lax.optimization_barrier(tuple(pieces) + others)[: len(pieces)]
        return [send(piece, pairs) for piece, pairs in zip(pieces, shifts)]

    def in_rank_order(got):
        return jnp.concatenate([choose(got, (my_micro - p) % micro) for p in range(micro)], axis=0)

    def from_micro(value):
        pieces = value.reshape(micro, rows, -1)
        return [
            lax.dynamic_index_in_dim(pieces, (my_micro - s) % micro, 0, False) for s in range(micro)
        ]

    def back(pieces):
        return [send(piece, [(b, a) for a, b in pairs]) for piece, pairs in zip(pieces, shifts)]

    def in_micro_order(got):
        return jnp.stack([choose(got, (m - src_rank) % micro) for m in range(micro)])

    def my_slab(value, axis):
        return lax.dynamic_slice_in_dim(value, me * slab, slab, axis)

    tie = Order()
    hc, fc = head_cols, hidden_cols
    half = model // 2

    small = jnp.concatenate([b_qv.reshape(-1), b_fc1])
    per_row = 4 * hc
    small_rows = -(-small.shape[0] // per_row)
    padded = jnp.pad(small, (0, small_rows * per_row - small.shape[0])).reshape(small_rows, per_row)
    thirds, rest = [], padded
    for _ in range(3):
        third = lax.reduce_precision(rest, 8, 7)
        thirds.append(third.astype(bf16))
        rest = rest - third
    extra = jnp.pad(jnp.concatenate(thirds), ((0, 16 - 3 * small_rows), (0, 0)))
    strip_a = jnp.concatenate(
        [my_slab(w_qkv[0], 0), my_slab(w_qkv[1], 0), my_slab(w_qkv[2], 0), my_slab(w_out, 1).T],
        axis=1,
    )
    strip_a = jnp.concatenate([strip_a, extra], axis=0)
    tie.mark(strip_a)
    head_masks = [1 << i for i in range(head_size.bit_length() - 1)]
    head_places = [0]
    for mask in head_masks[::-1]:
        head_places = head_places + [p ^ mask for p in head_places]

    class HeadGather:
        def __init__(self, strip):
            self.held, self.masks = strip[None], head_masks[::-1]
            self.send()

        def send(self):
            self.got = xor_swap(self.held, "head", self.masks.pop(0))

        def step(self):
            self.held = jnp.concatenate([tie(self.held), self.got], axis=0)
            tie.mark(self.held)
            if self.masks:
                self.send()
                return True
            return False

        def slots(self):
            while self.step():
                tie.pause()
            return [self.held[head_places.index(s)] for s in range(1, head_size)]

    gather_a = HeadGather(strip_a)
    acts_out = to_micro(tie(jnp.concatenate([activations, conditioning], axis=1)))
    tie.mark(*acts_out)
    tie.pause()
    gather_a.step()
    strip_f = jnp.concatenate([my_slab(tie(w_fc1), 0), my_slab(w_fc2, 1).T], axis=1)
    own_two_t = tie(w_fc2).T
    own_out_t = tie(w_out).T
    up_tile = jnp.broadcast_to(tie(up_gain)[None], (rows // UP, UP, model)).reshape(rows, model)
    cot_out = to_micro(tie(cotangent))
    tie.mark(strip_f, own_two_t, own_out_t, up_tile, *cot_out)
    tie.pause()
    slots_a = gather_a.slots()
    dp_orders = (masks, masks[::-1])
    dp_index = jnp.stack([me, here]).astype(jnp.int32)

    def colors_of(slots):
        rows_half = slab // 2
        held = [
            jnp.stack([v[c * rows_half : (c + 1) * rows_half] for v in slots])[None] for c in (0, 1)
        ]
        tie.mark(*held)
        return held

    def swap_stage(held, step):
        return [xor_swap(v, "dp", order[step]) for v, order in zip(held, dp_orders)]

    def widen(held, got):
        wider = [jnp.concatenate([a, b], axis=0) for a, b in zip(tie(*held), got)]
        tie.mark(*wider)
        return wider

    held_a = colors_of(tie(*slots_a))
    got_a = swap_stage(held_a, 0)
    got_acts = sent(acts_out, *held_a)
    for step in range(1, len(masks)):
        tie.pause()
        held_a = widen(held_a, got_a)
        got_a = swap_stage(held_a, step)
    tie.pause()
    held_a = widen(held_a, got_a)
    tables_a = held_a + [xor_swap(v, "dp", 1) for v in held_a]
    joined, normed, coarse = join(
        my_micro.reshape(1).astype(jnp.int32),
        tie(*got_acts),
        up_tile,
        norm1_gain.reshape(1, -1),
        norm1_shift.reshape(1, -1),
    )
    tie.mark(normed)

    stages_sub = [("head", 1 << i) for i in range(group.bit_length() - 1)]
    stage_lists = [stages_sub + [("dp", m) for m in order] for order in dp_orders]
    stages = len(stage_lists[0])
    shaped = tie(normed).reshape(blocks, BLOCK, model)
    far_held = [shaped[:, :, c * half : (c + 1) * half] for c in (0, 1)]
    tie.mark(*far_held)
    far_got = [xor_swap(v, *stage_lists[c][0]) for c, v in enumerate(far_held)]
    gather_f = HeadGather(tie(strip_f))
    for step in range(1, stages):
        tie.pause()
        far_held = widen(far_held, far_got)
        far_got = [xor_swap(v, *stage_lists[c][step]) for c, v in enumerate(far_held)]
    gather_f.step()
    limit = far_held[0].shape[0]
    table_row = lax.dynamic_index_in_dim(block_targets, my_micro, 0, False)

    def targets_of(device):
        return lax.dynamic_slice_in_dim(table_row, (device * group + my_sub) * blocks, blocks)

    targets = targets_of(me)
    targets_both = jnp.concatenate([targets, targets_of(me ^ 1)])
    owner = jnp.maximum(targets_both, 0) // blocks
    away = (owner // group) ^ me
    away_sub = (owner % group) ^ my_sub

    def table_index(stage_list):
        index = jnp.zeros_like(owner)
        for bit, (axis, mask) in enumerate(stage_list):
            far_bits = away if axis == "dp" else away_sub
            index = index + (((far_bits & mask) != 0).astype(jnp.int32) << bit)
        return index * blocks + jnp.maximum(targets_both, 0) % blocks

    index_a, index_b = table_index(stage_lists[0]), table_index(stage_lists[1])
    on_my_core = (away & 1) == 0
    has_far = (targets >= 0).astype(jnp.int32)
    valid = on_my_core & (targets_both >= 0)
    route_a = jnp.where(valid, index_a, -1)
    route_b = jnp.where(valid, index_b, -1)

    biases = [small]
    for value in slots_a:
        rows3 = value[slab : slab + 3 * small_rows].astype(f32).reshape(3, -1)
        biases.append(rows3[0] + rows3[1] + rows3[2])
    bias_q = jnp.concatenate([b[:hc] for b in biases])
    bias_v = jnp.concatenate([b[hc : 2 * hc] for b in biases])
    bias_one = jnp.concatenate([b[2 * hc : 2 * hc + fc] for b in biases])
    bias_kv = jnp.concatenate([jnp.zeros_like(bias_v), bias_v])
    w_qkv_all, w_out_t = assemble(
        dp_index,
        list(tie(*tables_a)),
        [w_qkv[0], w_qkv[1], w_qkv[2], own_out_t],
        [(t * hc, hc, 0, t * heads_all) for t in range(3)] + [(3 * hc, hc, 1, 0)],
        masks,
        [3 * heads_all, heads_all],
    )
    tie.mark(w_qkv_all, w_out_t)
    qkv = (mm(normed, w_qkv_all) + jnp.concatenate([bias_q, bias_kv])).astype(bf16)
    tie.mark(qkv)

    tie.pause()
    kept, passed = far_pick(list(zip(tie(*far_held), far_got)), index_a, index_b)
    tie.mark(kept, passed)
    passed_got = xor_swap(passed, "dp", 1)
    tie.pause()
    held_f = colors_of(gather_f.slots())
    got_f = swap_stage(held_f, 0)
    got_cot = sent(cot_out, *held_f)
    passed = passed_got
    for step in range(1, len(masks)):
        tie.pause()
        held_f = widen(held_f, got_f)
        got_f = swap_stage(held_f, step)
    far = jnp.where(on_my_core[:blocks, None, None], tie(kept), passed).reshape(tokens, model)
    kv_far = (mm(far, w_qkv_all[:, heads_all:]) + bias_kv).astype(bf16)
    tie.mark(kv_far)
    attended = attention_forward(has_far, qkv, tie(kv_far), heads_all)
    tie.mark(attended, *got_cot[1::2])
    residual = joined + (mm_nt(tie(attended), w_out_t) + b_out)
    normed2_f, standard_two, inverse_two = norm_forward(residual, norm2_gain, norm2_shift)
    normed_two = normed2_f.astype(bf16)
    tie.mark(residual, normed_two)

    incoming = in_rank_order(tie(*got_cot))
    incoming_f = incoming.astype(f32)
    grad_b2 = jnp.sum(incoming_f, axis=0, keepdims=True)
    normed_t, far_t = tie(normed).T, tie(far).T
    incoming_t, normed_two_t = incoming.T, tie(normed_two).T
    tie.mark(grad_b2, normed_t, far_t, incoming_t, normed_two_t)
    tie.pause()
    got_f = list(tie(*got_f))
    tables_f = [v for pair in zip(held_f, got_f) for v in pair]
    held_core = [xor_swap(v, "dp", 1) for v in held_f]
    got_core = [xor_swap(v, "dp", 1) for v in got_f]
    tables_f += [v for pair in zip(held_core, got_core) for v in pair]

    shape = jax.ShapeDtypeStruct
    slope, out, keep_two, send_two = feed_call(
        feed_forward_kernel,
        masks,
        dp_index,
        tables_f,
        w_fc1,
        own_two_t,
        0,
        [
            (normed_two, None),
            (bias_one.reshape(1, -1), (0, False)),
            (residual, None),
            (b_fc2.reshape(1, -1), None),
            (incoming_t, None),
        ],
        [(shape((tokens, hidden_all), bf16), (1, False)), (shape((tokens, model), bf16), None)],
        [pltpu.VMEM((tokens, model), f32)],
    )
    tie.mark(slope)
    got_two = xor_swap(send_two, "dp", 1)

    reversed_bits = [
        sum(m for m, back_m in zip(head_masks, head_masks[::-1]) if p & back_m) for p in range(head_size)
    ]

    class HeadSum:
        def __init__(self, piece):
            self.held = jnp.stack([piece(here ^ p) for p in reversed_bits])
            tie.mark(self.held)
            self.masks = list(head_masks)
            self.send()

        def send(self):
            half = self.held.shape[0] // 2
            self.got = xor_swap(self.held[half:], "head", self.masks.pop(0))

        def step(self):
            half = self.held.shape[0] // 2
            total = tie(self.held)[:half].astype(f32) + self.got.astype(f32)
            if half == 1:
                return total[0]
            self.held = total.astype(bf16)
            tie.mark(self.held)
            self.send()
            return None

        def finish(self):
            out = None
            while out is None:
                out = self.step()
            return out

    class Steps:
        def tokens_out(self):
            out_pieces = from_micro(tie(out))
            tie.mark(*out_pieces)
            self.got_out = back(out_pieces)

        def feed(self):
            self.grad_b1, self.grad_two, self.keep_one, self.send_one = feed_call(
                feed_backward_kernel,
                masks,
                dp_index,
                tables_f,
                own_two_t,
                w_fc1,
                1,
                [(tie(incoming), None), (slope, (1, False)), (normed_two_t, None)],
                [(shape((1, hidden_all), f32), (1, True)), (shape((tokens, model), f32), None)],
                [],
            )
            tie.mark(self.grad_b1)
            self.got_one = xor_swap(self.send_one, "dp", 1)

        def halves(self, keep, got):
            return [
                DpSum(tie, (keep, got), dp_orders[c], c * head_size, head_size)
                for c in range(HALVES)
            ]

        def two_first(self):
            self.sums_two = self.halves(keep_two, got_two)
            for part in self.sums_two:
                part.stage(0)

        def norm(self):
            grad_res_part, self.grad_g2, self.grad_s2 = norm_backward(
                tie(self.grad_two), standard_two, inverse_two, norm2_gain
            )
            self.grad_residual = incoming_f + grad_res_part
            self.grad_branch = self.grad_residual.astype(bf16)
            self.grad_bo = jnp.sum(self.grad_branch.astype(f32), axis=0)
            self.grad_att = mm(self.grad_branch, w_out_t).astype(bf16)
            tie.mark(self.grad_att)

        def attention(self):
            self.grad_qkv = attention_backward(has_far, qkv, kv_far, tie(self.grad_att))
            tie.mark(self.grad_qkv)

        def one_first(self):
            self.sums_one = self.halves(self.keep_one, self.got_one)
            for part in self.sums_one:
                part.stage(0)

        def far_back(self):
            self.far_rows = (
                mm_nt(tie(self.grad_qkv)[1, :, heads_all:], w_qkv_all[:, heads_all:])
                .astype(bf16)
                .reshape(blocks, BLOCK, model)
            )
            tie.mark(self.far_rows)
            self.far_other = xor_swap(self.far_rows, "dp", 1)

        def branch(self):
            self.branch_t = tie(self.grad_branch).T
            tie.mark(self.branch_t)

        def route(self):
            routed = far_route(tie(self.far_rows), self.far_other, route_a, route_b, limit)
            tie.mark(*routed)
            self.terms = [[routed[0]], [routed[2]]]
            for color in range(2):
                axis, mask = stage_lists[color][-1]
                self.terms[color].append(xor_swap(routed[2 * color + 1], axis, mask))

        def weights(self):
            keep, send_att = attention_weights(
                masks, dp_index, normed_t, far_t, self.branch_t, tie(self.grad_qkv), attended, hc
            )
            tie.mark(send_att)
            got = xor_swap(send_att, "dp", 1)
            groups = 2 * head_size
            self.sums_att = [
                DpSum(tie, (keep, got), dp_orders[c], c * groups, groups) for c in (0, 1)
            ]

        def own(self):
            self.grad_own = mm_nt(tie(self.grad_qkv)[0], w_qkv_all)
            self.grad_bq = jnp.sum(tie(self.grad_qkv)[0, :, :heads_all].astype(f32), axis=0)
            self.grad_bv = jnp.sum(
                tie(self.grad_qkv)[:, :, 2 * heads_all :].astype(f32), axis=(0, 1)
            )
            tie.mark(self.grad_own, self.grad_bq, self.grad_bv)

        def hidden_rest(self):
            for step in range(1, len(masks)):
                for c in range(HALVES):
                    pair = (self.sums_two[c], self.sums_one[c])
                    low, high = pair[0].rows >> (step + 1), pair[0].rows >> step
                    moved = jnp.concatenate([part.upto(low, high) for part in pair], axis=0)
                    tie.mark(moved)
                    moved = xor_swap(moved, "dp", dp_orders[c][step])
                    for i, part in enumerate(pair):
                        part.terms.append((moved, i * head_size))

        def hidden_head(self):
            ends = [part.final() for part in self.sums_two + self.sums_one]
            self.sum_f = HeadSum(
                lambda a: jnp.stack([lax.dynamic_index_in_dim(v, a, 0, False) for v in ends])
            )

        def hidden_step(self):
            self.sum_f.step()

        def far_rest(self):
            for step in range(stages - 2, -1, -1):
                low, high = blocks << step, blocks << (step + 1)
                moved = []
                for color in range(2):
                    value = sum(t[low:high].astype(f32) for t in tie(*self.terms[color]))
                    moved.append(value.astype(bf16))
                tie.mark(*moved)
                for color in range(2):
                    self.terms[color].append(xor_swap(moved[color], *stage_lists[color][step]))

        def att_first(self):
            for part in self.sums_att:
                part.stage(0)

        def att_rest(self):
            for step in range(1, len(masks)):
                for part in self.sums_att:
                    part.stage(step)

        def att_head(self):
            ends = [part.final().reshape(2, head_size, slab, hc) for part in self.sums_att]
            self.sum_att = HeadSum(
                lambda a: jnp.concatenate(
                    [lax.dynamic_index_in_dim(v, a ^ here, 1, False) for v in ends], axis=0
                )
            )

        def att_step(self):
            self.sum_att.step()

        def leave(self):
            self.grad_input, self.grad_up, self.grad_g1, self.grad_s1 = leave(
                tie(self.grad_own),
                joined,
                self.grad_residual,
                coarse,
                norm1_gain.reshape(1, -1),
                *self.terms,
            )
            tie.mark(self.grad_input)

        def tokens_back(self):
            in_pieces = from_micro(tie(self.grad_input))
            tie.mark(*in_pieces)
            self.got_input = back(in_pieces)

        def tokens_end(self):
            self.grad_input = in_micro_order(tie(*self.got_input)).astype(f32)
            self.grad_coarse = jnp.sum(
                self.grad_input.reshape(micro, -1, UP, model) * up_gain, axis=2
            )
            tie.mark(self.grad_input, self.grad_coarse)

        def small(self):
            by_slot = jnp.concatenate(
                [self.grad_bq.reshape(-1, hc), self.grad_bv.reshape(-1, hc)], axis=1
            )
            by_head = jnp.concatenate(
                [choose([by_slot[s] for s in range(head_size)], a ^ here) for a in range(head_size)]
            )
            self.total = jnp.concatenate(
                [tie(self.grad_up), self.grad_g1, self.grad_s1]
                + [v.reshape(1, -1) for v in (self.grad_bo, self.grad_g2, self.grad_s2)]
                + [grad_b2, self.grad_b1.reshape(-1, model), by_head.reshape(-1, model)]
            )
            tie.mark(self.total)
            self.small_stages = [("dp", m) for m in [1] + masks] + [("head", m) for m in head_masks]
            self.small_got = None

        def small_step(self):
            if self.small_got is not None:
                self.total = tie(self.total) + self.small_got
                tie.mark(self.total)
                self.small_got = None
            if self.small_stages:
                self.small_got = xor_swap(self.total, *self.small_stages.pop(0))

        def small_end(self):
            self.small_step()
            while self.small_got is not None:
                tie.pause()
                self.small_step()

        def layer(self):
            self.layer_out = in_micro_order(tie(*self.got_out))
            tie.mark(self.layer_out)

        def wait_out(self):
            tie.mark(*tie.last, *self.got_out)

        def wait_two(self):
            tie.mark(*tie.last, *[part.terms[-1][0] for part in self.sums_two])

        def wait_one(self):
            tie.mark(*tie.last, *[part.terms[-1][0] for part in self.sums_one])

        def wait_att(self):
            tie.mark(*tie.last, *[part.terms[-1][0] for part in self.sums_att])

        def wait_far(self):
            tie.mark(*tie.last, *[t[-1] for t in self.terms])

        def pause(self):
            tie.pause()

        def flush(self):
            tie.flush()

    it = Steps()
    for name in STEPS:
        getattr(it, name)()
    layer_out = it.layer_out
    grad_input, grad_coarse, total = it.grad_input, it.grad_coarse, it.total
    grad_wf, grad_wa = it.sum_f.finish(), it.sum_att.finish()
    grad_w2 = jnp.concatenate([grad_wf[c].T for c in range(HALVES)], axis=0)
    grad_w1 = jnp.concatenate([grad_wf[HALVES + c] for c in range(HALVES)], axis=1)
    grad_wqkv, grad_wo = grad_wa[:3], grad_wa[3].T
    s_g1, s_s1, s_bo, s_g2, s_s2, s_b2 = [total[UP + i] for i in range(6)]
    hidden_rows = hidden_all // model
    s_b1 = total[UP + 6 : UP + 6 + hidden_rows].reshape(-1)
    by_head = total[UP + 6 + hidden_rows :].reshape(head_size, 2 * hc)
    s_bq, s_bv = by_head[:, :hc].reshape(-1), by_head[:, hc:].reshape(-1)
    return (
        layer_out,
        grad_input,
        grad_coarse,
        total[:UP],
        s_g1,
        s_s1,
        grad_wqkv,
        jnp.stack([s_bq, s_bv]),
        grad_wo,
        s_bo,
        s_g2,
        s_s2,
        grad_w1,
        s_b1,
        grad_w2,
        s_b2,
    )


def solution(mesh):
    rows = P(None, ("dp", "head"), None)
    return jax.shard_map(
        local,
        mesh=mesh,
        in_specs=(
            rows,
            rows,
            rows,
            P(),
            P(),
            P(),
            P(),
            P(None, None, "head"),
            P(None, "head"),
            P("head", None),
            P(),
            P(),
            P(),
            P(None, "head"),
            P("head"),
            P("head", None),
            P(),
        ),
        out_specs=(
            rows,
            rows,
            rows,
            P(),
            P(),
            P(),
            P(None, "dp", "head"),
            P(),
            P("head", "dp"),
            P(),
            P(),
            P(),
            P("dp", "head"),
            P(),
            P("head", "dp"),
            P(),
        ),
        check_vma=False,
    )
```
